32 devices in a mesh: replica: 2 (over x), shard: 4 (over y, core), seq: 4 (over z).
Axes of the slice: x: 2, y: 2, z: 4, core: 2. Of those that a mesh axis runs over, the one named last changes fastest.
Arguments:
- states: float32 [6240, 1536], P(('replica', 'shard', 'seq')), may hold values from -6 to 6
- text_emb: bfloat16 [4096, 1536], P(('replica', 'shard', 'seq')), may hold values from -6 to 6
- grid_pos: int32 [3, 6240], P(None, ('replica', 'shard', 'seq')), may hold values from 0 to 63
- time_mod: float32 [8, 6, 1536], P(('replica', 'shard')), may hold values from -4 to 4
- w_qkv: bfloat16 [1536, 3, 1536], P(('shard', 'seq')), may hold values from -0.15625 to 0.15625
- w_out: bfloat16 [1536, 1536], P(('shard', 'seq')), may hold values from -2.5 to 2.5
- w_cross: bfloat16 [1536, 3, 1536], P(('shard', 'seq')), may hold values from -0.15625 to 0.15625
- w_crossout: bfloat16 [1536, 1536], P(('shard', 'seq')), may hold values from -2.5 to 2.5
- w_up: bfloat16 [1536, 8960], P(('shard', 'seq')), may hold values from -0.15625 to 0.15625
- w_down: bfloat16 [8960, 1536], P(('shard', 'seq')), may hold values from -0.0625 to 0.0625
- attn_bias: float32 [8, 1536], replicated, may hold values from -2 to 2
- qk_gain: float32 [4, 1536], replicated, may hold values from 0.5 to 1.5
- norm_gain: float32 [1536], replicated, may hold values from 0.5 to 1.5
- norm_bias: float32 [1536], replicated, may hold values from -2 to 2
- up_bias: float32 [8960], replicated, may hold values from -2 to 2
- down_bias: float32 [1536], replicated, may hold values from -2 to 2
- modulation: float32 [6, 1536], replicated, may hold values from -4 to 4
- out_grad: float32 [6240, 1536], P(('replica', 'shard', 'seq')), may hold values from -6 to 6
Outputs:
- block_out: float32 [6240, 1536], P(('replica', 'shard', 'seq'))
- states_grad: float32 [6240, 1536], P(('replica', 'shard', 'seq'))
- text_grad: float32 [4096, 1536], P(('replica', 'shard', 'seq'))
- time_grad: float32 [8, 6, 1536], P(('replica', 'shard'))
- qkv_grad: float32 [1536, 3, 1536], P(('shard', 'seq'))
- outproj_grad: float32 [1536, 1536], P(('shard', 'seq'))
- crossqkv_grad: float32 [1536, 3, 1536], P(('shard', 'seq'))
- crossout_grad: float32 [1536, 1536], P(('shard', 'seq'))
- up_grad: float32 [1536, 8960], P(('shard', 'seq'))
- down_grad: float32 [8960, 1536], P(('shard', 'seq'))
- bias_grad: float32 [8, 1536], replicated
- gain_grad: float32 [4, 1536], replicated
- lngain_grad: float32 [1536], replicated
- lnbias_grad: float32 [1536], replicated
- upbias_grad: float32 [8960], replicated
- downbias_grad: float32 [1536], replicated
- mod_grad: float32 [6, 1536], replicated
The draws below stay inside these ranges and needn't reach their ends.
All inputs are finite; a program needn't handle non-finite values.
Results may differ from the reference program's by a relative error of at most 0.02.
Values may be sent and summed in bfloat16 or wider, within the bound.
A program may use at most 448 MiB of HBM per device.

```python
import math
import jax
import jax.numpy as jnp
import numpy as np
from jax import lax

D = 1536
HEADS = 12
HD = 128
FF = 8960
TEXT = 512
LEN = 780
CLIPS_ALL = 8
TOKENS = 6240
TEXTS = 4096


def with_ends(drawn, key, smallest, top_value):
    dims = drawn.shape
    place = [jax.random.randint(jax.random.fold_in(key, axis), (), 0, dims[axis]) for axis in range(len(dims))]
    drawn = drawn.at[tuple(place)].set(smallest)
    longest = dims.index(max(dims))
    place[longest] = (place[longest] + 1) % dims[longest]
    return drawn.at[tuple(place)].set(top_value)


def block_levels(own_key, dims, pieces, low, largest):
    level = 1.0
    for position, blocks in pieces:
        steps = jax.random.uniform(jax.random.fold_in(jax.random.fold_in(own_key, 6), position), (blocks,), jnp.float32, low / len(pieces), largest / len(pieces))
        level = level * jnp.repeat(jnp.exp(steps), dims[position] // blocks).reshape((-1,) + (1,) * (len(dims) - 1 - position))
    return level


def centred(stream_key, dims, deviation, reach, shards=(), held_as=jnp.bfloat16):
    result = deviation * jax.random.normal(stream_key, dims, jnp.float32)
    if shards:
        result = result * block_levels(stream_key, dims, shards, -0.22, 0.18)
    return jnp.clip(result, -reach, reach).astype(held_as)


def setup_inputs(seed: int = 0) -> dict:
    arg_keys = jax.random.split(jax.random.key(seed), 19)
    states = centred(arg_keys[0], (TOKENS, D), 1.0, 6.0, ((0, 32),), jnp.float32)
    text_emb = centred(arg_keys[1], (TEXTS, D), 1.0, 6.0, ((0, 32),))
    grid_pos = with_ends(jax.random.randint(arg_keys[2], (3, TOKENS), 0, 64), jax.random.fold_in(arg_keys[2], 1), 0, 63).astype(jnp.int32)
    time_mod = centred(arg_keys[3], (CLIPS_ALL, 6, D), 0.5, 4.0, ((0, 8),), jnp.float32)
    w_qkv = centred(arg_keys[4], (D, 3, D), D ** -0.5, 0.15625, ((0, 16),))
    w_out = centred(arg_keys[5], (D, D), (max(D // 256, 4)) ** -0.5, 2.5, ((0, 16),))
    w_cross = centred(arg_keys[6], (D, 3, D), D ** -0.5, 0.15625, ((0, 16),))
    w_crossout = centred(arg_keys[7], (D, D), (max(D // 256, 4)) ** -0.5, 2.5, ((0, 16),))
    w_up = centred(arg_keys[8], (D, FF), D ** -0.5, 0.15625, ((0, 16),))
    w_down = centred(arg_keys[9], (FF, D), FF ** -0.5, 0.0625, ((0, 16),))
    attn_bias = centred(arg_keys[10], (8, D), 0.3, 2.0, (), jnp.float32)
    qk_gain = jnp.clip(1.0 + 0.1 * jax.random.normal(arg_keys[11], (4, D), jnp.float32), 0.5, 1.5)
    norm_gain = jnp.clip(1.0 + 0.1 * jax.random.normal(arg_keys[12], (D,), jnp.float32), 0.5, 1.5)
    norm_bias = centred(arg_keys[13], (D,), 0.3, 2.0, (), jnp.float32)
    up_bias = centred(arg_keys[14], (FF,), 0.3, 2.0, (), jnp.float32)
    down_bias = centred(arg_keys[15], (D,), 0.3, 2.0, (), jnp.float32)
    modulation = centred(arg_keys[16], (6, D), 0.5, 4.0, (), jnp.float32)
    out_grad = centred(arg_keys[17], (TOKENS, D), 1.0, 6.0, ((0, 32),), jnp.float32)
    return {"states": states, "text_emb": text_emb, "grid_pos": grid_pos, "time_mod": time_mod, "w_qkv": w_qkv, "w_out": w_out, "w_cross": w_cross, "w_crossout": w_crossout, "w_up": w_up, "w_down": w_down, "attn_bias": attn_bias, "qk_gain": qk_gain, "norm_gain": norm_gain, "norm_bias": norm_bias, "up_bias": up_bias, "down_bias": down_bias, "modulation": modulation, "out_grad": out_grad}


EPS = 1e-06
PRECISE = lax.Precision.HIGHEST

@jax.custom_vjp
def low(v):
    return lax.optimization_barrier(v.astype(jnp.bfloat16)).astype(jnp.float32)

@jax.custom_vjp
def low_back(v):
    return v

def low_keep(v):
    return (low(v), None)

def low_pass(kept, grad):
    return (grad,)

def back_keep(v):
    return (v, None)

def back_low(kept, grad):
    return (low(grad),)
low.defvjp(low_keep, low_pass)
low_back.defvjp(back_keep, back_low)

def rope_tables(grid_pos):
    pair_count = HD // 2
    third_part = pair_count // 3
    first_part = pair_count - 2 * third_part
    pair_index = np.arange(pair_count)
    part_of = np.where(pair_index < first_part, 0, np.where(pair_index < first_part + third_part, 1, 2))
    offset = np.where(part_of == 0, pair_index, np.where(part_of == 1, pair_index - first_part, pair_index - first_part - third_part))
    part_width = np.where(part_of == 0, first_part, third_part)
    frequency = 10000.0 ** (-offset / part_width)
    positions = grid_pos.astype(jnp.float32)
    angles = positions[0][:, None] * jnp.asarray(frequency * (part_of == 0), jnp.float32)[None, :]
    angles = angles + positions[1][:, None] * jnp.asarray(frequency * (part_of == 1), jnp.float32)[None, :]
    angles = angles + positions[2][:, None] * jnp.asarray(frequency * (part_of == 2), jnp.float32)[None, :]
    return (jnp.cos(angles), jnp.sin(angles))

def layer_norm(values):
    center = values - lax.optimization_barrier(jnp.mean(values, -1, keepdims=True))
    return center * lax.rsqrt(lax.optimization_barrier(jnp.mean(center * center, -1, keepdims=True)) + EPS)

def rms_norm(values, gain):
    return values * lax.rsqrt(lax.optimization_barrier(jnp.mean(values * values, -1, keepdims=True)) + EPS) * gain

def rotate(values, cosine_tab, sine_tab):
    row_count = values.shape[0]
    paired = values.reshape(row_count, HEADS, HD // 2, 2)
    even_part = paired[..., 0]
    odd_part = paired[..., 1]
    cosine = cosine_tab[:, None, :]
    sine_val = sine_tab[:, None, :]
    turned = jnp.stack([even_part * cosine - odd_part * sine_val, even_part * sine_val + odd_part * cosine], -1)
    return turned.reshape(row_count, HEADS * HD)

def attend(queries, key_rows, value_rows):
    scale_val = 1.0 / math.sqrt(HD)
    q_heads = queries.reshape(queries.shape[0], HEADS, HD)
    k_heads = key_rows.reshape(key_rows.shape[0], HEADS, HD)
    v_heads = value_rows.reshape(value_rows.shape[0], HEADS, HD)
    scores = low_back(jnp.einsum('qhd,khd->hqk', q_heads, k_heads, precision=PRECISE) * scale_val)
    attn_probs = jax.nn.softmax(scores, axis=-1)
    mixed = jnp.einsum('hqk,khd->qhd', low(attn_probs), v_heads, precision=PRECISE)
    return low_back(low(mixed.reshape(queries.shape[0], HEADS * HD)))

def clip_layer(params, clip_states, clip_text, clip_mod, clip_pos):
    w_qkv, w_out, w_cross, w_crossout, w_up, w_down, attn_bias, qk_gain, norm_gain, norm_bias, up_bias, down_bias, modulation = params
    mods = modulation + clip_mod
    cosine_tab, sine_tab = rope_tables(clip_pos)
    self_in = low(layer_norm(clip_states) * (1.0 + mods[1]) + mods[0])
    project = jnp.einsum('td,dkf->tkf', self_in, w_qkv, precision=PRECISE) + attn_bias[:3][None]
    query_pre = low_back(project[:, 0])
    key_pre = low_back(project[:, 1])
    value_rows = low_back(low(project[:, 2]))
    queries = low_back(low(rotate(rms_norm(query_pre, qk_gain[0]), cosine_tab, sine_tab)))
    key_rows = low_back(low(rotate(rms_norm(key_pre, qk_gain[1]), cosine_tab, sine_tab)))
    mixed = attend(queries, key_rows, value_rows)
    branch = low_back(jnp.dot(mixed, w_out, precision=PRECISE) + attn_bias[3])
    after_self = clip_states + branch * mods[2]
    cross_in = low(layer_norm(after_self) * norm_gain + norm_bias)
    cq_pre = low_back(jnp.dot(cross_in, w_cross[:, 0], precision=PRECISE) + attn_bias[4])
    ck_pre = low_back(jnp.dot(clip_text, w_cross[:, 1], precision=PRECISE) + attn_bias[5])
    cross_val = low_back(low(jnp.dot(clip_text, w_cross[:, 2], precision=PRECISE) + attn_bias[6]))
    cross_q = low(rms_norm(cq_pre, qk_gain[2]))
    cross_k = low(rms_norm(ck_pre, qk_gain[3]))
    cross_mix = attend(cross_q, cross_k, cross_val)
    cross_out = low_back(jnp.dot(cross_mix, w_crossout, precision=PRECISE) + attn_bias[7])
    after_cross = after_self + cross_out
    ffn_in = low(layer_norm(after_cross) * (1.0 + mods[4]) + mods[3])
    hidden_pre = low_back(jnp.dot(ffn_in, w_up, precision=PRECISE) + up_bias)
    hidden = low(jax.nn.gelu(hidden_pre, approximate=True))
    ffn_out = low_back(jnp.dot(hidden, w_down, precision=PRECISE) + down_bias)
    return after_cross + ffn_out * mods[5]

def reference(states, text_emb, grid_pos, time_mod, w_qkv, w_out, w_cross, w_crossout, w_up, w_down, attn_bias, qk_gain, norm_gain, norm_bias, up_bias, down_bias, modulation, out_grad):
    clips_all = time_mod.shape[0]
    clip_positions = grid_pos.reshape(3, clips_all, LEN).transpose(1, 0, 2)
    layer_saved = jax.checkpoint(clip_layer)

    def forward(states_in, text_in, time_in, *params):

        def scan_step(carried, clip_items):
            return (carried, layer_saved(params, clip_items[0], clip_items[1], clip_items[2], clip_items[3]))
        clip_inputs = (states_in.reshape(clips_all, LEN, D), text_in.reshape(clips_all, TEXT, D), time_in, clip_positions)
        _, outputs = lax.scan(scan_step, jnp.zeros((), jnp.float32), clip_inputs)
        return outputs.reshape(clips_all * LEN, D)
    params_in = (w_qkv.astype(jnp.float32), w_out.astype(jnp.float32), w_cross.astype(jnp.float32), w_crossout.astype(jnp.float32), w_up.astype(jnp.float32), w_down.astype(jnp.float32), attn_bias, qk_gain, norm_gain, norm_bias, up_bias, down_bias, modulation)
    block_out, pullback = jax.vjp(forward, states, text_emb.astype(jnp.float32), time_mod, *params_in)
    grads = pullback(out_grad)
    return (block_out, grads[0], grads[1], grads[2], grads[3], grads[4], grads[5], grads[6], grads[7], grads[8], grads[9], grads[10], grads[11], grads[12], grads[13], grads[14], grads[15])
```

```python
import math

import jax
import jax.numpy as jnp
import numpy as np
from jax import lax
from jax.sharding import Mesh, PartitionSpec as P

HD = 128
EPS = 1e-06
F32 = jnp.float32
BF16 = jnp.bfloat16
SCALE = 1.0 / math.sqrt(HD)
SWAP = [(0, 1), (1, 0)]


def rope_tables(grid_pos):
    pairs = HD // 2
    width = pairs // 3
    first = pairs - 2 * width
    index = np.arange(pairs)
    part = np.where(index < first, 0, np.where(index < first + width, 1, 2))
    offset = np.where(part == 0, index, np.where(part == 1, index - first, index - first - width))
    frequency = 10000.0 ** (-offset / np.where(part == 0, first, width))
    position = grid_pos.astype(F32)
    angles = 0.0
    for axis in range(3):
        lane = np.repeat(frequency * (part == axis), 2)
        angles = angles + position[axis][:, None] * jnp.asarray(lane, F32)[None, :]
    sign = np.where(np.arange(HD) % 2 == 0, -1.0, 1.0)
    return jnp.cos(angles), jnp.sin(angles) * jnp.asarray(sign, F32)[None, :]


def partner(values):
    even = (jnp.arange(values.shape[-1]) % 2) == 0
    return jnp.where(even, jnp.roll(values, -1, -1), jnp.roll(values, 1, -1))


def turn(values, cosine, sine):
    heads = values.shape[-1] // HD
    wide = (1,) * (values.ndim - 1) + (heads,)
    return values * jnp.tile(cosine, wide) + partner(values) * jnp.tile(sine, wide)


def layer_norm(values):
    center = values - jnp.mean(values, -1, keepdims=True)
    inverse = lax.rsqrt(jnp.mean(center * center, -1, keepdims=True) + EPS)
    return center * inverse, inverse


def norm_backward(normed, inverse, grad_in):
    return inverse * (
        grad_in
        - jnp.mean(grad_in, -1, keepdims=True)
        - normed * jnp.mean(grad_in * normed, -1, keepdims=True)
    )


def mm(a, b):
    return lax.dot_general(a, b, (((a.ndim - 1,), (0,)), ((), ())), preferred_element_type=F32)


def mm_t(a, b):
    return lax.dot_general(a, b, (((a.ndim - 1,), (1,)), ((), ())), preferred_element_type=F32)


def outer(a, b):
    lead = tuple(range(a.ndim - 1))
    return lax.dot_general(a, b, ((lead, lead), ((), ())), preferred_element_type=F32)


def on_device(
    states, text_emb, grid_pos, time_mod, w_qkv, w_out, w_cross, w_crossout, w_up, w_down,
    attn_bias, qk_gain, norm_gain, norm_bias, up_bias, down_bias, modulation, out_grad,
):
    x, y, core = lax.axis_index("x"), lax.axis_index("y"), lax.axis_index("core")
    seqs = lax.axis_size("z")
    reps = lax.axis_size("rep")
    dim = states.shape[1]
    block = y * 2 + x

    def from_y(a):
        return lax.ppermute(a, "y", SWAP)

    def from_x(a):
        return lax.ppermute(a, "x", SWAP)

    def from_xy(a):
        return lax.ppermute(a, ("x", "y"), [(i, 3 - i) for i in range(4)])

    def from_core(a):
        return lax.ppermute(a, "core", SWAP)

    def gather4(a):
        far, xs, ys = from_xy(a), from_x(a), from_y(a)
        return jnp.stack([a, ys, xs, far])

    def reduce4(term):
        far = from_xy(term(3).astype(BF16))
        xs = from_x(term(2).astype(BF16))
        ys = from_y(term(1).astype(BF16))
        return term(0) + ys.astype(F32) + xs.astype(F32) + far.astype(F32)

    def sum4(stat):
        far, xs, ys = from_xy(stat), from_x(stat), from_y(stat)
        return (
            stat
            + jnp.stack([ys[1], ys[0], ys[3], ys[2]])
            + jnp.stack([xs[2], xs[3], xs[0], xs[1]])
            + jnp.stack([far[3], far[2], far[1], far[0]])
        )

    def reorder(a):
        a = jnp.where(x == 1, jnp.stack([a[2], a[3], a[0], a[1]]), a)
        return jnp.where(y == 1, jnp.stack([a[1], a[0], a[3], a[2]]), a)

    def heads_swap(a):
        return lax.all_to_all(a, "z", split_axis=0, concat_axis=0, tiled=True)

    def pick(v, blocks=4):
        return lax.dynamic_index_in_dim(
            v.reshape(v.shape[:-1] + (blocks, v.shape[-1] // blocks)), block, v.ndim - 1, False
        )

    def spread(v):
        hot = (jnp.arange(4) == block).astype(F32)
        full = v[..., None, :] * hot[:, None]
        return full.reshape(v.shape[:-1] + (4 * v.shape[-1],))

    def column_block(w):
        rows, groups, width = w.shape[0], w.shape[1], w.shape[2] // 4
        mine = lax.dynamic_index_in_dim(w.reshape(rows, groups, 2, 2, width), x, 3, False)
        keep = lax.dynamic_index_in_dim(mine, y, 2, False).reshape(rows, groups * width)
        send = lax.dynamic_index_in_dim(mine, 1 - y, 2, False).reshape(rows, groups * width)
        recv = from_y(send)
        both = jnp.where(y == 0, jnp.stack([keep, recv]), jnp.stack([recv, keep]))
        full = lax.all_gather(both, ("core", "z"), axis=1, tiled=True)
        return full.reshape(-1, groups * width)

    def row_block(w):
        rows, half = w.shape[0], w.shape[1] // 2
        keep = lax.dynamic_slice_in_dim(w, core * half, half, 1)
        recv = from_core(lax.dynamic_slice_in_dim(w, (1 - core) * half, half, 1))
        mine = jnp.where(core == x, keep, recv)
        full = lax.all_gather(mine, ("core", "z"), axis=0, tiled=True)
        return full.reshape(2, seqs * rows, half).transpose(1, 0, 2).reshape(seqs * rows, 2 * half)

    def over_reps(a):
        return lax.psum(a, "rep") if reps > 1 else a

    def column_grad(g, groups):
        width = g.shape[1] // groups
        g = g.astype(BF16).reshape(2, 2, seqs, -1, groups * width)
        keep = lax.dynamic_index_in_dim(g, core, 1, False)
        recv = from_core(lax.dynamic_index_in_dim(g, 1 - core, 1, False))
        both = (keep.astype(F32) + recv.astype(F32)).astype(BF16)
        both = both.transpose(1, 0, 2, 3).reshape(-1, groups * width)
        part = lax.psum_scatter(both, "z", scatter_dimension=0, tiled=True)
        part = over_reps(part).reshape(2, -1, groups * width)
        keep = lax.dynamic_index_in_dim(part, y, 0, False)
        recv = from_y(lax.dynamic_index_in_dim(part, 1 - y, 0, False))
        ours = jnp.where(y == 0, jnp.stack([keep, recv]), jnp.stack([recv, keep]))
        theirs = from_x(ours)
        rows = ours.shape[1]
        ours = ours.reshape(2, rows, groups, width)
        theirs = theirs.reshape(2, rows, groups, width)
        full = jnp.where(x == 0, jnp.stack([ours, theirs], 1), jnp.stack([theirs, ours], 1))
        return full.transpose(2, 3, 0, 1, 4).reshape(rows, groups, 4 * width).astype(F32)

    def row_grad(g):
        rows, half = g.shape[0] // seqs, g.shape[1] // 2
        g = g.astype(BF16)
        keep = lax.dynamic_slice_in_dim(g, core * half, half, 1)
        recv = from_core(lax.dynamic_slice_in_dim(g, (1 - core) * half, half, 1))
        both = (keep.astype(F32) + recv.astype(F32)).astype(BF16)
        part = lax.psum_scatter(both, "z", scatter_dimension=0, tiled=True)
        part = over_reps(part)
        other = from_x(part)
        ours = jnp.where(core == x, part, other)
        theirs = from_core(jnp.where(core == x, other, part))
        full = jnp.where(
            core == 0,
            jnp.concatenate([ours, theirs], 1),
            jnp.concatenate([theirs, ours], 1),
        )
        return full.astype(F32)

    mods = modulation + time_mod[0]
    shift1, scale1, gate1, shift2, scale2, gate2 = [mods[i] for i in range(6)]

    self_normed, self_inverse = layer_norm(states)
    self_in = (self_normed * (1.0 + scale1) + shift1).astype(BF16)
    x_self = gather4(self_in)
    tables = gather4(jnp.concatenate(rope_tables(grid_pos), 1))
    cosine, sine = tables[..., :HD], tables[..., HD:]
    full_qkv = column_block(w_qkv)
    full_out = row_block(w_out)
    full_cross = column_block(w_cross)
    full_crossout = row_block(w_crossout)
    full_up = column_block(w_up[:, None, :])
    full_down = row_block(w_down)
    bias = pick(attn_bias)
    gain = pick(qk_gain)
    width = bias.shape[1]
    heads = width // HD

    def rms_scale(v):
        return lax.rsqrt(v / dim + EPS)[..., None]

    project = mm(x_self, full_qkv)
    q_pre = project[..., :width] + bias[0]
    k_pre = project[..., width : 2 * width] + bias[1]
    value = (project[..., 2 * width :] + bias[2]).astype(BF16)
    squares = sum4(jnp.stack([jnp.sum(q_pre * q_pre, -1), jnp.sum(k_pre * k_pre, -1)], 1))
    q_inv, k_inv = rms_scale(squares[:, 0]), rms_scale(squares[:, 1])
    q_unit, k_unit = q_pre * q_inv, k_pre * k_inv
    query = turn(q_unit * gain[0], cosine, sine).astype(BF16)
    key = turn(k_unit * gain[1], cosine, sine).astype(BF16)
    packed = heads_swap(reorder(jnp.concatenate([query, key, value], -1)))
    packed = packed.reshape(-1, 3, heads, HD)
    q_h, k_h, v_h = packed[:, 0], packed[:, 1], packed[:, 2]
    scores = jnp.einsum("qhd,khd->hqk", q_h, k_h, preferred_element_type=F32) * SCALE
    top = jnp.max(scores, -1, keepdims=True)
    weight = jnp.exp(scores - top)
    total = jnp.sum(weight, -1, keepdims=True)
    probs = weight / total
    mixed = jnp.einsum("hqk,khd->qhd", probs.astype(BF16), v_h, preferred_element_type=F32)
    self_lse = top + jnp.log(total)
    mixed = mixed.astype(BF16).reshape(seqs, -1, width)
    mixed = reorder(heads_swap(mixed))
    branch = reduce4(lambda k: mm(mixed[k], full_out)) + attn_bias[3]
    after_self = states + branch * gate1

    x_text = gather4(text_emb)
    text_proj = mm(x_text, full_cross[:, width:])
    ck_pre = text_proj[..., :width] + bias[5]
    cross_v = (text_proj[..., width:] + bias[6]).astype(BF16)
    ck_inv = rms_scale(sum4(jnp.sum(ck_pre * ck_pre, -1)))
    ck_unit = ck_pre * ck_inv
    cross_k = (ck_unit * gain[3]).astype(BF16)
    text_kv = lax.all_gather(jnp.concatenate([cross_k, cross_v], -1), "z", axis=1, tiled=True)
    text_kv = text_kv.reshape(4, -1, 2, heads, HD)
    ck_h, cv_h = text_kv[:, :, 0], text_kv[:, :, 1]

    cross_normed, cross_inverse = layer_norm(after_self)
    cross_in = (cross_normed * norm_gain + norm_bias).astype(BF16)
    x_cross = gather4(cross_in)
    cq_pre = mm(x_cross, full_cross[:, :width]) + bias[4]
    cq_inv = rms_scale(sum4(jnp.sum(cq_pre * cq_pre, -1)))
    cq_unit = cq_pre * cq_inv
    cross_q = (cq_unit * gain[2]).astype(BF16)
    rows = cross_q.shape[1]
    cq_h = cross_q.reshape(4, rows, heads, HD)
    c_scores = jnp.einsum("cqhd,ckhd->chqk", cq_h, ck_h, preferred_element_type=F32) * SCALE
    c_top = jnp.max(c_scores, -1, keepdims=True)
    c_weight = jnp.exp(c_scores - c_top)
    c_total = jnp.sum(c_weight, -1, keepdims=True)
    c_probs = c_weight / c_total
    cross_mix = jnp.einsum("chqk,ckhd->cqhd", c_probs.astype(BF16), cv_h, preferred_element_type=F32)
    cross_mix = cross_mix.astype(BF16).reshape(4, rows, width)
    c_lse = c_top + jnp.log(c_total)
    cross_out = reduce4(lambda k: mm(cross_mix[k], full_crossout)) + attn_bias[7]
    after_cross = after_self + cross_out

    ffn_normed, ffn_inverse = layer_norm(after_cross)
    ffn_in = (ffn_normed * (1.0 + scale2) + shift2).astype(BF16)
    d_ffnout = (out_grad * gate2).astype(BF16)
    g_ffn = gather4(d_ffnout)
    x_ffn = gather4(ffn_in)
    hidden_pre = mm(x_ffn, full_up) + pick(up_bias)
    root = math.sqrt(2.0 / math.pi)
    bent = jnp.tanh(root * (hidden_pre + 0.044715 * hidden_pre**3))
    hidden = (0.5 * hidden_pre * (1.0 + bent)).astype(BF16)
    slope = 0.5 * (1.0 + bent) + 0.5 * hidden_pre * (1.0 - bent * bent) * root * (
        1.0 + 3.0 * 0.044715 * hidden_pre * hidden_pre
    )
    d_hpre32 = mm_t(g_ffn, full_down) * slope
    d_hpre = d_hpre32.astype(BF16)
    d_ffnin = reduce4(lambda k: mm_t(d_hpre[k], full_up))
    ffn_out = reduce4(lambda k: mm(hidden[k], full_down)) + down_bias
    block_out = after_cross + ffn_out * gate2
    up_grad = column_grad(outer(x_ffn, d_hpre), 1)[:, 0]
    down_grad = row_grad(outer(hidden, g_ffn))
    d_cross = out_grad + norm_backward(ffn_normed, ffn_inverse, d_ffnin * (1.0 + scale2))

    d_crossout = d_cross.astype(BF16)
    g_cross = gather4(d_crossout)
    d_cmix = mm_t(g_cross, full_crossout).astype(BF16)
    d_cmix_h = d_cmix.reshape(4, rows, heads, HD)
    c_scores = jnp.einsum("cqhd,ckhd->chqk", cq_h, ck_h, preferred_element_type=F32) * SCALE
    c_probs = jnp.exp(c_scores - c_lse)
    c_dp = jnp.einsum("cqhd,ckhd->chqk", d_cmix_h, cv_h, preferred_element_type=F32)
    c_ds = (c_probs * (c_dp - jnp.sum(c_probs * c_dp, -1, keepdims=True))).astype(BF16)
    d_cqn = jnp.einsum("chqk,ckhd->cqhd", c_ds, ck_h, preferred_element_type=F32) * SCALE
    d_ckn = jnp.einsum("chqk,cqhd->ckhd", c_ds, cq_h, preferred_element_type=F32) * SCALE
    d_cvn = jnp.einsum("chqk,cqhd->ckhd", c_probs.astype(BF16), d_cmix_h, preferred_element_type=F32)
    d_ckv = jnp.concatenate([d_ckn.reshape(4, -1, width), d_cvn.reshape(4, -1, width)], -1)
    d_ckv = d_ckv.astype(BF16).reshape(4, seqs, -1, 2 * width).transpose(1, 0, 2, 3)
    d_ckv = lax.psum_scatter(d_ckv, "z", scatter_dimension=0, tiled=True)[0]

    def rms_back(grad, unit, inverse, scale, extra_sum):
        d_unit = grad * scale
        mean = extra_sum / dim
        return inverse * (d_unit - unit * mean[..., None])

    def inner(grad, unit, scale):
        return jnp.sum(grad * scale * unit, -1)

    d_cqn = d_cqn.reshape(4, rows, width)
    cq_stat = sum4(inner(d_cqn, cq_unit, gain[2]))
    d_cq = rms_back(d_cqn, cq_unit, cq_inv, gain[2], cq_stat).astype(BF16)
    cq_gain = jnp.sum(d_cqn * cq_unit, (0, 1))
    d_crossin = reduce4(lambda k: mm_t(d_cq[k], full_cross[:, :width]))

    d_ckn = d_ckv[..., :width].astype(F32)
    d_cv = d_ckv[..., width:]
    ck_stat = sum4(inner(d_ckn, ck_unit, gain[3]))
    d_ck = rms_back(d_ckn, ck_unit, ck_inv, gain[3], ck_stat).astype(BF16)
    ck_gain = jnp.sum(d_ckn * ck_unit, (0, 1))
    d_text = jnp.concatenate([d_ck, d_cv], -1)
    text_grad = reduce4(lambda k: mm_t(d_text[k], full_cross[:, width:]))
    cross_grad = column_grad(
        jnp.concatenate([outer(x_cross, d_cq), outer(x_text, d_text)], 1), 3
    )
    crossout_grad = row_grad(outer(cross_mix, g_cross))
    d_self = d_cross + norm_backward(cross_normed, cross_inverse, d_crossin * norm_gain)

    d_branch = (d_self * gate1).astype(BF16)
    g_self = gather4(d_branch)
    d_mix = mm_t(g_self, full_out).astype(BF16)
    d_mix_h = heads_swap(reorder(d_mix)).reshape(-1, heads, HD)
    scores = jnp.einsum("qhd,khd->hqk", q_h, k_h, preferred_element_type=F32) * SCALE
    probs = jnp.exp(scores - self_lse)
    dp = jnp.einsum("qhd,khd->hqk", d_mix_h, v_h, preferred_element_type=F32)
    ds = (probs * (dp - jnp.sum(probs * dp, -1, keepdims=True))).astype(BF16)
    dq = jnp.einsum("hqk,khd->qhd", ds, k_h, preferred_element_type=F32) * SCALE
    dk = jnp.einsum("hqk,qhd->khd", ds, q_h, preferred_element_type=F32) * SCALE
    dv = jnp.einsum("hqk,qhd->khd", probs.astype(BF16), d_mix_h, preferred_element_type=F32)
    d_packed = jnp.stack([dq, dk, dv], 1).astype(BF16).reshape(seqs, -1, 3 * width)
    d_packed = reorder(heads_swap(d_packed))
    d_value = d_packed[..., 2 * width :]
    d_qn = turn(d_packed[..., :width].astype(F32), cosine, -sine)
    d_kn = turn(d_packed[..., width : 2 * width].astype(F32), cosine, -sine)
    stats = sum4(jnp.stack([inner(d_qn, q_unit, gain[0]), inner(d_kn, k_unit, gain[1])], 1))
    d_q = rms_back(d_qn, q_unit, q_inv, gain[0], stats[:, 0]).astype(BF16)
    d_k = rms_back(d_kn, k_unit, k_inv, gain[1], stats[:, 1]).astype(BF16)
    q_gain = jnp.sum(d_qn * q_unit, (0, 1))
    k_gain = jnp.sum(d_kn * k_unit, (0, 1))
    d_qkv = jnp.concatenate([d_q, d_k, d_value], -1)
    d_selfin = reduce4(lambda k: mm_t(d_qkv[k], full_qkv))
    qkv_grad = column_grad(outer(x_self, d_qkv), 3)
    outproj_grad = row_grad(outer(mixed, g_self))
    states_grad = d_self + norm_backward(self_normed, self_inverse, d_selfin * (1.0 + scale1))

    def column_sum(v):
        return jnp.sum(v.astype(F32), tuple(range(v.ndim - 1)))

    def over_z(v):
        v = v + lax.ppermute(v, "z", [(i, i ^ 1) for i in range(seqs)])
        return v + lax.ppermute(v, "z", [(i, i ^ 2) for i in range(seqs)])

    def over_clips(v):
        v = v + from_core(v)
        v = v + from_x(v)
        v = v + from_y(v)
        return over_reps(v)

    early = jnp.stack(
        [
            column_sum(d_ffnin),
            column_sum(d_ffnin * ffn_normed),
            column_sum(out_grad * ffn_out),
            spread(column_sum(d_cq)),
            spread(column_sum(d_ck)),
            spread(column_sum(d_cv)),
            column_sum(d_crossout),
            spread(cq_gain),
            spread(ck_gain),
            column_sum(d_crossin * cross_normed),
            column_sum(d_crossin),
            column_sum(d_ffnout),
            column_sum(d_branch),
            column_sum(d_self * branch),
        ]
    )
    upbias = over_clips(over_z(spread(column_sum(d_hpre))))
    early_clip = over_z(early)
    early_all = over_clips(early_clip)
    late = jnp.stack(
        [
            column_sum(d_selfin),
            column_sum(d_selfin * self_normed),
            spread(column_sum(d_q)),
            spread(column_sum(d_k)),
            spread(column_sum(d_value)),
            spread(q_gain),
            spread(k_gain),
        ]
    )
    late_clip = over_z(late)
    late_all = over_clips(late_clip)

    def mod_rows(e, l):
        return jnp.stack([l[0], l[1], e[13], e[0], e[1], e[2]])

    time_grad = mod_rows(early_clip, late_clip)[None]
    mod_grad = mod_rows(early_all, late_all)
    bias_grad = jnp.stack(
        [late_all[2], late_all[3], late_all[4], early_all[12]] + [early_all[i] for i in (3, 4, 5, 6)]
    )
    gain_grad = jnp.stack([late_all[5], late_all[6], early_all[7], early_all[8]])
    return (
        block_out,
        states_grad,
        text_grad,
        time_grad,
        qkv_grad,
        outproj_grad,
        cross_grad,
        crossout_grad,
        up_grad,
        down_grad,
        bias_grad,
        gain_grad,
        early_all[9],
        early_all[10],
        upbias,
        early_all[11],
        mod_grad,
    )


def solution(mesh):
    reps, shards, seqs = mesh.shape["replica"], mesh.shape["shard"], mesh.shape["seq"]
    fine = Mesh(
        mesh.devices.reshape(reps // 2, 2, shards // 2, 2, seqs), ("rep", "x", "y", "core", "z")
    )
    tokens = P(("rep", "x", "y", "core", "z"), None)
    clips = P(("rep", "x", "y", "core"), None, None)
    rows2 = P(("y", "core", "z"), None)
    rows3 = P(("y", "core", "z"), None, None)
    return jax.shard_map(
        on_device,
        mesh=fine,
        in_specs=(
            tokens, tokens, P(None, ("rep", "x", "y", "core", "z")), clips,
            rows3, rows2, rows3, rows2, rows2, rows2,
            P(), P(), P(), P(), P(), P(), P(), tokens,
        ),
        out_specs=(
            tokens, tokens, tokens, clips,
            rows3, rows2, rows3, rows2, rows2, rows2,
            P(), P(), P(), P(), P(), P(), P(),
        ),
        check_vma=False,
    )
```

```python
import math
from types import SimpleNamespace

import jax
import jax.numpy as jnp
import numpy as np
from jax import lax
from jax.experimental import pallas as pl
from jax.experimental.pallas import tpu as pltpu
from jax.experimental.layout import Layout, with_layout_constraint
from jax.sharding import Mesh, PartitionSpec as P

HD = 128
EPS = 1e-06
F32 = jnp.float32
BF16 = jnp.bfloat16
SCALE = 1.0 / math.sqrt(HD)
SWAP = [(0, 1), (1, 0)]
ROWS = 16
FLOPS = 1_150_000_000
BYTES = 3_600_000


def rope_tables(grid_pos):
    pairs = HD // 2
    width = pairs // 3
    first = pairs - 2 * width
    index = np.arange(pairs)
    part = np.where(index < first, 0, np.where(index < first + width, 1, 2))
    offset = np.where(part == 0, index, np.where(part == 1, index - first, index - first - width))
    frequency = 10000.0 ** (-offset / np.where(part == 0, first, width))
    position = grid_pos.astype(F32)
    angles = 0.0
    for axis in range(3):
        lane = np.repeat(frequency * (part == axis), 2)
        angles = angles + position[axis][:, None] * jnp.asarray(lane, F32)[None, :]
    sign = np.where(np.arange(HD) % 2 == 0, -1.0, 1.0)
    return jnp.cos(angles), jnp.sin(angles) * jnp.asarray(sign, F32)[None, :]


def layer_norm(values):
    center = values - jnp.mean(values, -1, keepdims=True)
    inverse = lax.rsqrt(jnp.mean(center * center, -1, keepdims=True) + EPS)
    return center * inverse, inverse


def norm_backward(normed, inverse, grad_in):
    return inverse * (
        grad_in
        - jnp.mean(grad_in, -1, keepdims=True)
        - normed * jnp.mean(grad_in * normed, -1, keepdims=True)
    )


def mm(a, b):
    return lax.dot_general(a, b, (((a.ndim - 1,), (0,)), ((), ())), preferred_element_type=F32)


def mm_t(a, b):
    return lax.dot_general(a, b, (((a.ndim - 1,), (1,)), ((), ())), preferred_element_type=F32)


def rows_mm(a, w):
    return jnp.concatenate([mm(a, w[0]), mm(a, w[1])], -1)


def after(value, *done):
    return lax.optimization_barrier((value, done))[0]


def outer(a, b):
    lead = tuple(range(a.ndim - 1))
    return lax.dot_general(a, b, ((lead, lead), ((), ())), preferred_element_type=F32)


def column_chunks(total, size):
    return [(at, min(size, total - at)) for at in range(0, total, size)]


class Links:
    def __init__(self, named, stats, line):
        self.named = named
        self.used = 0
        self.started = []
        self.x, self.y, self.z = [lax.axis_index(n) for n in ("x", "y", "z")]
        self.seqs = lax.axis_size("z")
        barrier = pltpu.get_barrier_semaphore()
        peers = [{"x": 1 - self.x}, {"y": 1 - self.y}]
        if stats:
            peers.append({"x": 1 - self.x, "y": 1 - self.y})
        if line:
            peers += [{"z": (self.z + step) % self.seqs} for step in range(1, self.seqs)]
        for peer in peers:
            pl.semaphore_signal(
                barrier, inc=1, device_id=peer, device_id_type=pl.DeviceIdType.MESH
            )
        pl.semaphore_wait(barrier, len(peers))

    def clip_of(self, piece):
        return ((piece // 2 + self.x) % 2) * 2 + (piece % 2 + self.y) % 2

    def send(self, axis, src, dst):
        where = {a: 1 - lax.axis_index(a) for a in axis}
        index = self.used
        self.used += 1
        sems = self.named.sems
        copy = pltpu.make_async_remote_copy(
            src_ref=src,
            dst_ref=dst,
            send_sem=sems.at[0, index],
            recv_sem=sems.at[1, index],
            device_id=where,
            device_id_type=pl.DeviceIdType.MESH,
        )
        copy.start()
        self.started.append((None, copy))
        return copy

    def send_line(self, src, dst, to, slot, lane=0):
        sems = self.named.line
        copy = pltpu.make_async_remote_copy(
            src_ref=src,
            dst_ref=dst,
            send_sem=sems.at[0, lane, slot],
            recv_sem=sems.at[1, lane, self.z],
            device_id={"z": to},
            device_id_type=pl.DeviceIdType.MESH,
        )

        @pl.when(to != self.z)
        def _():
            copy.start()

        @pl.when(to == self.z)
        def _():
            dst[...] = src[...]

        self.started.append((to != self.z, copy))

    def wait_line(self, ref, source, lane=0):
        sems = self.named.line
        copy = pltpu.make_async_remote_copy(
            src_ref=ref,
            dst_ref=ref,
            send_sem=sems.at[0, lane, 0],
            recv_sem=sems.at[1, lane, source],
            device_id={"z": (self.z + 1) % self.seqs},
            device_id_type=pl.DeviceIdType.MESH,
        )

        @pl.when(source != self.z)
        def _():
            copy.wait_recv()

    def finish(self):
        for needed, copy in self.started:
            if needed is None:
                copy.wait_send()
            else:
                pl.when(needed)(copy.wait_send)


def split_rows(tokens):
    return ((tokens // 2 + ROWS - 1) // ROWS) * ROWS


def row_steps(tokens, body):
    @pl.loop(0, tokens // ROWS)
    def _(step):
        body(pl.ds(pl.multiple_of(step * ROWS, ROWS), ROWS), step)


def reduce_slice(links, refs, partial, middle, keep=None):
    mine, near, far, total = refs.mine, refs.near, refs.far, refs.total
    tokens = total.shape[0]
    half = split_rows(tokens)
    top, low = pl.ds(0, half), pl.ds(half, tokens - half)

    def store_low(slot):
        def store(columns, value):
            mine[slot, :, columns] = value.astype(BF16)

        return store

    def store_full(columns, value):
        total[:, columns] = value

    partial(refs, 3, store_low(2))
    far_x = links.send("x", mine.at[2, top], far.at[top])
    far_y = links.send("y", mine.at[2, low], far.at[low])
    partial(refs, 2, store_low(1))
    x_top = links.send("x", mine.at[1, top], near.at[1, top])
    partial(refs, 1, store_low(0))
    y_low = links.send("y", mine.at[0, low], near.at[0, low])
    far_x.wait_recv()
    mine[0, top] = (mine[0, top].astype(F32) + far[top].astype(F32)).astype(BF16)
    y_top = links.send("y", mine.at[0, top], near.at[0, top])
    far_y.wait_recv()
    mine[1, low] = (mine[1, low].astype(F32) + far[low].astype(F32)).astype(BF16)
    x_low = links.send("x", mine.at[1, low], near.at[1, low])
    partial(refs, 0, store_full)
    for copy in (x_top, y_low, y_top, x_low):
        copy.wait_recv()

    def body(rows, step):
        value = total[rows] + near[0, rows].astype(F32) + near[1, rows].astype(F32)
        sent = middle(refs, rows, step, value)
        if keep is not None:
            keep[0, rows] = sent

    row_steps(tokens, body)


def gather_begin(links, held):
    return links.send("x", held.at[0], held.at[2]), links.send("y", held.at[0], held.at[1])


def gather_relay(links, held, first):
    tokens = held.shape[1]
    half = split_rows(tokens)
    top, low = pl.ds(0, half), pl.ds(half, tokens - half)
    from_x, from_y = first
    from_x.wait_recv()
    far_top = links.send("y", held.at[2, top], held.at[3, top])
    from_y.wait_recv()
    far_low = links.send("x", held.at[1, low], held.at[3, low])
    return far_top, far_low


def gather_end(far):
    for copy in far:
        copy.wait_recv()


def gather_slice(links, refs, held, product, also=()):
    arrays = (held,) + tuple(also)
    first = [gather_begin(links, array) for array in arrays]
    product(refs, 0, held.at[0])
    far = [gather_relay(links, array, copies) for array, copies in zip(arrays, first)]
    product(refs, 1, held.at[1])
    product(refs, 2, held.at[2])
    for copies in far:
        gather_end(copies)
    product(refs, 3, held.at[3])


def sum_stats(links, refs):
    stat, other = refs.stat, refs.stats_in
    copies = [
        links.send("y", stat, other.at[0]),
        links.send("x", stat, other.at[1]),
        links.send("xy", stat, other.at[2]),
    ]
    for copy in copies:
        copy.wait_recv()
    for copy in copies:
        copy.wait_send()
    del links.started[-3:]
    for k in range(4):
        refs.stat_sum[k] = (
            stat[k] + other[0, k ^ 1] + other[1, k ^ 2] + other[2, k ^ 3]
        )


def to_row(column):
    size = column.shape[0]
    same = lax.broadcasted_iota(jnp.int32, (size, size), 0) == lax.broadcasted_iota(
        jnp.int32, (size, size), 1
    )
    return jnp.sum(jnp.where(same, column, 0.0), 0, keepdims=True)


def to_column(row):
    size = row.shape[1]
    same = lax.broadcasted_iota(jnp.int32, (size, size), 0) == lax.broadcasted_iota(
        jnp.int32, (size, size), 1
    )
    return jnp.sum(jnp.where(same, row, 0.0), 1, keepdims=True)


def run_kernel(name, cid, inputs, outputs, body, scratch, cost, stats=False, line=0):
    names_in, names_out = list(inputs), list(outputs)
    spaces = dict(sems=pltpu.SemaphoreType.DMA((2, 24)))
    if line:
        spaces.update(line=pltpu.SemaphoreType.DMA((2, line, 4)))
    if stats:
        spaces.update(
            stat=pltpu.VMEM((4, 8, 256), F32),
            stat_sum=pltpu.VMEM((4, 8, 256), F32),
            stats_in=pltpu.VMEM((3, 4, 8, 256), F32),
        )
    for key, (shape, dtype) in scratch.items():
        spaces[key] = pltpu.VMEM(shape, dtype)

    def kernel(*refs):
        named = SimpleNamespace(**dict(zip(names_in + names_out + list(spaces), refs)))
        links = Links(named, stats, line)
        body(links, named)
        links.finish()

    vmem = pl.BlockSpec(memory_space=pltpu.VMEM)
    result = pl.pallas_call(
        kernel,
        name=name,
        out_shape=[jax.ShapeDtypeStruct(*outputs[n]) for n in names_out],
        in_specs=[vmem] * len(names_in),
        out_specs=[vmem] * len(names_out),
        scratch_shapes=list(spaces.values()),
        cost_estimate=pl.CostEstimate(
            flops=cost * FLOPS, bytes_accessed=cost * BYTES, transcendentals=0
        ),
        compiler_params=pltpu.CompilerParams(
            collective_id=cid, has_side_effects=True, vmem_limit_bytes=60 * 1024 * 1024
        ),
    )(*[inputs[n] for n in names_in])
    return SimpleNamespace(**dict(zip(names_out, result)))


def reduce_scratch(tokens, dim):
    return dict(
        mine=((3, tokens, dim), BF16),
        near=((2, tokens, dim), BF16),
        far=((tokens, dim), BF16),
        total=((tokens, dim), F32),
    )


def add_rows(ref, index, value, step):
    @pl.when(step == 0)
    def _():
        ref[index] = jnp.zeros_like(ref[index])

    ref[index] += value[:8] + value[8:]


def fold_rows(value):
    return jnp.sum(value.reshape(value.shape[0] // 8, 8, value.shape[1]), 0)


def rows_partial(a, w):
    def partial(refs, k, store):
        piece = getattr(refs, a)[k]
        width = getattr(refs, w).shape[2]
        for half in range(2):
            for at, size in column_chunks(width, 384):
                store(
                    pl.ds(half * width + at, size),
                    mm(piece, getattr(refs, w)[half, :, pl.ds(at, size)]),
                )

    return partial


def turned_partial(a, w, size=256):
    def partial(refs, k, store):
        deep = getattr(refs, a).shape[2]

        @pl.loop(0, getattr(refs, w).shape[0] // size)
        def _(step):
            rows = pl.ds(pl.multiple_of(step * size, size), size)
            store(rows, mm_t(getattr(refs, a)[k], getattr(refs, w)[rows, pl.ds(0, deep)]))

    return partial


def rows_turned(piece, w):
    width = w.shape[2]
    return mm_t(piece[:, pl.ds(0, width)], w[0]) + mm_t(piece[:, pl.ds(width, width)], w[1])


def mm_l(a, b):
    return lax.dot_general(a, b, (((0,), (0,)), ((), ())), preferred_element_type=F32)


def swap_pairs(values):
    even = lax.broadcasted_iota(jnp.int32, values.shape, 1) % 2 == 0
    return jnp.where(even, pltpu.roll(values, HD - 1, 1), pltpu.roll(values, 1, 1))


def softmax(scores):
    weight = jnp.exp(scores - jnp.max(scores, -1, keepdims=True))
    return weight * (1.0 / jnp.sum(weight, -1, keepdims=True))


def head_at(h, base=0):
    return pl.ds(base + h * HD, HD)


def on_device(
    states, text_emb, grid_pos, time_mod, w_qkv, w_out, w_cross, w_crossout, w_up, w_down,
    attn_bias, qk_gain, norm_gain, norm_bias, up_bias, down_bias, modulation, out_grad,
):
    x, y, core = lax.axis_index("x"), lax.axis_index("y"), lax.axis_index("core")
    seqs = lax.axis_size("z")
    reps = lax.axis_size("rep")
    own_tokens, dim = states.shape
    tokens = -(-own_tokens // ROWS) * ROWS
    block = y * 2 + x
    pad = ((0, tokens - own_tokens), (0, 0))
    states_p = jnp.pad(states, pad)
    out_grad_p = jnp.pad(out_grad, pad)

    def from_y(a):
        return lax.ppermute(a, "y", SWAP)

    def from_x(a):
        return lax.ppermute(a, "x", SWAP)

    def from_xy(a):
        return lax.ppermute(a, ("x", "y"), [(i, 3 - i) for i in range(4)])

    def from_core(a):
        return lax.ppermute(a, "core", SWAP)

    def gather4(a):
        far, xs, ys = from_xy(a), from_x(a), from_y(a)
        return jnp.stack([a, ys, xs, far])

    def reduce4(term):
        far = from_xy(term(3).astype(BF16))
        xs = from_x(term(2).astype(BF16))
        ys = from_y(term(1).astype(BF16))
        return term(0) + ys.astype(F32) + xs.astype(F32) + far.astype(F32)

    def sum4(stat):
        far, xs, ys = from_xy(stat), from_x(stat), from_y(stat)
        return (
            stat
            + jnp.stack([ys[1], ys[0], ys[3], ys[2]])
            + jnp.stack([xs[2], xs[3], xs[0], xs[1]])
            + jnp.stack([far[3], far[2], far[1], far[0]])
        )

    def pick(v, blocks=4):
        return lax.dynamic_index_in_dim(
            v.reshape(v.shape[:-1] + (blocks, v.shape[-1] // blocks)), block, v.ndim - 1, False
        )

    def spread(v):
        hot = (jnp.arange(4) == block).astype(F32)
        full = v[..., None, :] * hot[:, None]
        return full.reshape(v.shape[:-1] + (4 * v.shape[-1],))

    def column_block(w, *done):
        rows, groups, width = w.shape[0], w.shape[1], w.shape[2] // 4
        mine = lax.dynamic_index_in_dim(w.reshape(rows, groups, 2, 2, width), x, 3, False)
        keep = lax.dynamic_index_in_dim(mine, y, 2, False).reshape(rows, groups * width)
        send = lax.dynamic_index_in_dim(mine, 1 - y, 2, False).reshape(rows, groups * width)
        recv = from_y(send)
        both = jnp.where(y == 0, jnp.stack([keep, recv]), jnp.stack([recv, keep]))
        full = lax.all_gather(after(both, *done), ("core", "z"), axis=1, tiled=True)
        return full.reshape(-1, groups * width)

    def row_block(w, *done):
        rows, half = w.shape[0], w.shape[1] // 2
        keep = lax.dynamic_slice_in_dim(w, core * half, half, 1)
        recv = from_core(lax.dynamic_slice_in_dim(w, (1 - core) * half, half, 1))
        mine = jnp.where(core == x, keep, recv)
        full = lax.all_gather(after(mine, *done), ("core", "z"), axis=0, tiled=True)
        return full.reshape(2, seqs * rows, half)

    def over_reps(a):
        return lax.psum(a, "rep") if reps > 1 else a

    def column_core(g):
        g = g.astype(BF16).reshape(2, 2, seqs, -1, g.shape[1])
        keep = lax.dynamic_index_in_dim(g, core, 1, False)
        recv = from_core(lax.dynamic_index_in_dim(g, 1 - core, 1, False))
        both = (keep.astype(F32) + recv.astype(F32)).astype(BF16)
        return both.transpose(1, 0, 2, 3).reshape(-1, g.shape[4])

    def row_core(g):
        half = g.shape[1] // 2
        g = g.astype(BF16)
        keep = lax.dynamic_slice_in_dim(g, core * half, half, 1)
        recv = from_core(lax.dynamic_slice_in_dim(g, (1 - core) * half, half, 1))
        return (keep.astype(F32) + recv.astype(F32)).astype(BF16)

    def scatter_z(a):
        return over_reps(lax.psum_scatter(a, "z", scatter_dimension=0, tiled=True))

    def column_done(part, groups):
        width = part.shape[1] // groups
        part = part.reshape(2, -1, groups * width)
        keep = lax.dynamic_index_in_dim(part, y, 0, False)
        recv = from_y(lax.dynamic_index_in_dim(part, 1 - y, 0, False))
        ours = jnp.where(y == 0, jnp.stack([keep, recv]), jnp.stack([recv, keep]))
        theirs = from_x(ours)
        rows = ours.shape[1]
        ours = ours.reshape(2, rows, groups, width)
        theirs = theirs.reshape(2, rows, groups, width)
        full = jnp.where(x == 0, jnp.stack([ours, theirs], 1), jnp.stack([theirs, ours], 1))
        return full.transpose(2, 3, 0, 1, 4).reshape(rows, groups, 4 * width).astype(F32)

    def row_done(part):
        other = from_x(part)
        ours = jnp.where(core == x, part, other)
        theirs = from_core(jnp.where(core == x, other, part))
        full = jnp.where(
            core == 0,
            jnp.concatenate([ours, theirs], 1),
            jnp.concatenate([theirs, ours], 1),
        )
        return full.astype(F32)

    mods = modulation + time_mod[0]
    shift1, scale1, gate1, shift2, scale2, gate2 = [mods[i] for i in range(6)]

    def vectors(*rows):
        return jnp.stack(rows + (jnp.zeros_like(rows[0]),) * (8 - len(rows)))

    full_qkv = column_block(w_qkv)
    full_out = row_block(w_out, full_qkv)
    full_cross = column_block(w_cross, full_qkv)
    text_z = lax.all_gather(after(text_emb, full_qkv), "z", axis=0, tiled=True)
    full_crossout = row_block(w_crossout, full_qkv)
    full_up = column_block(w_up[:, None, :], full_qkv)
    full_down = row_block(w_down, full_qkv)
    bias = pick(attn_bias)
    gain = pick(qk_gain)
    width = bias.shape[1]
    heads = width // HD
    hidden_width = full_up.shape[1]
    own_tables = jnp.pad(jnp.concatenate(rope_tables(grid_pos), 1), pad)
    d_ffnout = (out_grad_p * gate2).astype(BF16)

    def rms_scale(v):
        return lax.rsqrt(v / dim + EPS)[..., None]

    wide = ((tokens, dim), F32)
    held = ((4, tokens, dim), BF16)
    head_block = ((4, tokens, width), F32)

    blocks3 = 3 * width
    clip_rows = seqs * tokens

    def middle(refs, rows):
        normed, _ = layer_norm(refs.states[rows])
        vec = refs.vec
        return (normed * vec[0:1] + vec[1:2]).astype(BF16)

    def body(links, refs):
        refs.stat[...] = jnp.zeros_like(refs.stat)

        def rows_in(rows, step):
            refs.held[0, rows] = middle(refs, rows)

        def send_heads(k, columns, lane):
            links.send_line(
                refs.sent.at[k, :, columns], refs.packed.at[links.z, :, columns],
                links.clip_of(k), k, lane,
            )

        early, late = pl.ds(2 * width, width), pl.ds(0, 2 * width)

        def product(refs, k, piece):
            pre = mm(piece[...], refs.w[:, early]) + refs.bias[0:1, early]
            refs.sent[k, :, early] = pre.astype(BF16)
            send_heads(k, early, 0)
            for part in range(2):
                columns = pl.ds(part * width, width)
                pre = mm(piece[...], refs.w[:, columns]) + refs.bias[0:1, columns]
                refs.unit[k, :, columns] = pre
                square = jnp.sum(pre * pre, -1, keepdims=True)
                refs.stat[k, pl.ds(part, 1), pl.ds(0, tokens)] = to_row(square)

        refs.tables[0] = refs.own_tables[...]
        refs.grads[0] = refs.own_grads[...]
        row_steps(tokens, rows_in)
        gather_slice(links, refs, refs.held, product, (refs.tables,))
        sum_stats(links, refs)
        refs.inv[...] = lax.rsqrt(refs.stat_sum[...] / dim + EPS)
        first = gather_begin(links, refs.grads)
        for k in (3, 2, 1, 0):
            cosine, sine = refs.tables[k, :, pl.ds(0, HD)], refs.tables[k, :, pl.ds(HD, HD)]
            for part in range(2):
                inverse = to_column(refs.inv[k, pl.ds(part, 1), pl.ds(0, tokens)])
                for h in range(heads):
                    at = head_at(h, part * width)
                    unit = refs.unit[k, :, at] * inverse
                    refs.unit[k, :, at] = unit
                    scaled = unit * refs.gain[pl.ds(part, 1), head_at(h)]
                    turned = scaled * cosine + swap_pairs(scaled) * sine
                    refs.sent[k, :, at] = turned.astype(BF16)
            send_heads(k, late, 1)
        gather_end(gather_relay(links, refs.grads, first))
        for source in range(seqs):
            links.wait_line(refs.packed.at[source, :, early], source, 0)
            links.wait_line(refs.packed.at[source, :, late], source, 1)

    gains8 = jnp.pad(gain, ((0, 4), (0, 0)))
    first = run_kernel(
        "self_in", 1,
        dict(
            states=states_p, vec=vectors(1.0 + scale1, shift1), w=full_qkv,
            bias=jnp.broadcast_to(bias[:3].reshape(1, -1), (8, blocks3)),
            gain=gains8, own_tables=own_tables, own_grads=d_ffnout,
        ),
        dict(
            held=held, unit=((4, tokens, 2 * width), F32), inv=((4, 8, 256), F32),
            packed=((seqs, tokens, blocks3), BF16), grads=held,
            tables=((4, tokens, 2 * HD), F32),
        ),
        body, dict(sent=((4, tokens, blocks3), BF16)), stats=True, line=2, cost=70,
    )
    x_self, self_unit, self_inv, packed = first.held, first.unit, first.inv, first.packed
    g_ffn, tables = first.grads, first.tables

    texts = text_z.shape[0]
    text_z = with_layout_constraint(after(text_z, packed), Layout((0, 1)))
    text_pieces = [text_z, from_y(text_z), from_x(text_z), from_xy(text_z)]

    def masked_scores(q, keys):
        scores = mm_t(q, keys) * SCALE
        column = lax.broadcasted_iota(jnp.int32, scores.shape, 1)
        return jnp.where(column % tokens < own_tokens, scores, -1e30)

    def middle(refs, rows, step, total):
        vec = refs.vec
        branch = total + vec[0:1]
        refs.branch[rows] = branch
        joined = refs.states[rows] + branch * vec[1:2]
        refs.joined[rows] = joined
        normed, _ = layer_norm(joined)
        return (normed * vec[2:3] + vec[3:4]).astype(BF16)

    def product(refs, k, piece):
        pre = mm(piece[...], refs.w2[:, pl.ds(0, width)]) + refs.bias[0:1]
        refs.unit[k] = pre
        refs.stat[k, pl.ds(0, 1), pl.ds(0, tokens)] = to_row(jnp.sum(pre * pre, -1, keepdims=True))

    def body(links, refs):
        refs.stat[...] = jnp.zeros_like(refs.stat)
        packed = refs.packed
        for turn in (1, 2, 3, 0):
            to = (links.z + turn) % seqs
            for h in range(heads):
                keys = packed[:, :, head_at(h, width)].reshape(clip_rows, HD)
                values = packed[:, :, head_at(h, 2 * width)].reshape(clip_rows, HD)
                probs = softmax(masked_scores(packed[to, :, head_at(h)], keys))
                refs.outs[turn, :, head_at(h)] = mm(probs.astype(BF16), values).astype(BF16)
            links.send_line(
                refs.outs.at[turn], refs.mixed.at[links.clip_of(links.z)], to, turn
            )
        reduce_product = rows_partial("mixed", "w")

        def partial(refs, k, store):
            links.wait_line(refs.mixed.at[k], links.clip_of(k))
            reduce_product(refs, k, store)

        reduce_slice(links, refs, partial, middle, refs.held)
        gather_slice(links, refs, refs.held, product)
        sum_stats(links, refs)
        refs.inv[...] = lax.rsqrt(refs.stat_sum[...] / dim + EPS)

        @pl.loop(0, 4)
        def _(k):
            inverse = to_column(refs.inv[k, pl.ds(0, 1), pl.ds(0, tokens)])
            refs.unit[k] = refs.unit[k] * inverse

    second = run_kernel(
        "self_attend", 2,
        dict(
            packed=packed, w=full_out, states=states_p,
            vec=vectors(attn_bias[3], gate1, norm_gain, norm_bias),
            w2=full_cross, bias=jnp.broadcast_to(bias[4:5], (8, width)),
        ),
        dict(
            mixed=((4, tokens, width), BF16), branch=wide, joined=wide, held=held,
            unit=head_block, inv=((4, 8, 256), F32),
        ),
        body,
        dict(outs=((seqs, tokens, width), BF16), **reduce_scratch(tokens, dim)),
        stats=True, line=1,
        cost=80,
    )
    mixed, branch, after_self = second.mixed, second.branch, second.joined
    x_cross, cq_unit, cq_inv = second.held, second.unit, second.inv

    x_text = jnp.stack(after(text_pieces, cq_inv))
    text_proj = mm(x_text, full_cross[:, width:])
    ck_pre = text_proj[..., :width] + bias[5]
    cross_v = (text_proj[..., width:] + bias[6]).astype(BF16)
    ck_inv = rms_scale(sum4(jnp.sum(ck_pre * ck_pre, -1)))
    ck_unit = ck_pre * ck_inv
    cross_k = (ck_unit * gain[3]).astype(BF16)
    text_kv = jnp.concatenate([cross_k, cross_v], -1)

    def cross_heads(refs, k, h):
        q = (refs.unit[k, :, head_at(h)] * refs.gain[2:3, head_at(h)]).astype(BF16)
        keys = refs.kv[k, :, head_at(h)]
        values = refs.kv[k, :, head_at(h, width)]
        return q, keys, values, softmax(mm_t(q, keys) * SCALE)

    def middle(refs, rows, step, total):
        vec = refs.vec
        joined = refs.start[rows] + (total + vec[0:1])
        refs.joined[rows] = joined
        normed, _ = layer_norm(joined)
        return (normed * vec[1:2] + vec[2:3]).astype(BF16)

    root = math.sqrt(2.0 / math.pi)

    def product(refs, k, piece):
        for at, size in column_chunks(hidden_width, 640):
            columns = pl.ds(at, size)
            pre = mm(piece[...], refs.w2[:, columns]) + refs.bias[0:1, columns]
            bent = jnp.tanh(root * (pre + 0.044715 * pre * pre * pre))
            refs.hidden[k, :, columns] = (0.5 * pre * (1.0 + bent)).astype(BF16)
            refs.slope[k, :, columns] = 0.5 * (1.0 + bent) + 0.5 * pre * (
                1.0 - bent * bent
            ) * root * (1.0 + 3.0 * 0.044715 * pre * pre)

    def body(links, refs):
        reduce_product = rows_partial("mix", "w")

        def partial(refs, k, store):
            for h in range(heads):
                _, _, values, probs = cross_heads(refs, k, h)
                refs.mix[k, :, head_at(h)] = mm(probs.astype(BF16), values).astype(BF16)
            reduce_product(refs, k, store)

        reduce_slice(links, refs, partial, middle, refs.held)
        gather_slice(links, refs, refs.held, product)

    third = run_kernel(
        "cross_attend", 3,
        dict(
            unit=cq_unit, gain=gains8, kv=text_kv,
            w=full_crossout, start=after_self,
            vec=vectors(attn_bias[7], 1.0 + scale2, shift2),
            w2=full_up,
            bias=jnp.broadcast_to(pick(up_bias)[None], (8, hidden_width)),
        ),
        dict(
            mix=((4, tokens, width), BF16), joined=wide, held=held,
            hidden=((4, tokens, hidden_width), BF16),
            slope=((4, tokens, hidden_width), F32),
        ),
        body, reduce_scratch(tokens, dim),
        cost=60,
    )
    cross_mix, after_cross, x_ffn, hidden = third.mix, third.joined, third.held, third.hidden

    down_core = row_core(outer(hidden, g_ffn))
    down_part = scatter_z(down_core)
    inner_partial = turned_partial("d_hpre", "w_up")

    def ffn_partial(refs, k, store):
        w = refs.w_down
        deep = w.shape[2]
        for at, size in column_chunks(hidden_width, 640):
            columns = pl.ds(at, size)
            grad = mm_t(refs.g[k, :, pl.ds(0, deep)], w[0, columns])
            grad = grad + mm_t(refs.g[k, :, pl.ds(deep, deep)], w[1, columns])
            refs.d_hpre[k, :, columns] = (grad * refs.slope[k, :, columns]).astype(BF16)
        inner_partial(refs, k, store)

    def middle(refs, rows, step, total):
        normed, inverse = layer_norm(refs.joined[rows])
        d_cross = refs.top[rows] + norm_backward(normed, inverse, total * refs.vec[0:1])
        refs.d_cross[rows] = d_cross
        low = d_cross.astype(BF16)
        add_rows(refs.sums, 0, total, step)
        add_rows(refs.sums, 1, total * normed, step)
        add_rows(refs.sums, 2, low.astype(F32), step)
        return low

    def product(refs, k, piece):
        refs.d_mix[k] = rows_turned(piece, refs.w2).astype(BF16)

    def body(links, refs):
        reduce_slice(links, refs, ffn_partial, middle, refs.held)
        gather_slice(links, refs, refs.held, product)

    fourth = run_kernel(
        "ffn_back", 4,
        dict(
            g=after(g_ffn, down_core), w_down=full_down, slope=third.slope, w_up=full_up,
            joined=after_cross, top=out_grad_p, vec=vectors(1.0 + scale2),
            w2=full_crossout,
        ),
        dict(
            d_hpre=((4, tokens, hidden_width), BF16), d_cross=wide, held=held,
            d_mix=((4, tokens, width), BF16), sums=((3, 8, dim), F32),
        ),
        body, reduce_scratch(tokens, dim),
        cost=72,
    )
    d_hpre, d_cross, g_cross, d_cmix = fourth.d_hpre, fourth.d_cross, fourth.held, fourth.d_mix
    sums4 = jnp.sum(fourth.sums, 1)
    up_core = column_core(outer(x_ffn, d_hpre))
    up_part = scatter_z(up_core)

    def rms_back(grad, unit, inverse, mean):
        return inverse * (grad - unit * mean)

    def middle(refs, rows, step, total):
        normed, inverse = layer_norm(refs.joined[rows])
        vec = refs.vec
        d_self = refs.top[rows] + norm_backward(normed, inverse, total * vec[0:1])
        refs.d_self[rows] = d_self
        low = (d_self * vec[1:2]).astype(BF16)
        add_rows(refs.sums, 0, total * normed, step)
        add_rows(refs.sums, 1, total, step)
        add_rows(refs.sums, 2, low.astype(F32), step)
        add_rows(refs.sums, 3, d_self * refs.branch[rows], step)
        return low

    def body(links, refs):
        refs.stat[...] = jnp.zeros_like(refs.stat)
        refs.gains[...] = jnp.zeros_like(refs.gains)

        @pl.loop(0, 4)
        def _(k):
            square = jnp.zeros((tokens, 1), F32)
            for h in range(heads):
                q, keys, values, probs = cross_heads(refs, k, h)
                d_mix = refs.d_mix[k, :, head_at(h)]
                d_probs = mm_t(d_mix, values)
                delta = jnp.sum(probs * d_probs, -1, keepdims=True)
                d_scores = (probs * (d_probs - delta)).astype(BF16)
                d_q = mm(d_scores, keys) * SCALE
                refs.d_kv[k, :, head_at(h)] = (mm_l(d_scores, q) * SCALE).astype(BF16)
                refs.d_kv[k, :, head_at(h, width)] = mm_l(probs.astype(BF16), d_mix).astype(BF16)
                unit = refs.unit[k, :, head_at(h)]
                refs.gains[:, head_at(h)] += fold_rows(d_q * unit)
                d_q = d_q * refs.gain[2:3, head_at(h)]
                refs.d_unit[k, :, head_at(h)] = d_q
                square = square + jnp.sum(d_q * unit, -1, keepdims=True)
            refs.stat[k, pl.ds(0, 1), pl.ds(0, tokens)] = to_row(square)

        sum_stats(links, refs)

        @pl.loop(0, 4)
        def _(k):
            inverse = to_column(refs.inv[k, pl.ds(0, 1), pl.ds(0, tokens)])
            mean = to_column(refs.stat_sum[k, pl.ds(0, 1), pl.ds(0, tokens)]) / dim
            refs.d_pre[k] = rms_back(refs.d_unit[k], refs.unit[k], inverse, mean).astype(BF16)

        def product(refs, k, piece):
            refs.outs[k] = rows_turned(piece, refs.w2).astype(BF16)
            links.send_line(
                refs.outs.at[k], refs.d_heads.at[links.z], links.clip_of(k), k
            )

        reduce_slice(links, refs, turned_partial("d_pre", "w"), middle, refs.held)
        gather_slice(links, refs, refs.held, product)
        for source in range(seqs):
            links.wait_line(refs.d_heads.at[source], source)

    fifth = run_kernel(
        "cross_back", 5,
        dict(
            unit=cq_unit, inv=cq_inv, gain=gains8, kv=text_kv,
            d_mix=after(d_cmix, up_core, down_part),
            w=full_cross, joined=after_self, top=d_cross, branch=branch,
            vec=vectors(norm_gain, gate1), w2=full_out,
        ),
        dict(
            d_pre=((4, tokens, width), BF16), d_kv=((4, texts, 2 * width), BF16),
            gains=((8, width), F32), d_self=wide, held=held,
            d_heads=((seqs, tokens, width), BF16), sums=((4, 8, dim), F32),
        ),
        body,
        dict(
            d_unit=((4, tokens, width), F32), outs=((4, tokens, width), BF16),
            **reduce_scratch(tokens, dim),
        ),
        stats=True, line=1,
        cost=80,
    )
    d_cq, d_self, g_self, d_heads = fifth.d_pre, fifth.d_self, fifth.held, fifth.d_heads
    cq_gain = jnp.sum(fifth.gains, 0)
    sums5 = jnp.sum(fifth.sums, 1)
    d_ckv = after(fifth.d_kv, up_part).reshape(4, seqs, -1, 2 * width).transpose(1, 0, 2, 3)
    d_ckv = lax.psum_scatter(d_ckv, "z", scatter_dimension=0, tiled=True)[0]
    outproj_core = row_core(outer(mixed, g_self))
    crossout_core = row_core(outer(after(cross_mix, d_self), g_cross))

    d_ckn = d_ckv[..., :width].astype(F32)
    d_cv = d_ckv[..., width:]
    zpos = lax.axis_index("z")
    own = texts // seqs
    ck_unit = lax.dynamic_slice_in_dim(ck_unit, zpos * own, own, 1)
    ck_inv = lax.dynamic_slice_in_dim(ck_inv, zpos * own, own, 1)
    x_text = lax.dynamic_slice_in_dim(x_text, zpos * own, own, 1)
    d_cku = d_ckn * gain[3]
    ck_stat = sum4(jnp.sum(d_cku * ck_unit, -1)) / dim
    d_ck = rms_back(d_cku, ck_unit, ck_inv, ck_stat[..., None]).astype(BF16)
    ck_gain = jnp.sum(d_ckn * ck_unit, (0, 1))
    d_text = jnp.concatenate([d_ck, d_cv], -1)
    text_grad = reduce4(lambda k: mm_t(d_text[k], full_cross[:, width:]))
    cross_core = column_core(jnp.concatenate([outer(x_cross, d_cq), outer(x_text, d_text)], 1))
    cross_part = scatter_z(cross_core)
    outproj_part = scatter_z(after(outproj_core, cross_core))
    crossout_part = scatter_z(after(crossout_core, cross_core))

    def middle(refs, rows, step, total):
        normed, inverse = layer_norm(refs.states[rows])
        refs.out[rows] = refs.top[rows] + norm_backward(
            normed, inverse, total * refs.vec[0:1]
        )
        add_rows(refs.sums, 0, total, step)
        add_rows(refs.sums, 1, total * normed, step)

    def body(links, refs):
        refs.stat[...] = jnp.zeros_like(refs.stat)
        refs.gains[...] = jnp.zeros_like(refs.gains)
        packed, d_heads = refs.packed, refs.d_heads
        for h in range(heads):
            refs.d_keys[...] = jnp.zeros_like(refs.d_keys)
            refs.d_values[...] = jnp.zeros_like(refs.d_values)

            @pl.loop(0, seqs)
            def _(i):
                keys = packed[:, :, head_at(h, width)].reshape(clip_rows, HD)
                values = packed[:, :, head_at(h, 2 * width)].reshape(clip_rows, HD)
                q = packed[i, :, head_at(h)]
                d_mix = d_heads[i, :, head_at(h)]
                probs = softmax(masked_scores(q, keys))
                d_probs = mm_t(d_mix, values)
                delta = jnp.sum(probs * d_probs, -1, keepdims=True)
                d_scores = (probs * (d_probs - delta)).astype(BF16)
                refs.outs[h, i, :, pl.ds(0, HD)] = (mm(d_scores, keys) * SCALE).astype(BF16)
                refs.d_keys[...] += mm_l(d_scores, q)
                refs.d_values[...] += mm_l(probs.astype(BF16), d_mix)

            for i in range(seqs):
                rows = pl.ds(i * tokens, tokens)
                refs.outs[h, i, :, pl.ds(HD, HD)] = (refs.d_keys[rows] * SCALE).astype(BF16)
                refs.outs[h, i, :, pl.ds(2 * HD, HD)] = refs.d_values[rows].astype(BF16)
            for step in range(seqs):
                to = (links.z + 1 + step) % seqs
                links.send_line(
                    refs.outs.at[h, to],
                    refs.arrived.at[h, links.clip_of(links.z)],
                    to, step, h,
                )
        for k in range(4):
            for h in range(heads):
                links.wait_line(refs.arrived.at[h, k], links.clip_of(k), h)

        @pl.loop(0, 4)
        def _(k):
            for part in range(2):
                square = jnp.zeros((tokens, 1), F32)
                for h in range(heads):
                    at = head_at(h, part * width)
                    grad = refs.arrived[h, k, :, pl.ds(part * HD, HD)].astype(F32)
                    grad = grad * refs.tables[k, :, pl.ds(0, HD)] - swap_pairs(grad) * refs.tables[k, :, pl.ds(HD, HD)]
                    unit = refs.unit[k, :, at]
                    refs.gains[part, :, head_at(h)] += fold_rows(grad * unit)
                    grad = grad * refs.gain[pl.ds(part, 1), head_at(h)]
                    refs.d_unit[k, :, at] = grad
                    square = square + jnp.sum(grad * unit, -1, keepdims=True)
                refs.stat[k, pl.ds(part, 1), pl.ds(0, tokens)] = to_row(square)
            for h in range(heads):
                refs.d_qkv[k, :, head_at(h, 2 * width)] = refs.arrived[
                    h, k, :, pl.ds(2 * HD, HD)
                ]

        sum_stats(links, refs)

        @pl.loop(0, 4)
        def _(k):
            for part in range(2):
                row = (k, pl.ds(part, 1), pl.ds(0, tokens))
                inverse = to_column(refs.inv[row])
                mean = to_column(refs.stat_sum[row]) / dim
                at = pl.ds(part * width, width)
                refs.d_qkv[k, :, at] = rms_back(
                    refs.d_unit[k, :, at], refs.unit[k, :, at], inverse, mean
                ).astype(BF16)

        reduce_slice(links, refs, turned_partial("d_qkv", "w"), middle)

    sixth = run_kernel(
        "self_back", 6,
        dict(
            packed=packed, d_heads=d_heads, unit=self_unit, inv=self_inv,
            gain=gains8, tables=tables, w=full_qkv, states=states_p,
            top=after(d_self, crossout_core, outproj_core, cross_core), vec=vectors(1.0 + scale1),
        ),
        dict(
            d_qkv=((4, tokens, blocks3), BF16), gains=((2, 8, width), F32),
            out=wide, sums=((2, 8, dim), F32),
        ),
        body,
        dict(
            outs=((heads, seqs, tokens, 3 * HD), BF16),
            arrived=((heads, 4, tokens, 3 * HD), BF16),
            d_keys=((clip_rows, HD), F32), d_values=((clip_rows, HD), F32),
            d_unit=((4, tokens, 2 * width), F32),
            **reduce_scratch(tokens, dim),
        ),
        stats=True, line=heads,
        cost=120,
    )
    d_qkv = sixth.d_qkv
    d_qkv_sum = jnp.sum(d_qkv.astype(F32), (0, 1))
    q_gain, k_gain = jnp.sum(sixth.gains, 1)
    states_grad = sixth.out[:own_tokens]
    sums6 = jnp.sum(sixth.sums, 1)
    qkv_core = column_core(outer(x_self, d_qkv))
    qkv_part = scatter_z(qkv_core)

    ffn_out = reduce4(lambda k: rows_mm(hidden[k], full_down)) + down_bias
    block_out = (after_cross + ffn_out * gate2)[:own_tokens]
    up_grad = column_done(up_part, 1)[:, 0]
    down_grad = row_done(down_part)
    qkv_grad = column_done(qkv_part, 3)
    outproj_grad = row_done(outproj_part)
    cross_grad = column_done(cross_part, 3)
    crossout_grad = row_done(crossout_part)

    def column_sum(v):
        return jnp.sum(v.astype(F32), tuple(range(v.ndim - 1)))

    def over_z(v):
        v = v + lax.ppermute(v, "z", [(i, i ^ 1) for i in range(seqs)])
        return v + lax.ppermute(v, "z", [(i, i ^ 2) for i in range(seqs)])

    def over_clips(v):
        v = v + from_core(v)
        v = v + from_x(v)
        v = v + from_y(v)
        return over_reps(v)

    early = jnp.stack(
        [
            sums4[0],
            sums4[1],
            column_sum(out_grad_p * ffn_out),
            spread(column_sum(d_cq)),
            spread(column_sum(d_ck)),
            spread(column_sum(d_cv)),
            sums4[2],
            spread(cq_gain),
            spread(ck_gain),
            sums5[0],
            sums5[1],
            column_sum(d_ffnout),
            sums5[2],
            sums5[3],
        ]
    )
    upbias = over_clips(over_z(spread(column_sum(d_hpre))))
    early_clip = over_z(early)
    early_all = over_clips(early_clip)
    late = jnp.stack(
        [
            sums6[0],
            sums6[1],
            spread(d_qkv_sum[:width]),
            spread(d_qkv_sum[width : 2 * width]),
            spread(d_qkv_sum[2 * width :]),
            spread(q_gain),
            spread(k_gain),
        ]
    )
    late_clip = over_z(late)
    late_all = over_clips(late_clip)

    def mod_rows(e, l):
        return jnp.stack([l[0], l[1], e[13], e[0], e[1], e[2]])

    time_grad = mod_rows(early_clip, late_clip)[None]
    mod_grad = mod_rows(early_all, late_all)
    bias_grad = jnp.stack(
        [late_all[2], late_all[3], late_all[4], early_all[12]] + [early_all[i] for i in (3, 4, 5, 6)]
    )
    gain_grad = jnp.stack([late_all[5], late_all[6], early_all[7], early_all[8]])
    return (
        block_out, states_grad, text_grad, time_grad, qkv_grad, outproj_grad, cross_grad,
        crossout_grad, up_grad, down_grad, bias_grad, gain_grad, early_all[9], early_all[10],
        upbias, early_all[11], mod_grad,
    )


def solution(mesh):
    reps, shards, seqs = mesh.shape["replica"], mesh.shape["shard"], mesh.shape["seq"]
    fine = Mesh(
        mesh.devices.reshape(reps // 2, 2, shards // 2, 2, seqs), ("rep", "x", "y", "core", "z")
    )
    tokens = P(("rep", "x", "y", "core", "z"), None)
    clips = P(("rep", "x", "y", "core"), None, None)
    rows2 = P(("y", "core", "z"), None)
    rows3 = P(("y", "core", "z"), None, None)
    return jax.shard_map(
        on_device,
        mesh=fine,
        in_specs=(
            tokens, tokens, P(None, ("rep", "x", "y", "core", "z")), clips,
            rows3, rows2, rows3, rows2, rows2, rows2,
            P(), P(), P(), P(), P(), P(), P(), tokens,
        ),
        out_specs=(
            tokens, tokens, tokens, clips,
            rows3, rows2, rows3, rows2, rows2, rows2,
            P(), P(), P(), P(), P(), P(), P(),
        ),
        check_vma=False,
    )
```

```python
import math
from types import SimpleNamespace

import jax
import jax.numpy as jnp
import numpy as np
from jax import lax
from jax.experimental import pallas as pl
from jax.experimental.pallas import tpu as pltpu
from jax.sharding import Mesh, PartitionSpec as P

HD = 128
EPS = 1e-06
F32 = jnp.float32
BF16 = jnp.bfloat16
SCALE = 1.0 / math.sqrt(HD)
SWAP = [(0, 1), (1, 0)]
ROWS = 16
FLOPS = 1_150_000_000
BYTES = 3_600_000


def rope_tables(grid_pos):
    pairs = HD // 2
    width = pairs // 3
    first = pairs - 2 * width
    index = np.arange(pairs)
    part = np.where(index < first, 0, np.where(index < first + width, 1, 2))
    offset = np.where(part == 0, index, np.where(part == 1, index - first, index - first - width))
    frequency = 10000.0 ** (-offset / np.where(part == 0, first, width))
    position = grid_pos.astype(F32)
    angles = 0.0
    for axis in range(3):
        lane = np.repeat(frequency * (part == axis), 2)
        angles = angles + position[axis][:, None] * jnp.asarray(lane, F32)[None, :]
    sign = np.where(np.arange(HD) % 2 == 0, -1.0, 1.0)
    return jnp.cos(angles), jnp.sin(angles) * jnp.asarray(sign, F32)[None, :]


def layer_norm(values):
    center = values - jnp.mean(values, -1, keepdims=True)
    inverse = lax.rsqrt(jnp.mean(center * center, -1, keepdims=True) + EPS)
    return center * inverse, inverse


def norm_backward(normed, inverse, grad_in):
    return inverse * (
        grad_in
        - jnp.mean(grad_in, -1, keepdims=True)
        - normed * jnp.mean(grad_in * normed, -1, keepdims=True)
    )


def mm(a, b):
    return lax.dot_general(a, b, (((a.ndim - 1,), (0,)), ((), ())), preferred_element_type=F32)


def mm_t(a, b):
    return lax.dot_general(a, b, (((a.ndim - 1,), (1,)), ((), ())), preferred_element_type=F32)


def rows_mm(a, w):
    return jnp.concatenate([mm(a, w[0]), mm(a, w[1])], -1)


def after(value, *done):
    return lax.optimization_barrier((value, done))[0]


def outer(a, b):
    lead = tuple(range(a.ndim - 1))
    return lax.dot_general(a, b, ((lead, lead), ((), ())), preferred_element_type=F32)


def column_chunks(total, size):
    return [(at, min(size, total - at)) for at in range(0, total, size)]


class Links:
    def __init__(self, named, stats, line):
        self.named = named
        self.used = 0
        self.started = []
        self.x, self.y, self.z = [lax.axis_index(n) for n in ("x", "y", "z")]
        self.seqs = lax.axis_size("z")
        barrier = pltpu.get_barrier_semaphore()
        peers = [{"x": 1 - self.x}, {"y": 1 - self.y}]
        if stats:
            peers.append({"x": 1 - self.x, "y": 1 - self.y})
        if line:
            peers += [{"z": (self.z + step) % self.seqs} for step in range(1, self.seqs)]
        for peer in peers:
            pl.semaphore_signal(
                barrier, inc=1, device_id=peer, device_id_type=pl.DeviceIdType.MESH
            )
        pl.semaphore_wait(barrier, len(peers))

    def clip_of(self, piece):
        return ((piece // 2 + self.x) % 2) * 2 + (piece % 2 + self.y) % 2

    def send(self, axis, src, dst):
        where = {a: 1 - lax.axis_index(a) for a in axis}
        index = self.used
        self.used += 1
        sems = self.named.sems
        copy = pltpu.make_async_remote_copy(
            src_ref=src,
            dst_ref=dst,
            send_sem=sems.at[0, index],
            recv_sem=sems.at[1, index],
            device_id=where,
            device_id_type=pl.DeviceIdType.MESH,
        )
        copy.start()
        self.started.append((None, copy))
        return copy

    def send_line(self, src, dst, to, slot, lane=0):
        sems = self.named.line
        copy = pltpu.make_async_remote_copy(
            src_ref=src,
            dst_ref=dst,
            send_sem=sems.at[0, lane, slot],
            recv_sem=sems.at[1, lane, self.z],
            device_id={"z": to},
            device_id_type=pl.DeviceIdType.MESH,
        )

        @pl.when(to != self.z)
        def _():
            copy.start()

        @pl.when(to == self.z)
        def _():
            dst[...] = src[...]

        self.started.append((to != self.z, copy))

    def wait_line(self, ref, source, lane=0):
        sems = self.named.line
        copy = pltpu.make_async_remote_copy(
            src_ref=ref,
            dst_ref=ref,
            send_sem=sems.at[0, lane, 0],
            recv_sem=sems.at[1, lane, source],
            device_id={"z": (self.z + 1) % self.seqs},
            device_id_type=pl.DeviceIdType.MESH,
        )

        @pl.when(source != self.z)
        def _():
            copy.wait_recv()

    def finish(self):
        for needed, copy in self.started:
            if needed is None:
                copy.wait_send()
            else:
                pl.when(needed)(copy.wait_send)


def split_rows(tokens):
    return ((tokens // 2 + ROWS - 1) // ROWS) * ROWS


def row_steps(tokens, body):
    @pl.loop(0, tokens // ROWS)
    def _(step):
        body(pl.ds(pl.multiple_of(step * ROWS, ROWS), ROWS), step)


def reduce_slice(links, refs, partial, middle, keep=None):
    mine, near, far, total = refs.mine, refs.near, refs.far, refs.total
    tokens = total.shape[0]
    half = split_rows(tokens)
    top, low = pl.ds(0, half), pl.ds(half, tokens - half)

    def store_low(slot):
        def store(columns, value):
            mine[slot, :, columns] = value.astype(BF16)

        return store

    def store_full(columns, value):
        total[:, columns] = value

    partial(refs, 3, store_low(2))
    far_x = links.send("x", mine.at[2, top], far.at[top])
    far_y = links.send("y", mine.at[2, low], far.at[low])
    partial(refs, 2, store_low(1))
    x_top = links.send("x", mine.at[1, top], near.at[1, top])
    partial(refs, 1, store_low(0))
    y_low = links.send("y", mine.at[0, low], near.at[0, low])
    far_x.wait_recv()
    mine[0, top] = (mine[0, top].astype(F32) + far[top].astype(F32)).astype(BF16)
    y_top = links.send("y", mine.at[0, top], near.at[0, top])
    far_y.wait_recv()
    mine[1, low] = (mine[1, low].astype(F32) + far[low].astype(F32)).astype(BF16)
    x_low = links.send("x", mine.at[1, low], near.at[1, low])
    partial(refs, 0, store_full)
    for copy in (x_top, y_low, y_top, x_low):
        copy.wait_recv()

    def body(rows, step):
        value = total[rows] + near[0, rows].astype(F32) + near[1, rows].astype(F32)
        sent = middle(refs, rows, step, value)
        if keep is not None:
            keep[0, rows] = sent

    row_steps(tokens, body)


def gather_begin(links, held):
    return links.send("x", held.at[0], held.at[2]), links.send("y", held.at[0], held.at[1])


def gather_relay(links, held, first):
    tokens = held.shape[1]
    half = split_rows(tokens)
    top, low = pl.ds(0, half), pl.ds(half, tokens - half)
    from_x, from_y = first
    from_x.wait_recv()
    far_top = links.send("y", held.at[2, top], held.at[3, top])
    from_y.wait_recv()
    far_low = links.send("x", held.at[1, low], held.at[3, low])
    return far_top, far_low


def gather_end(far):
    for copy in far:
        copy.wait_recv()


def gather_slice(links, refs, held, product, also=()):
    arrays = (held,) + tuple(also)
    first = [gather_begin(links, array) for array in arrays]
    product(refs, 0, held.at[0])
    far = [gather_relay(links, array, copies) for array, copies in zip(arrays, first)]
    product(refs, 1, held.at[1])
    product(refs, 2, held.at[2])
    for copies in far:
        gather_end(copies)
    product(refs, 3, held.at[3])


def sum_stats(links, refs):
    stat, other = refs.stat, refs.stats_in
    copies = [
        links.send("y", stat, other.at[0]),
        links.send("x", stat, other.at[1]),
        links.send("xy", stat, other.at[2]),
    ]
    for copy in copies:
        copy.wait_recv()
    for copy in copies:
        copy.wait_send()
    del links.started[-3:]
    for k in range(4):
        refs.stat_sum[k] = (
            stat[k] + other[0, k ^ 1] + other[1, k ^ 2] + other[2, k ^ 3]
        )


def to_row(column):
    size = column.shape[0]
    same = lax.broadcasted_iota(jnp.int32, (size, size), 0) == lax.broadcasted_iota(
        jnp.int32, (size, size), 1
    )
    return jnp.sum(jnp.where(same, column, 0.0), 0, keepdims=True)


def to_column(row):
    size = row.shape[1]
    same = lax.broadcasted_iota(jnp.int32, (size, size), 0) == lax.broadcasted_iota(
        jnp.int32, (size, size), 1
    )
    return jnp.sum(jnp.where(same, row, 0.0), 1, keepdims=True)


def run_kernel(name, cid, inputs, outputs, body, scratch, cost, stats=False, line=0):
    names_in, names_out = list(inputs), list(outputs)
    spaces = dict(sems=pltpu.SemaphoreType.DMA((2, 24)))
    if line:
        spaces.update(line=pltpu.SemaphoreType.DMA((2, line, 4)))
    if stats:
        spaces.update(
            stat=pltpu.VMEM((4, 8, 256), F32),
            stat_sum=pltpu.VMEM((4, 8, 256), F32),
            stats_in=pltpu.VMEM((3, 4, 8, 256), F32),
        )
    for key, (shape, dtype) in scratch.items():
        spaces[key] = pltpu.VMEM(shape, dtype)

    def kernel(*refs):
        named = SimpleNamespace(**dict(zip(names_in + names_out + list(spaces), refs)))
        links = Links(named, stats, line)
        body(links, named)
        links.finish()

    vmem = pl.BlockSpec(memory_space=pltpu.VMEM)
    result = pl.pallas_call(
        kernel,
        name=name,
        out_shape=[jax.ShapeDtypeStruct(*outputs[n]) for n in names_out],
        in_specs=[vmem] * len(names_in),
        out_specs=[vmem] * len(names_out),
        scratch_shapes=list(spaces.values()),
        cost_estimate=pl.CostEstimate(
            flops=cost * FLOPS, bytes_accessed=cost * BYTES, transcendentals=0
        ),
        compiler_params=pltpu.CompilerParams(
            collective_id=cid, has_side_effects=True, vmem_limit_bytes=60 * 1024 * 1024
        ),
    )(*[inputs[n] for n in names_in])
    return SimpleNamespace(**dict(zip(names_out, result)))


def reduce_scratch(tokens, dim):
    return dict(
        mine=((3, tokens, dim), BF16),
        near=((2, tokens, dim), BF16),
        far=((tokens, dim), BF16),
        total=((tokens, dim), F32),
    )


def add_rows(ref, index, value, step):
    @pl.when(step == 0)
    def _():
        ref[index] = jnp.zeros_like(ref[index])

    ref[index] += value[:8] + value[8:]


def fold_rows(value):
    return jnp.sum(value.reshape(value.shape[0] // 8, 8, value.shape[1]), 0)


def rows_partial(a, w):
    def partial(refs, k, store):
        piece = getattr(refs, a)[k]
        blocks = getattr(refs, w)
        deep, width = piece.shape[1], blocks.shape[2]
        for half in range(2):
            for part in range(2):
                store(
                    pl.ds((half * 2 + part) * width, width),
                    mm(piece, blocks[part, pl.ds(half * deep, deep), :]),
                )

    return partial


def turned_partial(a, w, size=256):
    def partial(refs, k, store):
        deep = getattr(refs, a).shape[2]

        @pl.loop(0, getattr(refs, w).shape[0] // size)
        def _(step):
            rows = pl.ds(pl.multiple_of(step * size, size), size)
            store(rows, mm_t(getattr(refs, a)[k], getattr(refs, w)[rows, pl.ds(0, deep)]))

    return partial


def rows_turned(piece, w):
    deep, width = w.shape[1] // 2, w.shape[2]
    total = 0.0
    for half in range(2):
        for part in range(2):
            columns = pl.ds((half * 2 + part) * width, width)
            total = total + mm_t(piece[:, columns], w[part, pl.ds(half * deep, deep), :])
    return total


def mm_l(a, b):
    return lax.dot_general(a, b, (((0,), (0,)), ((), ())), preferred_element_type=F32)


def swap_pairs(values):
    even = lax.broadcasted_iota(jnp.int32, values.shape, 1) % 2 == 0
    return jnp.where(even, pltpu.roll(values, HD - 1, 1), pltpu.roll(values, 1, 1))


def softmax(scores):
    weight = jnp.exp(scores - jnp.max(scores, -1, keepdims=True))
    return weight * (1.0 / jnp.sum(weight, -1, keepdims=True))


def head_at(h, base=0):
    return pl.ds(base + h * HD, HD)


def on_device(
    states, text_emb, grid_pos, time_mod, w_qkv, w_out, w_cross, w_crossout, w_up, w_down,
    attn_bias, qk_gain, norm_gain, norm_bias, up_bias, down_bias, modulation, out_grad,
):
    x, y, core = lax.axis_index("x"), lax.axis_index("y"), lax.axis_index("core")
    seqs = lax.axis_size("z")
    reps = lax.axis_size("rep")
    own_tokens, dim = states.shape
    tokens = -(-own_tokens // ROWS) * ROWS
    block = y * 2 + x
    pad = ((0, tokens - own_tokens), (0, 0))
    states_p = jnp.pad(states, pad)
    out_grad_p = jnp.pad(out_grad, pad)

    def from_y(a):
        return lax.ppermute(a, "y", SWAP)

    def from_x(a):
        return lax.ppermute(a, "x", SWAP)

    def from_xy(a):
        return lax.ppermute(a, ("x", "y"), [(i, 3 - i) for i in range(4)])

    def from_core(a):
        return lax.ppermute(a, "core", SWAP)

    def gather4(a):
        far, xs, ys = from_xy(a), from_x(a), from_y(a)
        return jnp.stack([a, ys, xs, far])

    def reduce4(term):
        far = from_xy(term(3).astype(BF16))
        xs = from_x(term(2).astype(BF16))
        ys = from_y(term(1).astype(BF16))
        return term(0) + ys.astype(F32) + xs.astype(F32) + far.astype(F32)

    def sum4(stat):
        far, xs, ys = from_xy(stat), from_x(stat), from_y(stat)
        return (
            stat
            + jnp.stack([ys[1], ys[0], ys[3], ys[2]])
            + jnp.stack([xs[2], xs[3], xs[0], xs[1]])
            + jnp.stack([far[3], far[2], far[1], far[0]])
        )

    def pick(v, blocks=4):
        return lax.dynamic_index_in_dim(
            v.reshape(v.shape[:-1] + (blocks, v.shape[-1] // blocks)), block, v.ndim - 1, False
        )

    def spread(v):
        hot = (jnp.arange(4) == block).astype(F32)
        full = v[..., None, :] * hot[:, None]
        return full.reshape(v.shape[:-1] + (4 * v.shape[-1],))

    def column_own(w):
        rows, groups, width = w.shape[0], w.shape[1], w.shape[2] // 4
        mine = lax.dynamic_index_in_dim(w.reshape(rows, groups, 2, 2, width), x, 3, False)
        keep = lax.dynamic_index_in_dim(mine, y, 2, False).reshape(rows, groups * width)
        send = lax.dynamic_index_in_dim(mine, 1 - y, 2, False).reshape(rows, groups * width)
        recv = from_y(send)
        return jnp.where(y == 0, jnp.stack([keep, recv]), jnp.stack([recv, keep]))

    def column_block(w):
        full = lax.all_gather(column_own(w), ("core", "z"), axis=1, tiled=True)
        return full.reshape(-1, full.shape[2])

    def row_own(w):
        half = w.shape[1] // 2
        keep = lax.dynamic_slice_in_dim(w, core * half, half, 1)
        recv = from_core(lax.dynamic_slice_in_dim(w, (1 - core) * half, half, 1))
        return jnp.where(core == x, keep, recv)

    def row_block(w):
        full = lax.all_gather(row_own(w), ("core", "z"), axis=0, tiled=True)
        return full.reshape(2, -1, full.shape[1])

    def attention_blocks(w_cross, *row_weights):
        own = column_own(w_cross)
        width = own.shape[2] // 3
        blocks = [own[:, :, g * width : (g + 1) * width] for g in range(3)]
        for w in row_weights:
            mine = row_own(w)
            blocks.append(jnp.stack([mine[:, :width], mine[:, width:]]))
        return lax.all_gather(jnp.concatenate(blocks), ("core", "z"), axis=1, tiled=True)

    def over_reps(a):
        return lax.psum(a, "rep") if reps > 1 else a

    def column_core(g):
        g = g.astype(BF16).reshape(2, 2, seqs, -1, g.shape[1])
        keep = lax.dynamic_index_in_dim(g, core, 1, False)
        recv = from_core(lax.dynamic_index_in_dim(g, 1 - core, 1, False))
        both = (keep.astype(F32) + recv.astype(F32)).astype(BF16)
        return both.transpose(1, 0, 2, 3).reshape(-1, g.shape[4])

    def row_core(g):
        half = g.shape[1] // 2
        g = g.astype(BF16)
        keep = lax.dynamic_slice_in_dim(g, core * half, half, 1)
        recv = from_core(lax.dynamic_slice_in_dim(g, (1 - core) * half, half, 1))
        return (keep.astype(F32) + recv.astype(F32)).astype(BF16)

    def scatter_z(a):
        return over_reps(lax.psum_scatter(a, "z", scatter_dimension=0, tiled=True))

    def column_done(part, groups):
        width = part.shape[1] // groups
        part = part.reshape(2, -1, groups * width)
        keep = lax.dynamic_index_in_dim(part, y, 0, False)
        recv = from_y(lax.dynamic_index_in_dim(part, 1 - y, 0, False))
        ours = jnp.where(y == 0, jnp.stack([keep, recv]), jnp.stack([recv, keep]))
        theirs = from_x(ours)
        rows = ours.shape[1]
        ours = ours.reshape(2, rows, groups, width)
        theirs = theirs.reshape(2, rows, groups, width)
        full = jnp.where(x == 0, jnp.stack([ours, theirs], 1), jnp.stack([theirs, ours], 1))
        return full.transpose(2, 3, 0, 1, 4).reshape(rows, groups, 4 * width).astype(F32)

    def row_done(part):
        other = from_x(part)
        ours = jnp.where(core == x, part, other)
        theirs = from_core(jnp.where(core == x, other, part))
        full = jnp.where(
            core == 0,
            jnp.concatenate([ours, theirs], 1),
            jnp.concatenate([theirs, ours], 1),
        )
        return full.astype(F32)

    mods = modulation + time_mod[0]
    shift1, scale1, gate1, shift2, scale2, gate2 = [mods[i] for i in range(6)]

    def vectors(*rows):
        return jnp.stack(rows + (jnp.zeros_like(rows[0]),) * (8 - len(rows)))

    full_qkv = column_block(w_qkv)
    text_z = lax.all_gather(text_emb, "z", axis=0, tiled=True)
    attend_w = attention_blocks(w_cross, w_out, w_crossout)
    cross_wq, cross_wk, cross_wv = [
        attend_w[2 * g : 2 * g + 2].reshape(dim, -1) for g in range(3)
    ]
    full_out, full_crossout = attend_w[6:8], attend_w[8:10]
    full_up = column_block(w_up[:, None, :])
    full_down = row_block(w_down)
    bias = pick(attn_bias)
    gain = pick(qk_gain)
    width = bias.shape[1]
    heads = width // HD
    hidden_width = full_up.shape[1]
    own_tables = jnp.pad(jnp.concatenate(rope_tables(grid_pos), 1), pad)
    d_ffnout = (out_grad_p * gate2).astype(BF16)

    def rms_scale(v):
        return lax.rsqrt(v / dim + EPS)[..., None]

    wide = ((tokens, dim), F32)
    held = ((4, tokens, dim), BF16)
    head_block = ((4, tokens, width), F32)

    blocks3 = 3 * width
    clip_rows = seqs * tokens

    def middle(refs, rows):
        normed, _ = layer_norm(refs.states[rows])
        vec = refs.vec
        return (normed * vec[0:1] + vec[1:2]).astype(BF16)

    def body(links, refs):
        refs.stat[...] = jnp.zeros_like(refs.stat)

        def rows_in(rows, step):
            refs.held[0, rows] = middle(refs, rows)

        def send_heads(k, columns, lane):
            links.send_line(
                refs.sent.at[k, :, columns], refs.packed.at[links.z, :, columns],
                links.clip_of(k), k, lane,
            )

        early, late = pl.ds(2 * width, width), pl.ds(0, 2 * width)

        def product(refs, k, piece):
            pre = mm(piece[...], refs.w[:, early]) + refs.bias[0:1, early]
            refs.sent[k, :, early] = pre.astype(BF16)
            send_heads(k, early, 0)
            for part in range(2):
                columns = pl.ds(part * width, width)
                pre = mm(piece[...], refs.w[:, columns]) + refs.bias[0:1, columns]
                refs.unit[k, :, columns] = pre
                square = jnp.sum(pre * pre, -1, keepdims=True)
                refs.stat[k, pl.ds(part, 1), pl.ds(0, tokens)] = to_row(square)

        refs.tables[0] = refs.own_tables[...]
        refs.texts[0] = refs.text[...]
        row_steps(tokens, rows_in)
        gather_slice(links, refs, refs.held, product, (refs.tables,))
        sum_stats(links, refs)
        refs.inv[...] = lax.rsqrt(refs.stat_sum[...] / dim + EPS)
        first = gather_begin(links, refs.texts)
        for k in (3, 2, 1, 0):
            cosine, sine = refs.tables[k, :, pl.ds(0, HD)], refs.tables[k, :, pl.ds(HD, HD)]
            for part in range(2):
                inverse = to_column(refs.inv[k, pl.ds(part, 1), pl.ds(0, tokens)])
                for h in range(heads):
                    at = head_at(h, part * width)
                    unit = refs.unit[k, :, at] * inverse
                    refs.unit[k, :, at] = unit
                    scaled = unit * refs.gain[pl.ds(part, 1), head_at(h)]
                    turned = scaled * cosine + swap_pairs(scaled) * sine
                    refs.sent[k, :, at] = turned.astype(BF16)
            send_heads(k, late, 1)
        gather_end(gather_relay(links, refs.texts, first))
        for source in range(seqs):
            links.wait_line(refs.packed.at[source, :, early], source, 0)
            links.wait_line(refs.packed.at[source, :, late], source, 1)

    gains8 = jnp.pad(gain, ((0, 4), (0, 0)))
    texts = text_z.shape[0]
    first = run_kernel(
        "self_in", 1,
        dict(
            states=states_p, vec=vectors(1.0 + scale1, shift1), w=full_qkv,
            bias=jnp.broadcast_to(bias[:3].reshape(1, -1), (8, blocks3)),
            gain=gains8, own_tables=own_tables, text=text_z,
        ),
        dict(
            held=held, unit=((4, tokens, 2 * width), F32), inv=((4, 8, 256), F32),
            packed=((seqs, tokens, blocks3), BF16), texts=((4, texts, dim), BF16),
            tables=((4, tokens, 2 * HD), F32),
        ),
        body, dict(sent=((4, tokens, blocks3), BF16)), stats=True, line=2, cost=70,
    )
    x_self, self_unit, self_inv, packed = first.held, first.unit, first.inv, first.packed
    x_text, tables = first.texts, first.tables

    def masked_scores(q, keys):
        scores = mm_t(q, keys) * SCALE
        column = lax.broadcasted_iota(jnp.int32, scores.shape, 1)
        return jnp.where(column % tokens < own_tokens, scores, -1e30)

    def middle(refs, rows, step, total):
        vec = refs.vec
        branch = total + vec[0:1]
        refs.branch[rows] = branch
        joined = refs.states[rows] + branch * vec[1:2]
        refs.joined[rows] = joined
        normed, _ = layer_norm(joined)
        return (normed * vec[2:3] + vec[3:4]).astype(BF16)

    def product(refs, k, piece):
        pre = mm(piece[...], refs.w2[:, pl.ds(0, width)]) + refs.bias[0:1]
        refs.unit[k] = pre
        refs.stat[k, pl.ds(0, 1), pl.ds(0, tokens)] = to_row(jnp.sum(pre * pre, -1, keepdims=True))

    def body(links, refs):
        refs.stat[...] = jnp.zeros_like(refs.stat)
        packed = refs.packed
        refs.grads[0] = refs.own_grads[...]
        first = gather_begin(links, refs.grads)
        for turn in (1, 2, 3, 0):
            to = (links.z + turn) % seqs
            for h in range(heads):
                keys = packed[:, :, head_at(h, width)].reshape(clip_rows, HD)
                values = packed[:, :, head_at(h, 2 * width)].reshape(clip_rows, HD)
                probs = softmax(masked_scores(packed[to, :, head_at(h)], keys))
                refs.outs[turn, :, head_at(h)] = mm(probs.astype(BF16), values).astype(BF16)
            links.send_line(
                refs.outs.at[turn], refs.mixed.at[links.clip_of(links.z)], to, turn
            )
        far = gather_relay(links, refs.grads, first)
        reduce_product = rows_partial("mixed", "w")

        def partial(refs, k, store):
            links.wait_line(refs.mixed.at[k], links.clip_of(k))
            reduce_product(refs, k, store)

        reduce_slice(links, refs, partial, middle, refs.held)
        gather_slice(links, refs, refs.held, product)
        gather_end(far)
        sum_stats(links, refs)
        refs.inv[...] = lax.rsqrt(refs.stat_sum[...] / dim + EPS)

        @pl.loop(0, 4)
        def _(k):
            inverse = to_column(refs.inv[k, pl.ds(0, 1), pl.ds(0, tokens)])
            refs.unit[k] = refs.unit[k] * inverse

    second = run_kernel(
        "self_attend", 2,
        dict(
            packed=packed, w=full_out, states=states_p,
            vec=vectors(attn_bias[3], gate1, norm_gain, norm_bias),
            w2=cross_wq, bias=jnp.broadcast_to(bias[4:5], (8, width)),
            own_grads=d_ffnout,
        ),
        dict(
            mixed=((4, tokens, width), BF16), branch=wide, joined=wide, held=held, grads=held,
            unit=head_block, inv=((4, 8, 256), F32),
        ),
        body,
        dict(outs=((seqs, tokens, width), BF16), **reduce_scratch(tokens, dim)),
        stats=True, line=1,
        cost=80,
    )
    mixed, branch, after_self, g_ffn = second.mixed, second.branch, second.joined, second.grads
    x_cross, cq_unit, cq_inv = second.held, second.unit, second.inv

    ck_pre = mm(x_text, cross_wk) + bias[5]
    cross_v = (mm(x_text, cross_wv) + bias[6]).astype(BF16)
    ck_inv = rms_scale(sum4(jnp.sum(ck_pre * ck_pre, -1)))
    ck_unit = ck_pre * ck_inv
    cross_k = (ck_unit * gain[3]).astype(BF16)
    text_kv = jnp.concatenate([cross_k, cross_v], -1)

    def cross_heads(refs, k, h):
        q = (refs.unit[k, :, head_at(h)] * refs.gain[2:3, head_at(h)]).astype(BF16)
        keys = refs.kv[k, :, head_at(h)]
        values = refs.kv[k, :, head_at(h, width)]
        return q, keys, values, softmax(mm_t(q, keys) * SCALE)

    def middle(refs, rows, step, total):
        vec = refs.vec
        joined = refs.start[rows] + (total + vec[0:1])
        refs.joined[rows] = joined
        normed, _ = layer_norm(joined)
        return (normed * vec[1:2] + vec[2:3]).astype(BF16)

    root = math.sqrt(2.0 / math.pi)

    def product(refs, k, piece):
        for at, size in column_chunks(hidden_width, 640):
            columns = pl.ds(at, size)
            pre = mm(piece[...], refs.w2[:, columns]) + refs.bias[0:1, columns]
            bent = jnp.tanh(root * (pre + 0.044715 * pre * pre * pre))
            refs.hidden[k, :, columns] = (0.5 * pre * (1.0 + bent)).astype(BF16)
            refs.slope[k, :, columns] = 0.5 * (1.0 + bent) + 0.5 * pre * (
                1.0 - bent * bent
            ) * root * (1.0 + 3.0 * 0.044715 * pre * pre)

    def body(links, refs):
        reduce_product = rows_partial("mix", "w")

        def partial(refs, k, store):
            for h in range(heads):
                _, _, values, probs = cross_heads(refs, k, h)
                refs.mix[k, :, head_at(h)] = mm(probs.astype(BF16), values).astype(BF16)
            reduce_product(refs, k, store)

        reduce_slice(links, refs, partial, middle, refs.held)
        gather_slice(links, refs, refs.held, product)

    third = run_kernel(
        "cross_attend", 3,
        dict(
            unit=cq_unit, gain=gains8, kv=text_kv,
            w=full_crossout, start=after_self,
            vec=vectors(attn_bias[7], 1.0 + scale2, shift2),
            w2=full_up,
            bias=jnp.broadcast_to(pick(up_bias)[None], (8, hidden_width)),
        ),
        dict(
            mix=((4, tokens, width), BF16), joined=wide, held=held,
            hidden=((4, tokens, hidden_width), BF16),
            slope=((4, tokens, hidden_width), F32),
        ),
        body, reduce_scratch(tokens, dim),
        cost=60,
    )
    cross_mix, after_cross, x_ffn, hidden = third.mix, third.joined, third.held, third.hidden

    down_core = row_core(outer(hidden, g_ffn))
    down_part = scatter_z(down_core)
    inner_partial = turned_partial("d_hpre", "w_up")

    def ffn_partial(refs, k, store):
        w = refs.w_down
        deep = w.shape[2]
        for at, size in column_chunks(hidden_width, 640):
            columns = pl.ds(at, size)
            grad = mm_t(refs.g[k, :, pl.ds(0, deep)], w[0, columns])
            grad = grad + mm_t(refs.g[k, :, pl.ds(deep, deep)], w[1, columns])
            refs.d_hpre[k, :, columns] = (grad * refs.slope[k, :, columns]).astype(BF16)
        inner_partial(refs, k, store)

    def middle(refs, rows, step, total):
        normed, inverse = layer_norm(refs.joined[rows])
        d_cross = refs.top[rows] + norm_backward(normed, inverse, total * refs.vec[0:1])
        refs.d_cross[rows] = d_cross
        low = d_cross.astype(BF16)
        add_rows(refs.sums, 0, total, step)
        add_rows(refs.sums, 1, total * normed, step)
        add_rows(refs.sums, 2, low.astype(F32), step)
        return low

    def product(refs, k, piece):
        refs.d_mix[k] = rows_turned(piece, refs.w2).astype(BF16)

    def body(links, refs):
        reduce_slice(links, refs, ffn_partial, middle, refs.held)
        gather_slice(links, refs, refs.held, product)

    fourth = run_kernel(
        "ffn_back", 4,
        dict(
            g=after(g_ffn, down_core), w_down=full_down, slope=third.slope, w_up=full_up,
            joined=after_cross, top=out_grad_p, vec=vectors(1.0 + scale2),
            w2=full_crossout,
        ),
        dict(
            d_hpre=((4, tokens, hidden_width), BF16), d_cross=wide, held=held,
            d_mix=((4, tokens, width), BF16), sums=((3, 8, dim), F32),
        ),
        body, reduce_scratch(tokens, dim),
        cost=72,
    )
    d_hpre, d_cross, g_cross, d_cmix = fourth.d_hpre, fourth.d_cross, fourth.held, fourth.d_mix
    sums4 = jnp.sum(fourth.sums, 1)
    up_core = column_core(outer(x_ffn, d_hpre))
    up_part = scatter_z(up_core)

    def rms_back(grad, unit, inverse, mean):
        return inverse * (grad - unit * mean)

    def middle(refs, rows, step, total):
        normed, inverse = layer_norm(refs.joined[rows])
        vec = refs.vec
        d_self = refs.top[rows] + norm_backward(normed, inverse, total * vec[0:1])
        refs.d_self[rows] = d_self
        low = (d_self * vec[1:2]).astype(BF16)
        add_rows(refs.sums, 0, total * normed, step)
        add_rows(refs.sums, 1, total, step)
        add_rows(refs.sums, 2, low.astype(F32), step)
        add_rows(refs.sums, 3, d_self * refs.branch[rows], step)
        return low

    def body(links, refs):
        refs.stat[...] = jnp.zeros_like(refs.stat)
        refs.gains[...] = jnp.zeros_like(refs.gains)

        @pl.loop(0, 4)
        def _(k):
            square = jnp.zeros((tokens, 1), F32)
            for h in range(heads):
                q, keys, values, probs = cross_heads(refs, k, h)
                d_mix = refs.d_mix[k, :, head_at(h)]
                d_probs = mm_t(d_mix, values)
                delta = jnp.sum(probs * d_probs, -1, keepdims=True)
                d_scores = (probs * (d_probs - delta)).astype(BF16)
                d_q = mm(d_scores, keys) * SCALE
                refs.d_kv[k, :, head_at(h)] = (mm_l(d_scores, q) * SCALE).astype(BF16)
                refs.d_kv[k, :, head_at(h, width)] = mm_l(probs.astype(BF16), d_mix).astype(BF16)
                unit = refs.unit[k, :, head_at(h)]
                refs.gains[:, head_at(h)] += fold_rows(d_q * unit)
                d_q = d_q * refs.gain[2:3, head_at(h)]
                refs.d_unit[k, :, head_at(h)] = d_q
                square = square + jnp.sum(d_q * unit, -1, keepdims=True)
            refs.stat[k, pl.ds(0, 1), pl.ds(0, tokens)] = to_row(square)

        sum_stats(links, refs)

        @pl.loop(0, 4)
        def _(k):
            inverse = to_column(refs.inv[k, pl.ds(0, 1), pl.ds(0, tokens)])
            mean = to_column(refs.stat_sum[k, pl.ds(0, 1), pl.ds(0, tokens)]) / dim
            refs.d_pre[k] = rms_back(refs.d_unit[k], refs.unit[k], inverse, mean).astype(BF16)

        def product(refs, k, piece):
            refs.outs[k] = rows_turned(piece, refs.w2).astype(BF16)
            links.send_line(
                refs.outs.at[k], refs.d_heads.at[links.z], links.clip_of(k), k
            )

        reduce_slice(links, refs, turned_partial("d_pre", "w"), middle, refs.held)
        gather_slice(links, refs, refs.held, product)
        for source in range(seqs):
            links.wait_line(refs.d_heads.at[source], source)

    fifth = run_kernel(
        "cross_back", 5,
        dict(
            unit=cq_unit, inv=cq_inv, gain=gains8, kv=text_kv,
            d_mix=after(d_cmix, up_core, down_part),
            w=cross_wq, joined=after_self, top=d_cross, branch=branch,
            vec=vectors(norm_gain, gate1), w2=full_out,
        ),
        dict(
            d_pre=((4, tokens, width), BF16), d_kv=((4, texts, 2 * width), BF16),
            gains=((8, width), F32), d_self=wide, held=held,
            d_heads=((seqs, tokens, width), BF16), sums=((4, 8, dim), F32),
        ),
        body,
        dict(
            d_unit=((4, tokens, width), F32), outs=((4, tokens, width), BF16),
            **reduce_scratch(tokens, dim),
        ),
        stats=True, line=1,
        cost=80,
    )
    d_cq, d_self, g_self, d_heads = fifth.d_pre, fifth.d_self, fifth.held, fifth.d_heads
    cq_gain = jnp.sum(fifth.gains, 0)
    sums5 = jnp.sum(fifth.sums, 1)
    d_kv, mixed, cross_mix = after((fifth.d_kv, mixed, cross_mix), up_part)
    outproj_core = row_core(outer(mixed, g_self))
    crossout_core = row_core(outer(cross_mix, g_cross))
    d_kv = d_kv.reshape(4, seqs, -1, 2 * width).transpose(1, 0, 2, 3)
    parts = [d_kv.reshape(seqs, -1, 2 * width)]
    parts += [v.reshape(seqs, -1, 2 * width) for v in (outproj_core, crossout_core)]
    joint_core = jnp.concatenate(parts, 1)
    joint_part = lax.psum_scatter(joint_core, "z", scatter_dimension=0, tiled=True)[0]

    def middle(refs, rows, step, total):
        normed, inverse = layer_norm(refs.states[rows])
        refs.out[rows] = refs.top[rows] + norm_backward(
            normed, inverse, total * refs.vec[0:1]
        )
        add_rows(refs.sums, 0, total, step)
        add_rows(refs.sums, 1, total * normed, step)

    def body(links, refs):
        refs.stat[...] = jnp.zeros_like(refs.stat)
        refs.gains[...] = jnp.zeros_like(refs.gains)
        packed, d_heads = refs.packed, refs.d_heads
        for h in range(heads):
            refs.d_keys[...] = jnp.zeros_like(refs.d_keys)
            refs.d_values[...] = jnp.zeros_like(refs.d_values)

            @pl.loop(0, seqs)
            def _(i):
                keys = packed[:, :, head_at(h, width)].reshape(clip_rows, HD)
                values = packed[:, :, head_at(h, 2 * width)].reshape(clip_rows, HD)
                q = packed[i, :, head_at(h)]
                d_mix = d_heads[i, :, head_at(h)]
                probs = softmax(masked_scores(q, keys))
                d_probs = mm_t(d_mix, values)
                delta = jnp.sum(probs * d_probs, -1, keepdims=True)
                d_scores = (probs * (d_probs - delta)).astype(BF16)
                refs.outs[h, i, :, pl.ds(0, HD)] = (mm(d_scores, keys) * SCALE).astype(BF16)
                refs.d_keys[...] += mm_l(d_scores, q)
                refs.d_values[...] += mm_l(probs.astype(BF16), d_mix)

            for i in range(seqs):
                rows = pl.ds(i * tokens, tokens)
                refs.outs[h, i, :, pl.ds(HD, HD)] = (refs.d_keys[rows] * SCALE).astype(BF16)
                refs.outs[h, i, :, pl.ds(2 * HD, HD)] = refs.d_values[rows].astype(BF16)
            for step in range(seqs):
                to = (links.z + 1 + step) % seqs
                links.send_line(
                    refs.outs.at[h, to],
                    refs.arrived.at[h, links.clip_of(links.z)],
                    to, step, h,
                )
        for k in range(4):
            for h in range(heads):
                links.wait_line(refs.arrived.at[h, k], links.clip_of(k), h)

        @pl.loop(0, 4)
        def _(k):
            for part in range(2):
                square = jnp.zeros((tokens, 1), F32)
                for h in range(heads):
                    at = head_at(h, part * width)
                    grad = refs.arrived[h, k, :, pl.ds(part * HD, HD)].astype(F32)
                    grad = grad * refs.tables[k, :, pl.ds(0, HD)] - swap_pairs(grad) * refs.tables[k, :, pl.ds(HD, HD)]
                    unit = refs.unit[k, :, at]
                    refs.gains[part, :, head_at(h)] += fold_rows(grad * unit)
                    grad = grad * refs.gain[pl.ds(part, 1), head_at(h)]
                    refs.d_unit[k, :, at] = grad
                    square = square + jnp.sum(grad * unit, -1, keepdims=True)
                refs.stat[k, pl.ds(part, 1), pl.ds(0, tokens)] = to_row(square)
            for h in range(heads):
                refs.d_qkv[k, :, head_at(h, 2 * width)] = refs.arrived[
                    h, k, :, pl.ds(2 * HD, HD)
                ]

        sum_stats(links, refs)

        @pl.loop(0, 4)
        def _(k):
            for part in range(2):
                row = (k, pl.ds(part, 1), pl.ds(0, tokens))
                inverse = to_column(refs.inv[row])
                mean = to_column(refs.stat_sum[row]) / dim
                at = pl.ds(part * width, width)
                refs.d_qkv[k, :, at] = rms_back(
                    refs.d_unit[k, :, at], refs.unit[k, :, at], inverse, mean
                ).astype(BF16)

        reduce_slice(links, refs, turned_partial("d_qkv", "w"), middle)

    sixth = run_kernel(
        "self_back", 6,
        dict(
            packed=packed, d_heads=d_heads, unit=self_unit, inv=self_inv,
            gain=gains8, tables=tables, w=full_qkv, states=states_p,
            top=after(d_self, joint_core), vec=vectors(1.0 + scale1),
        ),
        dict(
            d_qkv=((4, tokens, blocks3), BF16), gains=((2, 8, width), F32),
            out=wide, sums=((2, 8, dim), F32),
        ),
        body,
        dict(
            outs=((heads, seqs, tokens, 3 * HD), BF16),
            arrived=((heads, 4, tokens, 3 * HD), BF16),
            d_keys=((clip_rows, HD), F32), d_values=((clip_rows, HD), F32),
            d_unit=((4, tokens, 2 * width), F32),
            **reduce_scratch(tokens, dim),
        ),
        stats=True, line=heads,
        cost=120,
    )
    d_qkv, hidden, d_hpre, d_cq, up_part, down_part = after(
        (sixth.d_qkv, hidden, d_hpre, d_cq, up_part, down_part),
        joint_part,
    )
    text_rows, weight_rows = parts[0].shape[1], parts[1].shape[1]
    d_ckv = joint_part[:text_rows].reshape(4, -1, 2 * width)
    outproj_part = over_reps(joint_part[text_rows : text_rows + weight_rows])
    crossout_part = over_reps(joint_part[text_rows + weight_rows :])
    d_qkv_sum = jnp.sum(d_qkv.astype(F32), (0, 1))
    q_gain, k_gain = jnp.sum(sixth.gains, 1)
    states_grad = sixth.out[:own_tokens]
    sums6 = jnp.sum(sixth.sums, 1)
    qkv_core = column_core(outer(x_self, d_qkv))
    qkv_part = scatter_z(qkv_core)

    d_ckn = d_ckv[..., :width].astype(F32)
    d_cv = d_ckv[..., width:]
    zpos = lax.axis_index("z")
    own = texts // seqs
    ck_unit = lax.dynamic_slice_in_dim(ck_unit, zpos * own, own, 1)
    ck_inv = lax.dynamic_slice_in_dim(ck_inv, zpos * own, own, 1)
    x_text = lax.dynamic_slice_in_dim(x_text, zpos * own, own, 1)
    d_cku = d_ckn * gain[3]
    ck_stat = sum4(jnp.sum(d_cku * ck_unit, -1)) / dim
    d_ck = rms_back(d_cku, ck_unit, ck_inv, ck_stat[..., None]).astype(BF16)
    ck_gain = jnp.sum(d_ckn * ck_unit, (0, 1))
    d_text = jnp.concatenate([d_ck, d_cv], -1)
    text_grad = reduce4(lambda k: mm_t(d_ck[k], cross_wk) + mm_t(d_cv[k], cross_wv))
    cross_core = column_core(jnp.concatenate([outer(x_cross, d_cq), outer(x_text, d_text)], 1))
    cross_part = scatter_z(cross_core)

    ffn_out = reduce4(lambda k: rows_mm(hidden[k], full_down)) + down_bias
    block_out = (after_cross + ffn_out * gate2)[:own_tokens]
    up_grad = column_done(up_part, 1)[:, 0]
    down_grad = row_done(down_part)
    qkv_grad = column_done(qkv_part, 3)
    outproj_grad = row_done(outproj_part)
    cross_grad = column_done(cross_part, 3)
    crossout_grad = row_done(crossout_part)

    def column_sum(v):
        return jnp.sum(v.astype(F32), tuple(range(v.ndim - 1)))

    def over_z(v):
        v = v + lax.ppermute(v, "z", [(i, i ^ 1) for i in range(seqs)])
        return v + lax.ppermute(v, "z", [(i, i ^ 2) for i in range(seqs)])

    def over_clips(v):
        v = v + from_core(v)
        v = v + from_x(v)
        v = v + from_y(v)
        return over_reps(v)

    early = jnp.stack(
        [
            sums4[0],
            sums4[1],
            column_sum(out_grad_p * ffn_out),
            spread(column_sum(d_cq)),
            spread(column_sum(d_ck)),
            spread(column_sum(d_cv)),
            sums4[2],
            spread(cq_gain),
            spread(ck_gain),
            sums5[0],
            sums5[1],
            column_sum(d_ffnout),
            sums5[2],
            sums5[3],
        ]
    )
    upbias = over_clips(over_z(spread(column_sum(d_hpre))))
    early_clip = over_z(early)
    early_all = over_clips(early_clip)
    late = jnp.stack(
        [
            sums6[0],
            sums6[1],
            spread(d_qkv_sum[:width]),
            spread(d_qkv_sum[width : 2 * width]),
            spread(d_qkv_sum[2 * width :]),
            spread(q_gain),
            spread(k_gain),
        ]
    )
    late_clip = over_z(late)
    late_all = over_clips(late_clip)

    def mod_rows(e, l):
        return jnp.stack([l[0], l[1], e[13], e[0], e[1], e[2]])

    time_grad = mod_rows(early_clip, late_clip)[None]
    mod_grad = mod_rows(early_all, late_all)
    bias_grad = jnp.stack(
        [late_all[2], late_all[3], late_all[4], early_all[12]] + [early_all[i] for i in (3, 4, 5, 6)]
    )
    gain_grad = jnp.stack([late_all[5], late_all[6], early_all[7], early_all[8]])
    return (
        block_out, states_grad, text_grad, time_grad, qkv_grad, outproj_grad, cross_grad,
        crossout_grad, up_grad, down_grad, bias_grad, gain_grad, early_all[9], early_all[10],
        upbias, early_all[11], mod_grad,
    )


def solution(mesh):
    reps, shards, seqs = mesh.shape["replica"], mesh.shape["shard"], mesh.shape["seq"]
    fine = Mesh(
        mesh.devices.reshape(reps // 2, 2, shards // 2, 2, seqs), ("rep", "x", "y", "core", "z")
    )
    tokens = P(("rep", "x", "y", "core", "z"), None)
    clips = P(("rep", "x", "y", "core"), None, None)
    rows2 = P(("y", "core", "z"), None)
    rows3 = P(("y", "core", "z"), None, None)
    return jax.shard_map(
        on_device,
        mesh=fine,
        in_specs=(
            tokens, tokens, P(None, ("rep", "x", "y", "core", "z")), clips,
            rows3, rows2, rows3, rows2, rows2, rows2,
            P(), P(), P(), P(), P(), P(), P(), tokens,
        ),
        out_specs=(
            tokens, tokens, tokens, clips,
            rows3, rows2, rows3, rows2, rows2, rows2,
            P(), P(), P(), P(), P(), P(), P(),
        ),
        check_vma=False,
    )
```

```python
import math
from types import SimpleNamespace

import jax
import jax.numpy as jnp
import numpy as np
from jax import lax
from jax.experimental import pallas as pl
from jax.experimental.pallas import tpu as pltpu
from jax.sharding import Mesh, PartitionSpec as P

HD = 128
EPS = 1e-06
F32 = jnp.float32
BF16 = jnp.bfloat16
SCALE = 1.0 / math.sqrt(HD)
SWAP = [(0, 1), (1, 0)]
ROWS = 16
FLOPS = 1_150_000_000
BYTES = 3_600_000


def rope_tables(grid_pos):
    pairs = HD // 2
    width = pairs // 3
    first = pairs - 2 * width
    index = np.arange(pairs)
    part = np.where(index < first, 0, np.where(index < first + width, 1, 2))
    offset = np.where(part == 0, index, np.where(part == 1, index - first, index - first - width))
    frequency = 10000.0 ** (-offset / np.where(part == 0, first, width))
    position = grid_pos.astype(F32)
    angles = 0.0
    for axis in range(3):
        lane = np.repeat(frequency * (part == axis), 2)
        angles = angles + position[axis][:, None] * jnp.asarray(lane, F32)[None, :]
    sign = np.where(np.arange(HD) % 2 == 0, -1.0, 1.0)
    return jnp.cos(angles), jnp.sin(angles) * jnp.asarray(sign, F32)[None, :]


def layer_norm(values):
    center = values - jnp.mean(values, -1, keepdims=True)
    inverse = lax.rsqrt(jnp.mean(center * center, -1, keepdims=True) + EPS)
    return center * inverse, inverse


def norm_backward(normed, inverse, grad_in):
    return inverse * (
        grad_in
        - jnp.mean(grad_in, -1, keepdims=True)
        - normed * jnp.mean(grad_in * normed, -1, keepdims=True)
    )


def mm(a, b):
    return lax.dot_general(a, b, (((a.ndim - 1,), (0,)), ((), ())), preferred_element_type=F32)


def mm_t(a, b):
    return lax.dot_general(a, b, (((a.ndim - 1,), (1,)), ((), ())), preferred_element_type=F32)


def rows_mm(a, w):
    return jnp.concatenate([mm(a, w[0]), mm(a, w[1])], -1)


def after(value, *done):
    return lax.optimization_barrier((value, done))[0]


def tied(value, done):
    anywhere = pl.BlockSpec(memory_space=pl.ANY)
    return pl.pallas_call(
        lambda *refs: None,
        name="tied",
        out_shape=jax.ShapeDtypeStruct(value.shape, value.dtype),
        in_specs=[anywhere] * 2,
        out_specs=anywhere,
        input_output_aliases={0: 0},
    )(value, done)


def outer(a, b):
    lead = tuple(range(a.ndim - 1))
    return lax.dot_general(a, b, ((lead, lead), ((), ())), preferred_element_type=F32)


def column_chunks(total, size):
    return [(at, min(size, total - at)) for at in range(0, total, size)]


class Links:
    def __init__(self, named, stats, line, pair):
        self.named = named
        self.used = 0
        self.started = []
        self.x, self.y, self.z = [lax.axis_index(n) for n in ("x", "y", "z")]
        self.seqs = lax.axis_size("z")
        barrier = pltpu.get_barrier_semaphore()
        peers = [{"x": 1 - self.x}, {"y": 1 - self.y}]
        if stats:
            peers.append({"x": 1 - self.x, "y": 1 - self.y})
        if pair:
            peers.append({"core": 1 - lax.axis_index("core")})
        if line:
            peers += [{"z": (self.z + step) % self.seqs} for step in range(1, self.seqs)]
        for peer in peers:
            pl.semaphore_signal(
                barrier, inc=1, device_id=peer, device_id_type=pl.DeviceIdType.MESH
            )
        pl.semaphore_wait(barrier, len(peers))

    def clip_of(self, piece):
        return ((piece // 2 + self.x) % 2) * 2 + (piece % 2 + self.y) % 2

    def send(self, axis, src, dst):
        return self.send_to({a: 1 - lax.axis_index(a) for a in axis}, src, dst)

    def send_to(self, where, src, dst):
        index = self.used
        self.used += 1
        sems = self.named.sems
        copy = pltpu.make_async_remote_copy(
            src_ref=src,
            dst_ref=dst,
            send_sem=sems.at[0, index],
            recv_sem=sems.at[1, index],
            device_id=where,
            device_id_type=pl.DeviceIdType.MESH,
        )
        copy.start()
        self.started.append((None, copy))
        return copy

    def send_line(self, src, dst, to, slot, lane=0):
        sems = self.named.line
        copy = pltpu.make_async_remote_copy(
            src_ref=src,
            dst_ref=dst,
            send_sem=sems.at[0, lane, slot],
            recv_sem=sems.at[1, lane, self.z],
            device_id={"z": to},
            device_id_type=pl.DeviceIdType.MESH,
        )

        @pl.when(to != self.z)
        def _():
            copy.start()

        @pl.when(to == self.z)
        def _():
            dst[...] = src[...]

        self.started.append((to != self.z, copy))

    def wait_line(self, ref, source, lane=0):
        sems = self.named.line
        copy = pltpu.make_async_remote_copy(
            src_ref=ref,
            dst_ref=ref,
            send_sem=sems.at[0, lane, 0],
            recv_sem=sems.at[1, lane, source],
            device_id={"z": (self.z + 1) % self.seqs},
            device_id_type=pl.DeviceIdType.MESH,
        )

        @pl.when(source != self.z)
        def _():
            copy.wait_recv()

    def finish(self):
        for needed, copy in self.started:
            if needed is None:
                copy.wait_send()
            else:
                pl.when(needed)(copy.wait_send)


def split_rows(tokens):
    return ((tokens // 2 + ROWS - 1) // ROWS) * ROWS


def row_steps(tokens, body):
    @pl.loop(0, tokens // ROWS)
    def _(step):
        body(pl.ds(pl.multiple_of(step * ROWS, ROWS), ROWS), step)


def reduce_begin(links, refs, buffers, partial):
    mine, near, far, total = buffers
    tokens = total.shape[0]
    half = split_rows(tokens)
    top, low = pl.ds(0, half), pl.ds(half, tokens - half)

    def store_low(slot):
        def store(columns, value):
            mine[slot, :, columns] = value.astype(BF16)

        return store

    partial(refs, 3, store_low(2))
    far_x = links.send("x", mine.at[2, top], far.at[top])
    far_y = links.send("y", mine.at[2, low], far.at[low])
    partial(refs, 2, store_low(1))
    x_top = links.send("x", mine.at[1, top], near.at[1, top])
    partial(refs, 1, store_low(0))
    y_low = links.send("y", mine.at[0, low], near.at[0, low])
    return far_x, far_y, x_top, y_low


def reduce_relay(links, buffers, copies):
    mine, near, far, total = buffers
    tokens = total.shape[0]
    half = split_rows(tokens)
    top, low = pl.ds(0, half), pl.ds(half, tokens - half)
    far_x, far_y, x_top, y_low = copies
    far_x.wait_recv()
    mine[0, top] = (mine[0, top].astype(F32) + far[top].astype(F32)).astype(BF16)
    y_top = links.send("y", mine.at[0, top], near.at[0, top])
    far_y.wait_recv()
    mine[1, low] = (mine[1, low].astype(F32) + far[low].astype(F32)).astype(BF16)
    x_low = links.send("x", mine.at[1, low], near.at[1, low])
    return x_top, y_low, y_top, x_low


def reduce_own(refs, buffers, partial):
    total = buffers[3]

    def store_full(columns, value):
        total[:, columns] = value

    partial(refs, 0, store_full)


def reduce_end(refs, buffers, copies, middle, keep=None):
    mine, near, far, total = buffers
    for copy in copies:
        copy.wait_recv()

    def body(rows, step):
        value = total[rows] + near[0, rows].astype(F32) + near[1, rows].astype(F32)
        sent = middle(refs, rows, step, value)
        if keep is not None:
            keep[0, rows] = sent

    row_steps(total.shape[0], body)


def reduce_slice(links, refs, partial, middle, keep=None):
    buffers = (refs.mine, refs.near, refs.far, refs.total)
    copies = reduce_begin(links, refs, buffers, partial)
    copies = reduce_relay(links, buffers, copies)
    reduce_own(refs, buffers, partial)
    reduce_end(refs, buffers, copies, middle, keep)


def gather_begin(links, held):
    return links.send("x", held.at[0], held.at[2]), links.send("y", held.at[0], held.at[1])


def gather_relay(links, held, first):
    tokens = held.shape[1]
    half = split_rows(tokens)
    top, low = pl.ds(0, half), pl.ds(half, tokens - half)
    from_x, from_y = first
    from_x.wait_recv()
    far_top = links.send("y", held.at[2, top], held.at[3, top])
    from_y.wait_recv()
    far_low = links.send("x", held.at[1, low], held.at[3, low])
    return far_top, far_low


def gather_end(far):
    for copy in far:
        copy.wait_recv()


def gather_slice(links, refs, held, product, also=()):
    arrays = (held,) + tuple(also)
    first = [gather_begin(links, array) for array in arrays]
    product(refs, 0, held.at[0])
    far = [gather_relay(links, array, copies) for array, copies in zip(arrays, first)]
    product(refs, 1, held.at[1])
    product(refs, 2, held.at[2])
    for copies in far:
        gather_end(copies)
    product(refs, 3, held.at[3])


def sum_stats(links, refs):
    stat, other = refs.stat, refs.stats_in
    copies = [
        links.send("y", stat, other.at[0]),
        links.send("x", stat, other.at[1]),
        links.send("xy", stat, other.at[2]),
    ]
    for copy in copies:
        copy.wait_recv()
    for copy in copies:
        copy.wait_send()
    del links.started[-3:]
    for k in range(4):
        refs.stat_sum[k] = (
            stat[k] + other[0, k ^ 1] + other[1, k ^ 2] + other[2, k ^ 3]
        )


def to_row(column):
    size = column.shape[0]
    same = lax.broadcasted_iota(jnp.int32, (size, size), 0) == lax.broadcasted_iota(
        jnp.int32, (size, size), 1
    )
    return jnp.sum(jnp.where(same, column, 0.0), 0, keepdims=True)


def to_column(row):
    size = row.shape[1]
    same = lax.broadcasted_iota(jnp.int32, (size, size), 0) == lax.broadcasted_iota(
        jnp.int32, (size, size), 1
    )
    return jnp.sum(jnp.where(same, row, 0.0), 1, keepdims=True)


def run_kernel(name, cid, inputs, outputs, body, scratch, cost, stats=False, line=0, pair=False):
    names_in, names_out = list(inputs), list(outputs)
    spaces = dict(sems=pltpu.SemaphoreType.DMA((2, 24)))
    if line:
        spaces.update(line=pltpu.SemaphoreType.DMA((2, line, 4)))
    if stats:
        spaces.update(
            stat=pltpu.VMEM((4, 8, 256), F32),
            stat_sum=pltpu.VMEM((4, 8, 256), F32),
            stats_in=pltpu.VMEM((3, 4, 8, 256), F32),
        )
    for key, (shape, dtype) in scratch.items():
        spaces[key] = pltpu.VMEM(shape, dtype)

    def kernel(*refs):
        named = SimpleNamespace(**dict(zip(names_in + names_out + list(spaces), refs)))
        links = Links(named, stats, line, pair)
        body(links, named)
        links.finish()

    vmem = pl.BlockSpec(memory_space=pltpu.VMEM)
    result = pl.pallas_call(
        kernel,
        name=name,
        out_shape=[jax.ShapeDtypeStruct(*outputs[n]) for n in names_out],
        in_specs=[vmem] * len(names_in),
        out_specs=[vmem] * len(names_out),
        scratch_shapes=list(spaces.values()),
        cost_estimate=pl.CostEstimate(
            flops=cost * FLOPS, bytes_accessed=cost * BYTES, transcendentals=0
        ),
        compiler_params=pltpu.CompilerParams(
            collective_id=cid, has_side_effects=True, vmem_limit_bytes=60 * 1024 * 1024
        ),
    )(*[inputs[n] for n in names_in])
    return SimpleNamespace(**dict(zip(names_out, result)))


def reduce_scratch(tokens, dim):
    return dict(
        mine=((3, tokens, dim), BF16),
        near=((2, tokens, dim), BF16),
        far=((tokens, dim), BF16),
        total=((tokens, dim), F32),
    )


def add_rows(ref, index, value, step):
    @pl.when(step == 0)
    def _():
        ref[index] = jnp.zeros_like(ref[index])

    ref[index] += value[:8] + value[8:]


def fold_rows(value):
    return jnp.sum(value.reshape(value.shape[0] // 8, 8, value.shape[1]), 0)


def rows_partial(a, w):
    def partial(refs, k, store):
        piece = getattr(refs, a)[k]
        blocks = getattr(refs, w)
        deep, width = piece.shape[1], blocks.shape[2]
        for half in range(2):
            for part in range(2):
                store(
                    pl.ds((half * 2 + part) * width, width),
                    mm(piece, blocks[part, pl.ds(half * deep, deep), :]),
                )

    return partial


def turned_partial(a, w, size=256):
    def partial(refs, k, store):
        deep = getattr(refs, a).shape[2]

        @pl.loop(0, getattr(refs, w).shape[0] // size)
        def _(step):
            rows = pl.ds(pl.multiple_of(step * size, size), size)
            store(rows, mm_t(getattr(refs, a)[k], getattr(refs, w)[rows, pl.ds(0, deep)]))

    return partial


def rows_turned(piece, w):
    deep, width = w.shape[1] // 2, w.shape[2]
    total = 0.0
    for half in range(2):
        for part in range(2):
            columns = pl.ds((half * 2 + part) * width, width)
            total = total + mm_t(piece[:, columns], w[part, pl.ds(half * deep, deep), :])
    return total


def mm_l(a, b):
    return lax.dot_general(a, b, (((0,), (0,)), ((), ())), preferred_element_type=F32)


def swap_pairs(values):
    even = lax.broadcasted_iota(jnp.int32, values.shape, 1) % 2 == 0
    return jnp.where(even, pltpu.roll(values, HD - 1, 1), pltpu.roll(values, 1, 1))


def softmax(scores):
    weight = jnp.exp(scores - jnp.max(scores, -1, keepdims=True))
    return weight * (1.0 / jnp.sum(weight, -1, keepdims=True))


def head_at(h, base=0):
    return pl.ds(base + h * HD, HD)


def on_device(
    states, text_emb, grid_pos, time_mod, w_qkv, w_out, w_cross, w_crossout, w_up, w_down,
    attn_bias, qk_gain, norm_gain, norm_bias, up_bias, down_bias, modulation, out_grad,
):
    x, y, core = lax.axis_index("x"), lax.axis_index("y"), lax.axis_index("core")
    seqs = lax.axis_size("z")
    reps = lax.axis_size("rep")
    own_tokens, dim = states.shape
    tokens = -(-own_tokens // ROWS) * ROWS
    block = y * 2 + x
    pad = ((0, tokens - own_tokens), (0, 0))
    states_p = jnp.pad(states, pad)
    out_grad_p = jnp.pad(out_grad, pad)

    def from_y(a):
        return lax.ppermute(a, "y", SWAP)

    def from_x(a):
        return lax.ppermute(a, "x", SWAP)

    def from_xy(a):
        return lax.ppermute(a, ("x", "y"), [(i, 3 - i) for i in range(4)])

    def from_core(a):
        return lax.ppermute(a, "core", SWAP)

    def gather4(a):
        far, xs, ys = from_xy(a), from_x(a), from_y(a)
        return jnp.stack([a, ys, xs, far])

    def reduce4(term):
        far = from_xy(term(3).astype(BF16))
        xs = from_x(term(2).astype(BF16))
        ys = from_y(term(1).astype(BF16))
        return term(0) + ys.astype(F32) + xs.astype(F32) + far.astype(F32)

    def sum4(stat):
        far, xs, ys = from_xy(stat), from_x(stat), from_y(stat)
        return (
            stat
            + jnp.stack([ys[1], ys[0], ys[3], ys[2]])
            + jnp.stack([xs[2], xs[3], xs[0], xs[1]])
            + jnp.stack([far[3], far[2], far[1], far[0]])
        )

    def pick(v, blocks=4):
        return lax.dynamic_index_in_dim(
            v.reshape(v.shape[:-1] + (blocks, v.shape[-1] // blocks)), block, v.ndim - 1, False
        )

    def spread(v):
        hot = (jnp.arange(4) == block).astype(F32)
        full = v[..., None, :] * hot[:, None]
        return full.reshape(v.shape[:-1] + (4 * v.shape[-1],))

    def column_own(w):
        rows, groups, width = w.shape[0], w.shape[1], w.shape[2] // 4
        mine = lax.dynamic_index_in_dim(w.reshape(rows, groups, 2, 2, width), x, 3, False)
        keep = lax.dynamic_index_in_dim(mine, y, 2, False).reshape(rows, groups * width)
        send = lax.dynamic_index_in_dim(mine, 1 - y, 2, False).reshape(rows, groups * width)
        recv = from_y(send)
        return jnp.where(y == 0, jnp.stack([keep, recv]), jnp.stack([recv, keep]))

    def column_block(w):
        full = lax.all_gather(column_own(w), ("core", "z"), axis=1, tiled=True)
        return full.reshape(-1, full.shape[2])

    def row_own(w):
        half = w.shape[1] // 2
        keep = lax.dynamic_slice_in_dim(w, core * half, half, 1)
        recv = from_core(lax.dynamic_slice_in_dim(w, (1 - core) * half, half, 1))
        return jnp.where(core == x, keep, recv)

    def row_block(w):
        full = lax.all_gather(row_own(w), ("core", "z"), axis=0, tiled=True)
        return full.reshape(2, -1, full.shape[1])

    def row_halves(w):
        mine = row_own(w)
        half = mine.shape[1] // 2
        return jnp.stack([mine[:, :half], mine[:, half:]])

    def attention_blocks(w_cross, w_out):
        own = column_own(w_cross)
        width = own.shape[2] // 3
        blocks = [own[:, :, g * width : (g + 1) * width] for g in range(3)]
        blocks.append(row_halves(w_out))
        return lax.all_gather(jnp.concatenate(blocks), ("core", "z"), axis=1, tiled=True)

    def up_block(w_up, w_crossout):
        own = jnp.concatenate([column_own(w_up[:, None, :]), row_halves(w_crossout)], 2)
        return lax.all_gather(own, ("core", "z"), axis=1, tiled=True)

    def over_reps(a):
        return lax.psum(a, "rep") if reps > 1 else a

    def column_core(g):
        g = g.astype(BF16).reshape(2, 2, seqs, -1, g.shape[1])
        keep = lax.dynamic_index_in_dim(g, core, 1, False)
        recv = from_core(lax.dynamic_index_in_dim(g, 1 - core, 1, False))
        both = (keep.astype(F32) + recv.astype(F32)).astype(BF16)
        return both.transpose(1, 0, 2, 3).reshape(-1, g.shape[4])

    def row_core(g):
        half = g.shape[1] // 2
        g = g.astype(BF16)
        keep = lax.dynamic_slice_in_dim(g, core * half, half, 1)
        recv = from_core(lax.dynamic_slice_in_dim(g, (1 - core) * half, half, 1))
        return (keep.astype(F32) + recv.astype(F32)).astype(BF16)

    def scatter_z(a):
        return over_reps(lax.psum_scatter(a, "z", scatter_dimension=0, tiled=True))

    def column_done(part, groups):
        width = part.shape[1] // groups
        part = part.reshape(2, -1, groups * width)
        keep = lax.dynamic_index_in_dim(part, y, 0, False)
        recv = from_y(lax.dynamic_index_in_dim(part, 1 - y, 0, False))
        ours = jnp.where(y == 0, jnp.stack([keep, recv]), jnp.stack([recv, keep]))
        theirs = from_x(ours)
        rows = ours.shape[1]
        ours = ours.reshape(2, rows, groups, width)
        theirs = theirs.reshape(2, rows, groups, width)
        full = jnp.where(x == 0, jnp.stack([ours, theirs], 1), jnp.stack([theirs, ours], 1))
        return full.transpose(2, 3, 0, 1, 4).reshape(rows, groups, 4 * width).astype(F32)

    def row_done(part):
        other = from_x(part)
        ours = jnp.where(core == x, part, other)
        theirs = from_core(jnp.where(core == x, other, part))
        full = jnp.where(
            core == 0,
            jnp.concatenate([ours, theirs], 1),
            jnp.concatenate([theirs, ours], 1),
        )
        return full.astype(F32)

    mods = modulation + time_mod[0]
    shift1, scale1, gate1, shift2, scale2, gate2 = [mods[i] for i in range(6)]

    def vectors(*rows):
        return jnp.stack(rows + (jnp.zeros_like(rows[0]),) * (8 - len(rows)))

    full_qkv = column_block(w_qkv)
    text_z = lax.all_gather(text_emb, "z", axis=0, tiled=True)
    attend_w = attention_blocks(w_cross, w_out)
    cross_wq, cross_wk, cross_wv = [
        attend_w[2 * g : 2 * g + 2].reshape(dim, -1) for g in range(3)
    ]
    full_out = attend_w[6:8]
    up_w = up_block(w_up, w_crossout)
    hidden_width = w_up.shape[1] // 4
    full_crossout = up_w[:, :, hidden_width:]
    full_up = up_w.reshape(dim, -1)
    full_down = row_block(w_down)
    bias = pick(attn_bias)
    gain = pick(qk_gain)
    width = bias.shape[1]
    heads = width // HD
    own_tables = jnp.pad(jnp.concatenate(rope_tables(grid_pos), 1), pad)
    d_ffnout = (out_grad_p * gate2).astype(BF16)

    def rms_scale(v):
        return lax.rsqrt(v / dim + EPS)[..., None]

    wide = ((tokens, dim), F32)
    held = ((4, tokens, dim), BF16)
    head_block = ((4, tokens, width), F32)

    blocks3 = 3 * width
    clip_rows = seqs * tokens

    def middle(refs, rows):
        normed, _ = layer_norm(refs.states[rows])
        vec = refs.vec
        return (normed * vec[0:1] + vec[1:2]).astype(BF16)

    def body(links, refs):
        refs.stat[...] = jnp.zeros_like(refs.stat)

        def rows_in(rows, step):
            refs.held[0, rows] = middle(refs, rows)

        def send_heads(k, columns, lane):
            links.send_line(
                refs.sent.at[k, :, columns], refs.packed.at[links.z, :, columns],
                links.clip_of(k), k, lane,
            )

        early, late = pl.ds(2 * width, width), pl.ds(0, 2 * width)

        def product(refs, k, piece):
            pre = mm(piece[...], refs.w[:, early]) + refs.bias[0:1, early]
            refs.sent[k, :, early] = pre.astype(BF16)
            send_heads(k, early, 0)
            for part in range(2):
                columns = pl.ds(part * width, width)
                pre = mm(piece[...], refs.w[:, columns]) + refs.bias[0:1, columns]
                refs.unit[k, :, columns] = pre
                square = jnp.sum(pre * pre, -1, keepdims=True)
                refs.stat[k, pl.ds(part, 1), pl.ds(0, tokens)] = to_row(square)

        refs.tables[0] = refs.own_tables[...]
        refs.texts[0] = refs.text[...]
        row_steps(tokens, rows_in)
        gather_slice(links, refs, refs.held, product, (refs.tables,))
        sum_stats(links, refs)
        refs.inv[...] = lax.rsqrt(refs.stat_sum[...] / dim + EPS)
        first = gather_begin(links, refs.texts)
        for k in (3, 2, 1, 0):
            cosine, sine = refs.tables[k, :, pl.ds(0, HD)], refs.tables[k, :, pl.ds(HD, HD)]
            for part in range(2):
                inverse = to_column(refs.inv[k, pl.ds(part, 1), pl.ds(0, tokens)])
                for h in range(heads):
                    at = head_at(h, part * width)
                    unit = refs.unit[k, :, at] * inverse
                    refs.unit[k, :, at] = unit
                    scaled = unit * refs.gain[pl.ds(part, 1), head_at(h)]
                    turned = scaled * cosine + swap_pairs(scaled) * sine
                    refs.sent[k, :, at] = turned.astype(BF16)
            send_heads(k, late, 1)
        gather_end(gather_relay(links, refs.texts, first))
        for source in range(seqs):
            links.wait_line(refs.packed.at[source, :, early], source, 0)
            links.wait_line(refs.packed.at[source, :, late], source, 1)

    gains8 = jnp.pad(gain, ((0, 4), (0, 0)))
    texts = text_z.shape[0]
    first = run_kernel(
        "self_in", 1,
        dict(
            states=states_p, vec=vectors(1.0 + scale1, shift1), w=full_qkv,
            bias=jnp.broadcast_to(bias[:3].reshape(1, -1), (8, blocks3)),
            gain=gains8, own_tables=own_tables, text=text_z,
        ),
        dict(
            held=held, unit=((4, tokens, 2 * width), F32), inv=((4, 8, 256), F32),
            packed=((seqs, tokens, blocks3), BF16), texts=((4, texts, dim), BF16),
            tables=((4, tokens, 2 * HD), F32),
        ),
        body, dict(sent=((4, tokens, blocks3), BF16)), stats=True, line=2, cost=70,
    )
    x_self, self_unit, self_inv, packed = first.held, first.unit, first.inv, first.packed
    x_text, tables = first.texts, first.tables

    def masked_scores(q, keys):
        scores = mm_t(q, keys) * SCALE
        column = lax.broadcasted_iota(jnp.int32, scores.shape, 1)
        return jnp.where(column % tokens < own_tokens, scores, -1e30)

    def middle(refs, rows, step, total):
        vec = refs.vec
        branch = total + vec[0:1]
        refs.branch[rows] = branch
        joined = refs.states[rows] + branch * vec[1:2]
        refs.joined[rows] = joined
        normed, _ = layer_norm(joined)
        return (normed * vec[2:3] + vec[3:4]).astype(BF16)

    def product(refs, k, piece):
        pre = mm(piece[...], refs.w2[:, pl.ds(0, width)]) + refs.bias[0:1]
        refs.unit[k] = pre
        refs.stat[k, pl.ds(0, 1), pl.ds(0, tokens)] = to_row(jnp.sum(pre * pre, -1, keepdims=True))

    def body(links, refs):
        refs.stat[...] = jnp.zeros_like(refs.stat)
        packed = refs.packed
        refs.grads[0] = refs.own_grads[...]
        first = gather_begin(links, refs.grads)
        for turn in (1, 2, 3, 0):
            to = (links.z + turn) % seqs
            for h in range(heads):
                keys = packed[:, :, head_at(h, width)].reshape(clip_rows, HD)
                values = packed[:, :, head_at(h, 2 * width)].reshape(clip_rows, HD)
                probs = softmax(masked_scores(packed[to, :, head_at(h)], keys))
                refs.outs[turn, :, head_at(h)] = mm(probs.astype(BF16), values).astype(BF16)
            links.send_line(
                refs.outs.at[turn], refs.mixed.at[links.clip_of(links.z)], to, turn
            )
        far = gather_relay(links, refs.grads, first)
        reduce_product = rows_partial("mixed", "w")

        def partial(refs, k, store):
            links.wait_line(refs.mixed.at[k], links.clip_of(k))
            reduce_product(refs, k, store)

        reduce_slice(links, refs, partial, middle, refs.held)
        gather_slice(links, refs, refs.held, product)
        gather_end(far)
        sum_stats(links, refs)
        refs.inv[...] = lax.rsqrt(refs.stat_sum[...] / dim + EPS)

        @pl.loop(0, 4)
        def _(k):
            inverse = to_column(refs.inv[k, pl.ds(0, 1), pl.ds(0, tokens)])
            refs.unit[k] = refs.unit[k] * inverse

    second = run_kernel(
        "self_attend", 2,
        dict(
            packed=packed, w=full_out, states=states_p,
            vec=vectors(attn_bias[3], gate1, norm_gain, norm_bias),
            w2=cross_wq, bias=jnp.broadcast_to(bias[4:5], (8, width)),
            own_grads=d_ffnout,
        ),
        dict(
            mixed=((4, tokens, width), BF16), branch=wide, joined=wide, held=held, grads=held,
            unit=head_block, inv=((4, 8, 256), F32),
        ),
        body,
        dict(outs=((seqs, tokens, width), BF16), **reduce_scratch(tokens, dim)),
        stats=True, line=1,
        cost=80,
    )
    mixed, branch, after_self, g_ffn = second.mixed, second.branch, second.joined, second.grads
    x_cross, cq_unit, cq_inv = second.held, second.unit, second.inv

    ck_pre = mm(x_text, cross_wk) + bias[5]
    cross_v = (mm(x_text, cross_wv) + bias[6]).astype(BF16)
    ck_inv = rms_scale(sum4(jnp.sum(ck_pre * ck_pre, -1)))
    ck_unit = ck_pre * ck_inv
    cross_k = (ck_unit * gain[3]).astype(BF16)
    text_kv = jnp.concatenate([cross_k, cross_v], -1)

    def cross_heads(refs, k, h):
        q = (refs.unit[k, :, head_at(h)] * refs.gain[2:3, head_at(h)]).astype(BF16)
        keys = refs.kv[k, :, head_at(h)]
        values = refs.kv[k, :, head_at(h, width)]
        return q, keys, values, softmax(mm_t(q, keys) * SCALE)

    def middle(refs, rows, step, total):
        vec = refs.vec
        joined = refs.start[rows] + (total + vec[0:1])
        refs.joined[rows] = joined
        normed, _ = layer_norm(joined)
        return (normed * vec[1:2] + vec[2:3]).astype(BF16)

    root = math.sqrt(2.0 / math.pi)

    def product(refs, k, piece):
        for at, size in column_chunks(hidden_width, 640):
            columns = pl.ds(at, size)
            pre = mm(piece[...], refs.w2[:, columns]) + refs.bias[0:1, columns]
            bent = jnp.tanh(root * (pre + 0.044715 * pre * pre * pre))
            refs.hidden[k, :, columns] = (0.5 * pre * (1.0 + bent)).astype(BF16)
            refs.slope[k, :, columns] = 0.5 * (1.0 + bent) + 0.5 * pre * (
                1.0 - bent * bent
            ) * root * (1.0 + 3.0 * 0.044715 * pre * pre)

    def body(links, refs):
        reduce_product = rows_partial("mix", "w")

        def partial(refs, k, store):
            for h in range(heads):
                _, _, values, probs = cross_heads(refs, k, h)
                refs.mix[k, :, head_at(h)] = mm(probs.astype(BF16), values).astype(BF16)
            reduce_product(refs, k, store)

        reduce_slice(links, refs, partial, middle, refs.held)
        gather_slice(links, refs, refs.held, product)

    third = run_kernel(
        "cross_attend", 3,
        dict(
            unit=cq_unit, gain=gains8, kv=text_kv,
            w=full_crossout, start=after_self,
            vec=vectors(attn_bias[7], 1.0 + scale2, shift2),
            w2=full_up,
            bias=jnp.broadcast_to(pick(up_bias)[None], (8, hidden_width)),
        ),
        dict(
            mix=((4, tokens, width), BF16), joined=wide, held=held,
            hidden=((4, tokens, hidden_width), BF16),
            slope=((4, tokens, hidden_width), F32),
        ),
        body, reduce_scratch(tokens, dim),
        cost=60,
    )
    cross_mix, after_cross, x_ffn, hidden = third.mix, third.joined, third.held, third.hidden

    down_core = row_core(outer(hidden, g_ffn))
    down_part = scatter_z(down_core)
    inner_partial = turned_partial("d_hpre", "w_up")

    def ffn_partial(refs, k, store):
        w = refs.w_down
        deep = w.shape[2]
        for at, size in column_chunks(hidden_width, 640):
            columns = pl.ds(at, size)
            grad = mm_t(refs.g[k, :, pl.ds(0, deep)], w[0, columns])
            grad = grad + mm_t(refs.g[k, :, pl.ds(deep, deep)], w[1, columns])
            refs.d_hpre[k, :, columns] = (grad * refs.slope[k, :, columns]).astype(BF16)
        inner_partial(refs, k, store)

    def middle(refs, rows, step, total):
        normed, inverse = layer_norm(refs.joined[rows])
        d_cross = refs.top[rows] + norm_backward(normed, inverse, total * refs.vec[0:1])
        refs.d_cross[rows] = d_cross
        low = d_cross.astype(BF16)
        add_rows(refs.sums, 0, total, step)
        add_rows(refs.sums, 1, total * normed, step)
        add_rows(refs.sums, 2, low.astype(F32), step)
        return low

    def product(refs, k, piece):
        refs.d_mix[k] = rows_turned(piece, refs.w2).astype(BF16)

    def body(links, refs):
        reduce_slice(links, refs, ffn_partial, middle, refs.held)
        gather_slice(links, refs, refs.held, product)

    fourth = run_kernel(
        "ffn_back", 4,
        dict(
            g=after(g_ffn, down_core), w_down=full_down, slope=third.slope, w_up=full_up,
            joined=after_cross, top=out_grad_p, vec=vectors(1.0 + scale2),
            w2=full_crossout,
        ),
        dict(
            d_hpre=((4, tokens, hidden_width), BF16), d_cross=wide, held=held,
            d_mix=((4, tokens, width), BF16), sums=((3, 8, dim), F32),
        ),
        body, reduce_scratch(tokens, dim),
        cost=72,
    )
    d_hpre, d_cross, g_cross, d_cmix = fourth.d_hpre, fourth.d_cross, fourth.held, fourth.d_mix
    sums4 = jnp.sum(fourth.sums, 1)
    up_core = column_core(outer(x_ffn, d_hpre))
    up_part = scatter_z(up_core)

    def rms_back(grad, unit, inverse, mean):
        return inverse * (grad - unit * mean)

    def middle(refs, rows, step, total):
        normed, inverse = layer_norm(refs.joined[rows])
        vec = refs.vec
        d_self = refs.top[rows] + norm_backward(normed, inverse, total * vec[0:1])
        refs.d_self[rows] = d_self
        low = (d_self * vec[1:2]).astype(BF16)
        add_rows(refs.sums, 0, total * normed, step)
        add_rows(refs.sums, 1, total, step)
        add_rows(refs.sums, 2, low.astype(F32), step)
        add_rows(refs.sums, 3, d_self * refs.branch[rows], step)
        return low

    def ffn_out_partial(refs, k, store):
        half_width = refs.w_down.shape[2]
        for half in range(2):
            for at, size in column_chunks(half_width, 384):
                store(
                    pl.ds(half * half_width + at, size),
                    mm(refs.hidden[k], refs.w_down[half, :, pl.ds(at, size)]),
                )

    def ffn_out_rows(refs, rows, step, total):
        ffn_out = total + refs.vec[2:3]
        refs.block_out[rows] = refs.crossed[rows] + ffn_out * refs.vec[3:4]
        add_rows(refs.sums, 4, refs.out_grad[rows] * ffn_out, step)

    def body(links, refs):
        refs.stat[...] = jnp.zeros_like(refs.stat)
        refs.gains[...] = jnp.zeros_like(refs.gains)
        ffn_buffers = (refs.ffn_mine, refs.ffn_near, refs.ffn_far, refs.ffn_total)
        copies = reduce_begin(links, refs, ffn_buffers, ffn_out_partial)
        reduce_own(refs, ffn_buffers, ffn_out_partial)

        @pl.loop(0, 4)
        def _(k):
            square = jnp.zeros((tokens, 1), F32)
            for h in range(heads):
                q, keys, values, probs = cross_heads(refs, k, h)
                d_mix = refs.d_mix[k, :, head_at(h)]
                d_probs = mm_t(d_mix, values)
                delta = jnp.sum(probs * d_probs, -1, keepdims=True)
                d_scores = (probs * (d_probs - delta)).astype(BF16)
                d_q = mm(d_scores, keys) * SCALE
                refs.d_kv[k, :, head_at(h)] = (mm_l(d_scores, q) * SCALE).astype(BF16)
                refs.d_kv[k, :, head_at(h, width)] = mm_l(probs.astype(BF16), d_mix).astype(BF16)
                unit = refs.unit[k, :, head_at(h)]
                refs.gains[:, head_at(h)] += fold_rows(d_q * unit)
                d_q = d_q * refs.gain[2:3, head_at(h)]
                refs.d_unit[k, :, head_at(h)] = d_q
                square = square + jnp.sum(d_q * unit, -1, keepdims=True)
            refs.stat[k, pl.ds(0, 1), pl.ds(0, tokens)] = to_row(square)

        sum_stats(links, refs)
        copies = reduce_relay(links, ffn_buffers, copies)

        @pl.loop(0, 4)
        def _(k):
            inverse = to_column(refs.inv[k, pl.ds(0, 1), pl.ds(0, tokens)])
            mean = to_column(refs.stat_sum[k, pl.ds(0, 1), pl.ds(0, tokens)]) / dim
            refs.d_pre[k] = rms_back(refs.d_unit[k], refs.unit[k], inverse, mean).astype(BF16)

        def product(refs, k, piece):
            refs.outs[k] = rows_turned(piece, refs.w2).astype(BF16)
            links.send_line(
                refs.outs.at[k], refs.d_heads.at[links.z], links.clip_of(k), k
            )

        reduce_slice(links, refs, turned_partial("d_pre", "w"), middle, refs.held)
        gather_slice(links, refs, refs.held, product)
        reduce_end(refs, ffn_buffers, copies, ffn_out_rows)
        for source in range(seqs):
            links.wait_line(refs.d_heads.at[source], source)

    fifth = run_kernel(
        "cross_back", 5,
        dict(
            unit=cq_unit, inv=cq_inv, gain=gains8, kv=text_kv,
            d_mix=after(d_cmix, up_core, down_part),
            w=cross_wq, joined=after_self, top=d_cross, branch=branch,
            vec=vectors(norm_gain, gate1, down_bias, gate2), w2=full_out,
            hidden=hidden, w_down=full_down, crossed=after_cross, out_grad=out_grad_p,
        ),
        dict(
            d_pre=((4, tokens, width), BF16), d_kv=((4, texts, 2 * width), BF16),
            gains=((8, width), F32), d_self=wide, held=held,
            d_heads=((seqs, tokens, width), BF16), sums=((5, 8, dim), F32), block_out=wide,
        ),
        body,
        dict(
            d_unit=((4, tokens, width), F32), outs=((4, tokens, width), BF16),
            **reduce_scratch(tokens, dim),
            **{"ffn_" + n: v for n, v in reduce_scratch(tokens, dim).items()},
        ),
        stats=True, line=1,
        cost=80,
    )
    d_cq, d_self, g_self, d_heads = fifth.d_pre, fifth.d_self, fifth.held, fifth.d_heads
    cq_gain = jnp.sum(fifth.gains, 0)
    sums5 = jnp.sum(fifth.sums, 1)
    d_kv, mixed, cross_mix = after((fifth.d_kv, mixed, cross_mix), up_part)
    outproj_core = row_core(outer(mixed, g_self))
    crossout_core = row_core(outer(cross_mix, g_cross))
    d_kv = d_kv.reshape(4, seqs, -1, 2 * width).transpose(1, 0, 2, 3)
    parts = [d_kv.reshape(seqs, -1, 2 * width)]
    parts += [v.reshape(seqs, -1, 2 * width) for v in (outproj_core, crossout_core)]
    joint_core = jnp.concatenate(parts, 1)
    joint_part = lax.psum_scatter(joint_core, "z", scatter_dimension=0, tiled=True)[0]

    def middle(refs, rows, step, total):
        normed, inverse = layer_norm(refs.states[rows])
        refs.out[rows] = refs.top[rows] + norm_backward(
            normed, inverse, total * refs.vec[0:1]
        )
        add_rows(refs.sums, 0, total, step)
        add_rows(refs.sums, 1, total * normed, step)

    def body(links, refs):
        refs.stat[...] = jnp.zeros_like(refs.stat)
        refs.gains[...] = jnp.zeros_like(refs.gains)
        packed, d_heads = refs.packed, refs.d_heads
        x, y, core = links.x, links.y, lax.axis_index("core")
        refs.ups[y, x] = refs.up_part[y]
        refs.downs[x] = refs.down_part[...]
        over_y = links.send("y", refs.up_part.at[1 - y], refs.ups.at[y, x])
        over_x = [
            links.send("x", refs.up_part.at[y], refs.ups.at[y, x]),
            links.send("x", refs.down_part, refs.downs.at[x]),
        ]
        for h in range(heads):
            refs.d_keys[...] = jnp.zeros_like(refs.d_keys)
            refs.d_values[...] = jnp.zeros_like(refs.d_values)

            @pl.loop(0, seqs)
            def _(i):
                keys = packed[:, :, head_at(h, width)].reshape(clip_rows, HD)
                values = packed[:, :, head_at(h, 2 * width)].reshape(clip_rows, HD)
                q = packed[i, :, head_at(h)]
                d_mix = d_heads[i, :, head_at(h)]
                probs = softmax(masked_scores(q, keys))
                d_probs = mm_t(d_mix, values)
                delta = jnp.sum(probs * d_probs, -1, keepdims=True)
                d_scores = (probs * (d_probs - delta)).astype(BF16)
                refs.outs[h, i, :, pl.ds(0, HD)] = (mm(d_scores, keys) * SCALE).astype(BF16)
                refs.d_keys[...] += mm_l(d_scores, q)
                refs.d_values[...] += mm_l(probs.astype(BF16), d_mix)

            for i in range(seqs):
                rows = pl.ds(i * tokens, tokens)
                refs.outs[h, i, :, pl.ds(HD, HD)] = (refs.d_keys[rows] * SCALE).astype(BF16)
                refs.outs[h, i, :, pl.ds(2 * HD, HD)] = refs.d_values[rows].astype(BF16)
            for step in range(seqs):
                to = (links.z + 1 + step) % seqs
                links.send_line(
                    refs.outs.at[h, to],
                    refs.arrived.at[h, links.clip_of(links.z)],
                    to, step, h,
                )
            if h == 0:
                over_y.wait_recv()
                over_x.append(links.send("x", refs.ups.at[1 - y, x], refs.ups.at[1 - y, x]))
            if h == 1:
                over_x[1].wait_recv()
                over_core = links.send(("core",), refs.downs.at[1 - core], refs.columns)

        for copy in (over_x[0], over_x[2], over_core):
            copy.wait_recv()
        for block in range(4):
            refs.up_grad[:, pl.ds(block * hidden_width, hidden_width)] = refs.ups[
                block // 2, block % 2
            ].astype(F32)
        half = refs.columns.shape[1]
        for part, value in ((core, refs.downs.at[core]), (1 - core, refs.columns)):
            at = pl.ds(pl.multiple_of(part * half, half), half)
            refs.down_grad[:, at] = value[...].astype(F32)
        for k in range(4):
            for h in range(heads):
                links.wait_line(refs.arrived.at[h, k], links.clip_of(k), h)

        @pl.loop(0, 4)
        def _(k):
            for part in range(2):
                square = jnp.zeros((tokens, 1), F32)
                for h in range(heads):
                    at = head_at(h, part * width)
                    grad = refs.arrived[h, k, :, pl.ds(part * HD, HD)].astype(F32)
                    grad = grad * refs.tables[k, :, pl.ds(0, HD)] - swap_pairs(grad) * refs.tables[k, :, pl.ds(HD, HD)]
                    unit = refs.unit[k, :, at]
                    refs.gains[part, :, head_at(h)] += fold_rows(grad * unit)
                    grad = grad * refs.gain[pl.ds(part, 1), head_at(h)]
                    refs.d_unit[k, :, at] = grad
                    square = square + jnp.sum(grad * unit, -1, keepdims=True)
                refs.stat[k, pl.ds(part, 1), pl.ds(0, tokens)] = to_row(square)
            for h in range(heads):
                refs.d_qkv[k, :, head_at(h, 2 * width)] = refs.arrived[
                    h, k, :, pl.ds(2 * HD, HD)
                ]

        sum_stats(links, refs)

        @pl.loop(0, 4)
        def _(k):
            for part in range(2):
                row = (k, pl.ds(part, 1), pl.ds(0, tokens))
                inverse = to_column(refs.inv[row])
                mean = to_column(refs.stat_sum[row]) / dim
                at = pl.ds(part * width, width)
                refs.d_qkv[k, :, at] = rms_back(
                    refs.d_unit[k, :, at], refs.unit[k, :, at], inverse, mean
                ).astype(BF16)

        reduce_slice(links, refs, turned_partial("d_qkv", "w"), middle)

    sixth = run_kernel(
        "self_back", 6,
        dict(
            packed=packed, d_heads=d_heads, unit=self_unit, inv=self_inv,
            gain=gains8, tables=tables, w=full_qkv, states=states_p,
            top=after(d_self, joint_core), vec=vectors(1.0 + scale1),
            up_part=up_part.reshape(2, -1, hidden_width), down_part=down_part,
        ),
        dict(
            d_qkv=((4, tokens, blocks3), BF16), gains=((2, 8, width), F32),
            out=wide, sums=((2, 8, dim), F32),
            up_grad=((up_part.shape[0] // 2, 4 * hidden_width), F32),
            down_grad=((down_part.shape[0], dim), F32),
        ),
        body,
        dict(
            outs=((heads, seqs, tokens, 3 * HD), BF16),
            arrived=((heads, 4, tokens, 3 * HD), BF16),
            d_keys=((clip_rows, HD), F32), d_values=((clip_rows, HD), F32),
            d_unit=((4, tokens, 2 * width), F32),
            ups=((2, 2, up_part.shape[0] // 2, hidden_width), BF16),
            downs=((2,) + down_part.shape, BF16), columns=(down_part.shape, BF16),
            **reduce_scratch(tokens, dim),
        ),
        stats=True, line=heads, pair=True,
        cost=120,
    )
    d_qkv = tied(sixth.d_qkv, joint_part)
    d_hpre, d_cq = after((d_hpre, d_cq), d_qkv)
    text_rows, weight_rows = parts[0].shape[1], parts[1].shape[1]
    d_ckv = joint_part[:text_rows].reshape(4, -1, 2 * width)
    outproj_part = over_reps(joint_part[text_rows : text_rows + weight_rows])
    crossout_part = over_reps(joint_part[text_rows + weight_rows :])
    d_qkv_sum = jnp.sum(d_qkv.astype(F32), (0, 1))
    q_gain, k_gain = jnp.sum(sixth.gains, 1)
    states_grad = sixth.out[:own_tokens]
    sums6 = jnp.sum(sixth.sums, 1)
    qkv_core = column_core(outer(x_self, d_qkv))
    qkv_part = scatter_z(qkv_core)

    d_ckn = d_ckv[..., :width].astype(F32)
    d_cv = d_ckv[..., width:]
    zpos = lax.axis_index("z")
    own = texts // seqs
    ck_unit = lax.dynamic_slice_in_dim(ck_unit, zpos * own, own, 1)
    ck_inv = lax.dynamic_slice_in_dim(ck_inv, zpos * own, own, 1)
    x_text = lax.dynamic_slice_in_dim(x_text, zpos * own, own, 1)
    d_cku = d_ckn * gain[3]
    ck_stat = sum4(jnp.sum(d_cku * ck_unit, -1)) / dim
    d_ck = rms_back(d_cku, ck_unit, ck_inv, ck_stat[..., None]).astype(BF16)
    ck_gain = jnp.sum(d_ckn * ck_unit, (0, 1))
    d_text = jnp.concatenate([d_ck, d_cv], -1)
    text_grad = reduce4(lambda k: mm_t(d_ck[k], cross_wk) + mm_t(d_cv[k], cross_wv))
    cross_core = column_core(jnp.concatenate([outer(x_cross, d_cq), outer(x_text, d_text)], 1))
    cross_part = scatter_z(cross_core)

    block_out = fifth.block_out[:own_tokens]
    up_grad, down_grad = sixth.up_grad, sixth.down_grad
    qkv_grad = column_done(qkv_part, 3)
    outproj_grad = row_done(outproj_part)
    cross_grad = column_done(cross_part, 3)
    crossout_grad = row_done(crossout_part)

    def column_sum(v):
        return jnp.sum(v.astype(F32), tuple(range(v.ndim - 1)))

    early = jnp.stack(
        [
            sums4[0],
            sums4[1],
            sums5[4],
            spread(column_sum(d_cq)),
            spread(column_sum(d_ck)),
            spread(column_sum(d_cv)),
            sums4[2],
            spread(cq_gain),
            spread(ck_gain),
            sums5[0],
            sums5[1],
            column_sum(d_ffnout),
            sums5[2],
            sums5[3],
        ]
    )
    late = jnp.stack(
        [
            sums6[0],
            sums6[1],
            spread(d_qkv_sum[:width]),
            spread(d_qkv_sum[width : 2 * width]),
            spread(d_qkv_sum[2 * width :]),
            spread(q_gain),
            spread(k_gain),
        ]
    )
    upbias_rows = jnp.pad(spread(column_sum(d_hpre)), (0, -4 * hidden_width % dim)).reshape(-1, dim)
    counts = early.shape[0], late.shape[0], upbias_rows.shape[0]
    rows = -(-sum(counts) // 8) * 8
    small = jnp.concatenate([early, late, upbias_rows])
    small = jnp.pad(small, ((0, rows - sum(counts)), (0, 0)))

    def body(links, refs):
        refs.stages[0] = refs.small[...]
        flip = links.z + 1 - 2 * (links.z % 2)
        hops = [
            {"z": flip}, {"z": (links.z + seqs // 2) % seqs},
            {"core": 1 - lax.axis_index("core")}, {"x": 1 - links.x}, {"y": 1 - links.y},
        ]
        for step, where in enumerate(hops):
            copy = links.send_to(where, refs.stages.at[step], refs.others.at[step])
            copy.wait_recv()
            refs.stages[step + 1] = refs.stages[step] + refs.others[step]
        refs.clip[...] = refs.stages[2]
        refs.all[...] = refs.stages[5]

    shape = ((rows, dim), F32)
    summed = run_kernel(
        "small_sums", 8, dict(small=after(small, cross_core)), dict(clip=shape, all=shape),
        body, dict(stages=((6, rows, dim), F32), others=((5, rows, dim), F32)),
        line=1, pair=True, cost=25,
    )
    total = over_reps(summed.all)
    early_clip, late_clip = summed.clip[: counts[0]], summed.clip[counts[0] :]
    early_all, late_all = total[: counts[0]], total[counts[0] :]
    upbias = total[counts[0] + counts[1] : sum(counts)].reshape(-1)[: 4 * hidden_width]

    def mod_rows(e, l):
        return jnp.stack([l[0], l[1], e[13], e[0], e[1], e[2]])

    time_grad = mod_rows(early_clip, late_clip)[None]
    mod_grad = mod_rows(early_all, late_all)
    bias_grad = jnp.stack(
        [late_all[2], late_all[3], late_all[4], early_all[12]] + [early_all[i] for i in (3, 4, 5, 6)]
    )
    gain_grad = jnp.stack([late_all[5], late_all[6], early_all[7], early_all[8]])
    return (
        block_out, states_grad, text_grad, time_grad, qkv_grad, outproj_grad, cross_grad,
        crossout_grad, up_grad, down_grad, bias_grad, gain_grad, early_all[9], early_all[10],
        upbias, early_all[11], mod_grad,
    )


def solution(mesh):
    reps, shards, seqs = mesh.shape["replica"], mesh.shape["shard"], mesh.shape["seq"]
    fine = Mesh(
        mesh.devices.reshape(reps // 2, 2, shards // 2, 2, seqs), ("rep", "x", "y", "core", "z")
    )
    tokens = P(("rep", "x", "y", "core", "z"), None)
    clips = P(("rep", "x", "y", "core"), None, None)
    rows2 = P(("y", "core", "z"), None)
    rows3 = P(("y", "core", "z"), None, None)
    return jax.shard_map(
        on_device,
        mesh=fine,
        in_specs=(
            tokens, tokens, P(None, ("rep", "x", "y", "core", "z")), clips,
            rows3, rows2, rows3, rows2, rows2, rows2,
            P(), P(), P(), P(), P(), P(), P(), tokens,
        ),
        out_specs=(
            tokens, tokens, tokens, clips,
            rows3, rows2, rows3, rows2, rows2, rows2,
            P(), P(), P(), P(), P(), P(), P(),
        ),
        check_vma=False,
    )
```

```python
import math
from types import SimpleNamespace

import jax
import jax.numpy as jnp
import numpy as np
from jax import lax
from jax.experimental import pallas as pl
from jax.experimental.pallas import tpu as pltpu
from jax.sharding import Mesh, PartitionSpec as P

HD = 128
EPS = 1e-06
F32 = jnp.float32
BF16 = jnp.bfloat16
SCALE = 1.0 / math.sqrt(HD)
SWAP = [(0, 1), (1, 0)]
ROWS = 16
FLOPS = 1_150_000_000
BYTES = 3_600_000


def rope_tables(grid_pos):
    pairs = HD // 2
    width = pairs // 3
    first = pairs - 2 * width
    index = np.arange(pairs)
    part = np.where(index < first, 0, np.where(index < first + width, 1, 2))
    offset = np.where(part == 0, index, np.where(part == 1, index - first, index - first - width))
    frequency = 10000.0 ** (-offset / np.where(part == 0, first, width))
    position = grid_pos.astype(F32)
    angles = 0.0
    for axis in range(3):
        lane = np.repeat(frequency * (part == axis), 2)
        angles = angles + position[axis][:, None] * jnp.asarray(lane, F32)[None, :]
    sign = np.where(np.arange(HD) % 2 == 0, -1.0, 1.0)
    return jnp.cos(angles), jnp.sin(angles) * jnp.asarray(sign, F32)[None, :]


def layer_norm(values):
    center = values - jnp.mean(values, -1, keepdims=True)
    inverse = lax.rsqrt(jnp.mean(center * center, -1, keepdims=True) + EPS)
    return center * inverse, inverse


def norm_backward(normed, inverse, grad_in):
    return inverse * (
        grad_in
        - jnp.mean(grad_in, -1, keepdims=True)
        - normed * jnp.mean(grad_in * normed, -1, keepdims=True)
    )


def mm(a, b):
    return lax.dot_general(a, b, (((a.ndim - 1,), (0,)), ((), ())), preferred_element_type=F32)


def mm_t(a, b):
    return lax.dot_general(a, b, (((a.ndim - 1,), (1,)), ((), ())), preferred_element_type=F32)


def rows_mm(a, w):
    return jnp.concatenate([mm(a, w[0]), mm(a, w[1])], -1)


def after(value, *done):
    return lax.optimization_barrier((value, done))[0]


def tied(value, done):
    anywhere = pl.BlockSpec(memory_space=pl.ANY)
    return pl.pallas_call(
        lambda *refs: None,
        name="tied",
        out_shape=jax.ShapeDtypeStruct(value.shape, value.dtype),
        in_specs=[anywhere] * 2,
        out_specs=anywhere,
        input_output_aliases={0: 0},
    )(value, done)


def outer(a, b):
    lead = tuple(range(a.ndim - 1))
    return lax.dot_general(a, b, ((lead, lead), ((), ())), preferred_element_type=F32)


def column_chunks(total, size):
    return [(at, min(size, total - at)) for at in range(0, total, size)]


class Links:
    def __init__(self, named, stats, line, pair, near):
        self.named = named
        self.used = 0
        self.started = []
        self.x, self.y, self.z = [lax.axis_index(n) for n in ("x", "y", "z")]
        self.seqs = lax.axis_size("z")
        barrier = pltpu.get_barrier_semaphore()
        peers = [{"x": 1 - self.x}, {"y": 1 - self.y}] if near else []
        if stats:
            peers.append({"x": 1 - self.x, "y": 1 - self.y})
        if pair:
            peers.append({"core": 1 - lax.axis_index("core")})
        if line:
            peers += [{"z": (self.z + step) % self.seqs} for step in range(1, self.seqs)]
        for peer in peers:
            pl.semaphore_signal(
                barrier, inc=1, device_id=peer, device_id_type=pl.DeviceIdType.MESH
            )
        pl.semaphore_wait(barrier, len(peers))

    def clip_of(self, piece):
        return ((piece // 2 + self.x) % 2) * 2 + (piece % 2 + self.y) % 2

    def send(self, axis, src, dst):
        return self.send_to({a: 1 - lax.axis_index(a) for a in axis}, src, dst)

    def send_to(self, where, src, dst):
        index = self.used
        self.used += 1
        sems = self.named.sems
        copy = pltpu.make_async_remote_copy(
            src_ref=src,
            dst_ref=dst,
            send_sem=sems.at[0, index],
            recv_sem=sems.at[1, index],
            device_id=where,
            device_id_type=pl.DeviceIdType.MESH,
        )
        copy.start()
        self.started.append((None, copy))
        return copy

    def send_line(self, src, dst, to, slot, lane=0):
        sems = self.named.line
        copy = pltpu.make_async_remote_copy(
            src_ref=src,
            dst_ref=dst,
            send_sem=sems.at[0, lane, slot],
            recv_sem=sems.at[1, lane, self.z],
            device_id={"z": to},
            device_id_type=pl.DeviceIdType.MESH,
        )

        @pl.when(to != self.z)
        def _():
            copy.start()

        @pl.when(to == self.z)
        def _():
            dst[...] = src[...]

        self.started.append((to != self.z, copy))

    def wait_line(self, ref, source, lane=0):
        sems = self.named.line
        copy = pltpu.make_async_remote_copy(
            src_ref=ref,
            dst_ref=ref,
            send_sem=sems.at[0, lane, 0],
            recv_sem=sems.at[1, lane, source],
            device_id={"z": (self.z + 1) % self.seqs},
            device_id_type=pl.DeviceIdType.MESH,
        )

        @pl.when(source != self.z)
        def _():
            copy.wait_recv()

    def finish(self):
        for needed, copy in self.started:
            if needed is None:
                copy.wait_send()
            else:
                pl.when(needed)(copy.wait_send)


def split_rows(tokens):
    return ((tokens // 2 + ROWS - 1) // ROWS) * ROWS


def row_steps(tokens, body):
    @pl.loop(0, tokens // ROWS)
    def _(step):
        body(pl.ds(pl.multiple_of(step * ROWS, ROWS), ROWS), step)


def reduce_begin(links, refs, buffers, partial):
    mine, near, far, total = buffers
    tokens = total.shape[0]
    half = split_rows(tokens)
    top, low = pl.ds(0, half), pl.ds(half, tokens - half)

    def store_low(slot):
        def store(columns, value):
            mine[slot, :, columns] = value.astype(BF16)

        return store

    partial(refs, 3, store_low(2))
    far_x = links.send("x", mine.at[2, top], far.at[top])
    far_y = links.send("y", mine.at[2, low], far.at[low])
    partial(refs, 2, store_low(1))
    x_top = links.send("x", mine.at[1, top], near.at[1, top])
    partial(refs, 1, store_low(0))
    y_low = links.send("y", mine.at[0, low], near.at[0, low])
    return far_x, far_y, x_top, y_low


def reduce_relay(links, buffers, copies):
    mine, near, far, total = buffers
    tokens = total.shape[0]
    half = split_rows(tokens)
    top, low = pl.ds(0, half), pl.ds(half, tokens - half)
    far_x, far_y, x_top, y_low = copies
    far_x.wait_recv()
    mine[0, top] = (mine[0, top].astype(F32) + far[top].astype(F32)).astype(BF16)
    y_top = links.send("y", mine.at[0, top], near.at[0, top])
    far_y.wait_recv()
    mine[1, low] = (mine[1, low].astype(F32) + far[low].astype(F32)).astype(BF16)
    x_low = links.send("x", mine.at[1, low], near.at[1, low])
    return x_top, y_low, y_top, x_low


def reduce_own(refs, buffers, partial):
    total = buffers[3]

    def store_full(columns, value):
        total[:, columns] = value

    partial(refs, 0, store_full)


def reduce_end(refs, buffers, copies, middle, keep=None):
    mine, near, far, total = buffers
    for copy in copies:
        copy.wait_recv()

    def body(rows, step):
        value = total[rows] + near[0, rows].astype(F32) + near[1, rows].astype(F32)
        sent = middle(refs, rows, step, value)
        if keep is not None:
            keep[0, rows] = sent

    row_steps(total.shape[0], body)


def reduce_slice(links, refs, partial, middle, keep=None):
    buffers = (refs.mine, refs.near, refs.far, refs.total)
    copies = reduce_begin(links, refs, buffers, partial)
    copies = reduce_relay(links, buffers, copies)
    reduce_own(refs, buffers, partial)
    reduce_end(refs, buffers, copies, middle, keep)


def gather_begin(links, held):
    return links.send("x", held.at[0], held.at[2]), links.send("y", held.at[0], held.at[1])


def gather_relay(links, held, first):
    tokens = held.shape[1]
    half = split_rows(tokens)
    top, low = pl.ds(0, half), pl.ds(half, tokens - half)
    from_x, from_y = first
    from_x.wait_recv()
    far_top = links.send("y", held.at[2, top], held.at[3, top])
    from_y.wait_recv()
    far_low = links.send("x", held.at[1, low], held.at[3, low])
    return far_top, far_low


def gather_end(far):
    for copy in far:
        copy.wait_recv()


def gather_slice(links, refs, held, product, also=()):
    arrays = (held,) + tuple(also)
    first = [gather_begin(links, array) for array in arrays]
    product(refs, 0, held.at[0])
    far = [gather_relay(links, array, copies) for array, copies in zip(arrays, first)]
    product(refs, 1, held.at[1])
    product(refs, 2, held.at[2])
    for copies in far:
        gather_end(copies)
    product(refs, 3, held.at[3])


def sum_stats(links, refs):
    stat, other = refs.stat, refs.stats_in
    copies = [
        links.send("y", stat, other.at[0]),
        links.send("x", stat, other.at[1]),
        links.send("xy", stat, other.at[2]),
    ]
    for copy in copies:
        copy.wait_recv()
    for copy in copies:
        copy.wait_send()
    del links.started[-3:]
    for k in range(4):
        refs.stat_sum[k] = (
            stat[k] + other[0, k ^ 1] + other[1, k ^ 2] + other[2, k ^ 3]
        )


def to_row(column):
    size = column.shape[0]
    same = lax.broadcasted_iota(jnp.int32, (size, size), 0) == lax.broadcasted_iota(
        jnp.int32, (size, size), 1
    )
    return jnp.sum(jnp.where(same, column, 0.0), 0, keepdims=True)


def to_column(row):
    size = row.shape[1]
    same = lax.broadcasted_iota(jnp.int32, (size, size), 0) == lax.broadcasted_iota(
        jnp.int32, (size, size), 1
    )
    return jnp.sum(jnp.where(same, row, 0.0), 1, keepdims=True)


def run_kernel(name, cid, inputs, outputs, body, scratch, cost, stats=False, line=0, pair=False, near=True):
    names_in, names_out = list(inputs), list(outputs)
    spaces = dict(sems=pltpu.SemaphoreType.DMA((2, 24)))
    if line:
        spaces.update(line=pltpu.SemaphoreType.DMA((2, line, 4)))
    if stats:
        spaces.update(
            stat=pltpu.VMEM((4, 8, 256), F32),
            stat_sum=pltpu.VMEM((4, 8, 256), F32),
            stats_in=pltpu.VMEM((3, 4, 8, 256), F32),
        )
    for key, (shape, dtype) in scratch.items():
        spaces[key] = pltpu.VMEM(shape, dtype)

    def kernel(*refs):
        named = SimpleNamespace(**dict(zip(names_in + names_out + list(spaces), refs)))
        links = Links(named, stats, line, pair, near)
        body(links, named)
        links.finish()

    vmem = pl.BlockSpec(memory_space=pltpu.VMEM)
    result = pl.pallas_call(
        kernel,
        name=name,
        out_shape=[jax.ShapeDtypeStruct(*outputs[n]) for n in names_out],
        in_specs=[vmem] * len(names_in),
        out_specs=[vmem] * len(names_out),
        scratch_shapes=list(spaces.values()),
        cost_estimate=pl.CostEstimate(
            flops=cost * FLOPS, bytes_accessed=cost * BYTES, transcendentals=0
        ),
        compiler_params=pltpu.CompilerParams(
            collective_id=cid, has_side_effects=True, vmem_limit_bytes=60 * 1024 * 1024
        ),
    )(*[inputs[n] for n in names_in])
    return SimpleNamespace(**dict(zip(names_out, result)))


def reduce_scratch(tokens, dim):
    return dict(
        mine=((3, tokens, dim), BF16),
        near=((2, tokens, dim), BF16),
        far=((tokens, dim), BF16),
        total=((tokens, dim), F32),
    )


def add_rows(ref, index, value, step):
    @pl.when(step == 0)
    def _():
        ref[index] = jnp.zeros_like(ref[index])

    ref[index] += value[:8] + value[8:]


def fold_rows(value):
    return jnp.sum(value.reshape(value.shape[0] // 8, 8, value.shape[1]), 0)


def rows_partial(a, w):
    def partial(refs, k, store):
        piece = getattr(refs, a)[k]
        blocks = getattr(refs, w)
        deep, width = piece.shape[1], blocks.shape[2]
        for half in range(2):
            for part in range(2):
                store(
                    pl.ds((half * 2 + part) * width, width),
                    mm(piece, blocks[part, pl.ds(half * deep, deep), :]),
                )

    return partial


def turned_partial(a, w, size=256):
    def partial(refs, k, store):
        deep = getattr(refs, a).shape[2]

        @pl.loop(0, getattr(refs, w).shape[0] // size)
        def _(step):
            rows = pl.ds(pl.multiple_of(step * size, size), size)
            store(rows, mm_t(getattr(refs, a)[k], getattr(refs, w)[rows, pl.ds(0, deep)]))

    return partial


def rows_turned(piece, w):
    deep, width = w.shape[1] // 2, w.shape[2]
    total = 0.0
    for half in range(2):
        for part in range(2):
            columns = pl.ds((half * 2 + part) * width, width)
            total = total + mm_t(piece[:, columns], w[part, pl.ds(half * deep, deep), :])
    return total


def mm_l(a, b):
    return lax.dot_general(a, b, (((0,), (0,)), ((), ())), preferred_element_type=F32)


def swap_pairs(values):
    even = lax.broadcasted_iota(jnp.int32, values.shape, 1) % 2 == 0
    return jnp.where(even, pltpu.roll(values, HD - 1, 1), pltpu.roll(values, 1, 1))


def softmax(scores):
    weight = jnp.exp(scores - jnp.max(scores, -1, keepdims=True))
    return weight * (1.0 / jnp.sum(weight, -1, keepdims=True))


def head_at(h, base=0):
    return pl.ds(base + h * HD, HD)


def column_terms(a, b, c, seqs, at, store):
    tall, quarter = a.shape[0] * a.shape[1], a.shape[2] // 4
    rows = quarter // seqs
    for part in range(2):
        lanes = pl.ds(pl.multiple_of((part * 2 + c) * quarter, HD), quarter)
        left = a[:, :, lanes].reshape(tall, quarter)
        for column, size in column_chunks(b.shape[2], 640):
            value = mm_l(left, b[:, :, pl.ds(column, size)].reshape(tall, size))
            for z in range(seqs):
                store(
                    (z, part, slice(None), pl.ds(at + column, size)),
                    value[z * rows : (z + 1) * rows],
                )


def row_terms(a, b, c, store):
    tall, half = a.shape[0] * a.shape[1], b.shape[2] // 2
    right = b[:, :, pl.ds(pl.multiple_of(c * half, HD), half)].reshape(tall, half)
    for row, size in column_chunks(a.shape[2], 640):
        value = mm_l(a[:, :, pl.ds(row, size)].reshape(tall, size), right)
        store((pl.ds(row, size), slice(None)), value)


def weight_sums(name, cid, shapes, jobs, seqs, cost):
    inputs, outputs, scratch = {}, {}, {}
    for index, (out, left, right, column) in enumerate(jobs):
        inputs[f"a{index}"], inputs[f"b{index}"] = left, right
    for index, shape in enumerate(shapes):
        outputs[f"out{index}"] = (shape, BF16)
        scratch[f"mine{index}"] = scratch[f"theirs{index}"] = (shape, BF16)

    def body(links, refs):
        core = lax.axis_index("core")

        def terms(c, out, store):
            for index, (into, _, _, column) in enumerate(jobs):
                if into != out:
                    continue
                a, b = getattr(refs, f"a{index}"), getattr(refs, f"b{index}")
                if column is None:
                    row_terms(a, b, c, store)
                else:
                    column_terms(a, b, c, seqs, column, store)

        copies = []
        for out in range(len(shapes)):
            mine, theirs = getattr(refs, f"mine{out}"), getattr(refs, f"theirs{out}")

            def store_mine(at, value):
                mine[at] = value.astype(BF16)

            terms(1 - core, out, store_mine)
            copies.append(links.send(("core",), mine, theirs))
        for out in range(len(shapes)):
            result, theirs = getattr(refs, f"out{out}"), getattr(refs, f"theirs{out}")

            def store_result(at, value):
                result[at] = value.astype(BF16)

            terms(core, out, store_result)
            copies[out].wait_recv()
            result[...] = (result[...].astype(F32) + theirs[...].astype(F32)).astype(BF16)

    done = run_kernel(name, cid, inputs, outputs, body, scratch, cost=cost, pair=True, near=False)
    return [getattr(done, f"out{index}") for index in range(len(shapes))]


def on_device(
    states, text_emb, grid_pos, time_mod, w_qkv, w_out, w_cross, w_crossout, w_up, w_down,
    attn_bias, qk_gain, norm_gain, norm_bias, up_bias, down_bias, modulation, out_grad,
):
    x, y, core = lax.axis_index("x"), lax.axis_index("y"), lax.axis_index("core")
    seqs = lax.axis_size("z")
    reps = lax.axis_size("rep")
    own_tokens, dim = states.shape
    tokens = -(-own_tokens // ROWS) * ROWS
    block = y * 2 + x
    pad = ((0, tokens - own_tokens), (0, 0))
    states_p = jnp.pad(states, pad)
    out_grad_p = jnp.pad(out_grad, pad)

    def from_y(a):
        return lax.ppermute(a, "y", SWAP)

    def from_x(a):
        return lax.ppermute(a, "x", SWAP)

    def from_xy(a):
        return lax.ppermute(a, ("x", "y"), [(i, 3 - i) for i in range(4)])

    def from_core(a):
        return lax.ppermute(a, "core", SWAP)

    def gather4(a):
        far, xs, ys = from_xy(a), from_x(a), from_y(a)
        return jnp.stack([a, ys, xs, far])

    def reduce4(term):
        far = from_xy(term(3).astype(BF16))
        xs = from_x(term(2).astype(BF16))
        ys = from_y(term(1).astype(BF16))
        return term(0) + ys.astype(F32) + xs.astype(F32) + far.astype(F32)

    def sum4(stat):
        far, xs, ys = from_xy(stat), from_x(stat), from_y(stat)
        return (
            stat
            + jnp.stack([ys[1], ys[0], ys[3], ys[2]])
            + jnp.stack([xs[2], xs[3], xs[0], xs[1]])
            + jnp.stack([far[3], far[2], far[1], far[0]])
        )

    def pick(v, blocks=4):
        return lax.dynamic_index_in_dim(
            v.reshape(v.shape[:-1] + (blocks, v.shape[-1] // blocks)), block, v.ndim - 1, False
        )

    def spread(v):
        hot = (jnp.arange(4) == block).astype(F32)
        full = v[..., None, :] * hot[:, None]
        return full.reshape(v.shape[:-1] + (4 * v.shape[-1],))

    def column_own(w):
        rows, groups, width = w.shape[0], w.shape[1], w.shape[2] // 4
        mine = lax.dynamic_index_in_dim(w.reshape(rows, groups, 2, 2, width), x, 3, False)
        keep = lax.dynamic_index_in_dim(mine, y, 2, False).reshape(rows, groups * width)
        send = lax.dynamic_index_in_dim(mine, 1 - y, 2, False).reshape(rows, groups * width)
        recv = from_y(send)
        return jnp.where(y == 0, jnp.stack([keep, recv]), jnp.stack([recv, keep]))

    def column_block(w):
        full = lax.all_gather(column_own(w), ("core", "z"), axis=1, tiled=True)
        return full.reshape(-1, full.shape[2])

    def row_own(w):
        half = w.shape[1] // 2
        keep = lax.dynamic_slice_in_dim(w, core * half, half, 1)
        recv = from_core(lax.dynamic_slice_in_dim(w, (1 - core) * half, half, 1))
        return jnp.where(core == x, keep, recv)

    def row_block(w):
        full = lax.all_gather(row_own(w), ("core", "z"), axis=0, tiled=True)
        return full.reshape(2, -1, full.shape[1])

    def row_halves(w):
        mine = row_own(w)
        half = mine.shape[1] // 2
        return jnp.stack([mine[:, :half], mine[:, half:]])

    def attention_blocks(w_cross, w_out):
        own = column_own(w_cross)
        width = own.shape[2] // 3
        blocks = [own[:, :, g * width : (g + 1) * width] for g in range(3)]
        blocks.append(row_halves(w_out))
        return lax.all_gather(jnp.concatenate(blocks), ("core", "z"), axis=1, tiled=True)

    def up_block(w_up, w_crossout):
        own = jnp.concatenate([column_own(w_up[:, None, :]), row_halves(w_crossout)], 2)
        return lax.all_gather(own, ("core", "z"), axis=1, tiled=True)

    def over_reps(a):
        return lax.psum(a, "rep") if reps > 1 else a

    def scatter_z(a):
        return over_reps(lax.psum_scatter(a, "z", scatter_dimension=0, tiled=True))

    def column_done(part, groups):
        width = part.shape[1] // groups
        part = part.reshape(2, -1, groups * width)
        keep = lax.dynamic_index_in_dim(part, y, 0, False)
        recv = from_y(lax.dynamic_index_in_dim(part, 1 - y, 0, False))
        ours = jnp.where(y == 0, jnp.stack([keep, recv]), jnp.stack([recv, keep]))
        theirs = from_x(ours)
        rows = ours.shape[1]
        ours = ours.reshape(2, rows, groups, width)
        theirs = theirs.reshape(2, rows, groups, width)
        full = jnp.where(x == 0, jnp.stack([ours, theirs], 1), jnp.stack([theirs, ours], 1))
        return full.transpose(2, 3, 0, 1, 4).reshape(rows, groups, 4 * width).astype(F32)

    def row_done(part):
        other = from_x(part)
        ours = jnp.where(core == x, part, other)
        theirs = from_core(jnp.where(core == x, other, part))
        full = jnp.where(
            core == 0,
            jnp.concatenate([ours, theirs], 1),
            jnp.concatenate([theirs, ours], 1),
        )
        return full.astype(F32)

    mods = modulation + time_mod[0]
    shift1, scale1, gate1, shift2, scale2, gate2 = [mods[i] for i in range(6)]

    def vectors(*rows):
        return jnp.stack(rows + (jnp.zeros_like(rows[0]),) * (8 - len(rows)))

    full_qkv = column_block(w_qkv)
    text_z = lax.all_gather(text_emb, "z", axis=0, tiled=True)
    attend_w = attention_blocks(w_cross, w_out)
    cross_wq, cross_wk, cross_wv = [
        attend_w[2 * g : 2 * g + 2].reshape(dim, -1) for g in range(3)
    ]
    full_out = attend_w[6:8]
    up_w = up_block(w_up, w_crossout)
    hidden_width = w_up.shape[1] // 4
    full_crossout = up_w[:, :, hidden_width:]
    full_up = up_w.reshape(dim, -1)
    full_down = row_block(w_down)
    bias = pick(attn_bias)
    gain = pick(qk_gain)
    width = bias.shape[1]
    heads = width // HD
    own_tables = jnp.pad(jnp.concatenate(rope_tables(grid_pos), 1), pad)
    d_ffnout = (out_grad_p * gate2).astype(BF16)

    def rms_scale(v):
        return lax.rsqrt(v / dim + EPS)[..., None]

    wide = ((tokens, dim), F32)
    held = ((4, tokens, dim), BF16)
    head_block = ((4, tokens, width), F32)

    blocks3 = 3 * width
    clip_rows = seqs * tokens

    def middle(refs, rows):
        normed, _ = layer_norm(refs.states[rows])
        vec = refs.vec
        return (normed * vec[0:1] + vec[1:2]).astype(BF16)

    def body(links, refs):
        refs.stat[...] = jnp.zeros_like(refs.stat)

        def rows_in(rows, step):
            refs.held[0, rows] = middle(refs, rows)

        def send_heads(k, columns, lane):
            links.send_line(
                refs.sent.at[k, :, columns], refs.packed.at[links.z, :, columns],
                links.clip_of(k), k, lane,
            )

        early, late = pl.ds(2 * width, width), pl.ds(0, 2 * width)

        def product(refs, k, piece):
            pre = mm(piece[...], refs.w[:, early]) + refs.bias[0:1, early]
            refs.sent[k, :, early] = pre.astype(BF16)
            send_heads(k, early, 0)
            for part in range(2):
                columns = pl.ds(part * width, width)
                pre = mm(piece[...], refs.w[:, columns]) + refs.bias[0:1, columns]
                refs.unit[k, :, columns] = pre
                square = jnp.sum(pre * pre, -1, keepdims=True)
                refs.stat[k, pl.ds(part, 1), pl.ds(0, tokens)] = to_row(square)

        refs.tables[0] = refs.own_tables[...]
        refs.texts[0] = refs.text[...]
        row_steps(tokens, rows_in)
        gather_slice(links, refs, refs.held, product, (refs.tables,))
        sum_stats(links, refs)
        refs.inv[...] = lax.rsqrt(refs.stat_sum[...] / dim + EPS)
        first = gather_begin(links, refs.texts)
        for k in (3, 2, 1, 0):
            cosine, sine = refs.tables[k, :, pl.ds(0, HD)], refs.tables[k, :, pl.ds(HD, HD)]
            for part in range(2):
                inverse = to_column(refs.inv[k, pl.ds(part, 1), pl.ds(0, tokens)])
                for h in range(heads):
                    at = head_at(h, part * width)
                    unit = refs.unit[k, :, at] * inverse
                    refs.unit[k, :, at] = unit
                    scaled = unit * refs.gain[pl.ds(part, 1), head_at(h)]
                    turned = scaled * cosine + swap_pairs(scaled) * sine
                    refs.sent[k, :, at] = turned.astype(BF16)
            send_heads(k, late, 1)
        gather_end(gather_relay(links, refs.texts, first))
        for source in range(seqs):
            links.wait_line(refs.packed.at[source, :, early], source, 0)
            links.wait_line(refs.packed.at[source, :, late], source, 1)

    gains8 = jnp.pad(gain, ((0, 4), (0, 0)))
    texts = text_z.shape[0]
    first = run_kernel(
        "self_in", 1,
        dict(
            states=states_p, vec=vectors(1.0 + scale1, shift1), w=full_qkv,
            bias=jnp.broadcast_to(bias[:3].reshape(1, -1), (8, blocks3)),
            gain=gains8, own_tables=own_tables, text=text_z,
        ),
        dict(
            held=held, unit=((4, tokens, 2 * width), F32), inv=((4, 8, 256), F32),
            packed=((seqs, tokens, blocks3), BF16), texts=((4, texts, dim), BF16),
            tables=((4, tokens, 2 * HD), F32),
        ),
        body, dict(sent=((4, tokens, blocks3), BF16)), stats=True, line=2, cost=70,
    )
    x_self, self_unit, self_inv, packed = first.held, first.unit, first.inv, first.packed
    x_text, tables = first.texts, first.tables

    def masked_scores(q, keys):
        scores = mm_t(q, keys) * SCALE
        column = lax.broadcasted_iota(jnp.int32, scores.shape, 1)
        return jnp.where(column % tokens < own_tokens, scores, -1e30)

    def middle(refs, rows, step, total):
        vec = refs.vec
        branch = total + vec[0:1]
        refs.branch[rows] = branch
        joined = refs.states[rows] + branch * vec[1:2]
        refs.joined[rows] = joined
        normed, _ = layer_norm(joined)
        return (normed * vec[2:3] + vec[3:4]).astype(BF16)

    def product(refs, k, piece):
        pre = mm(piece[...], refs.w2[:, pl.ds(0, width)]) + refs.bias[0:1]
        refs.unit[k] = pre
        refs.stat[k, pl.ds(0, 1), pl.ds(0, tokens)] = to_row(jnp.sum(pre * pre, -1, keepdims=True))

    def body(links, refs):
        refs.stat[...] = jnp.zeros_like(refs.stat)
        packed = refs.packed
        refs.grads[0] = refs.own_grads[...]
        first = gather_begin(links, refs.grads)
        for turn in (1, 2, 3, 0):
            to = (links.z + turn) % seqs
            for h in range(heads):
                keys = packed[:, :, head_at(h, width)].reshape(clip_rows, HD)
                values = packed[:, :, head_at(h, 2 * width)].reshape(clip_rows, HD)
                probs = softmax(masked_scores(packed[to, :, head_at(h)], keys))
                refs.outs[turn, :, head_at(h)] = mm(probs.astype(BF16), values).astype(BF16)
            links.send_line(
                refs.outs.at[turn], refs.mixed.at[links.clip_of(links.z)], to, turn
            )
        far = gather_relay(links, refs.grads, first)
        reduce_product = rows_partial("mixed", "w")

        def partial(refs, k, store):
            links.wait_line(refs.mixed.at[k], links.clip_of(k))
            reduce_product(refs, k, store)

        reduce_slice(links, refs, partial, middle, refs.held)
        gather_slice(links, refs, refs.held, product)
        gather_end(far)
        sum_stats(links, refs)
        refs.inv[...] = lax.rsqrt(refs.stat_sum[...] / dim + EPS)

        @pl.loop(0, 4)
        def _(k):
            inverse = to_column(refs.inv[k, pl.ds(0, 1), pl.ds(0, tokens)])
            refs.unit[k] = refs.unit[k] * inverse

    second = run_kernel(
        "self_attend", 2,
        dict(
            packed=packed, w=full_out, states=states_p,
            vec=vectors(attn_bias[3], gate1, norm_gain, norm_bias),
            w2=cross_wq, bias=jnp.broadcast_to(bias[4:5], (8, width)),
            own_grads=d_ffnout,
        ),
        dict(
            mixed=((4, tokens, width), BF16), branch=wide, joined=wide, held=held, grads=held,
            unit=head_block, inv=((4, 8, 256), F32),
        ),
        body,
        dict(outs=((seqs, tokens, width), BF16), **reduce_scratch(tokens, dim)),
        stats=True, line=1,
        cost=80,
    )
    mixed, branch, after_self, g_ffn = second.mixed, second.branch, second.joined, second.grads
    x_cross, cq_unit, cq_inv = second.held, second.unit, second.inv

    ck_pre = mm(x_text, cross_wk) + bias[5]
    cross_v = (mm(x_text, cross_wv) + bias[6]).astype(BF16)
    ck_inv = rms_scale(sum4(jnp.sum(ck_pre * ck_pre, -1)))
    ck_unit = ck_pre * ck_inv
    cross_k = (ck_unit * gain[3]).astype(BF16)
    text_kv = jnp.concatenate([cross_k, cross_v], -1)

    def cross_heads(refs, k, h):
        q = (refs.unit[k, :, head_at(h)] * refs.gain[2:3, head_at(h)]).astype(BF16)
        keys = refs.kv[k, :, head_at(h)]
        values = refs.kv[k, :, head_at(h, width)]
        return q, keys, values, softmax(mm_t(q, keys) * SCALE)

    def middle(refs, rows, step, total):
        vec = refs.vec
        joined = refs.start[rows] + (total + vec[0:1])
        refs.joined[rows] = joined
        normed, _ = layer_norm(joined)
        return (normed * vec[1:2] + vec[2:3]).astype(BF16)

    root = math.sqrt(2.0 / math.pi)

    def product(refs, k, piece):
        for at, size in column_chunks(hidden_width, 640):
            columns = pl.ds(at, size)
            pre = mm(piece[...], refs.w2[:, columns]) + refs.bias[0:1, columns]
            bent = jnp.tanh(root * (pre + 0.044715 * pre * pre * pre))
            refs.hidden[k, :, columns] = (0.5 * pre * (1.0 + bent)).astype(BF16)
            refs.slope[k, :, columns] = 0.5 * (1.0 + bent) + 0.5 * pre * (
                1.0 - bent * bent
            ) * root * (1.0 + 3.0 * 0.044715 * pre * pre)

    def body(links, refs):
        reduce_product = rows_partial("mix", "w")

        def partial(refs, k, store):
            for h in range(heads):
                _, _, values, probs = cross_heads(refs, k, h)
                refs.mix[k, :, head_at(h)] = mm(probs.astype(BF16), values).astype(BF16)
            reduce_product(refs, k, store)

        reduce_slice(links, refs, partial, middle, refs.held)
        gather_slice(links, refs, refs.held, product)

    third = run_kernel(
        "cross_attend", 3,
        dict(
            unit=cq_unit, gain=gains8, kv=text_kv,
            w=full_crossout, start=after_self,
            vec=vectors(attn_bias[7], 1.0 + scale2, shift2),
            w2=full_up,
            bias=jnp.broadcast_to(pick(up_bias)[None], (8, hidden_width)),
        ),
        dict(
            mix=((4, tokens, width), BF16), joined=wide, held=held,
            hidden=((4, tokens, hidden_width), BF16),
            slope=((4, tokens, hidden_width), F32),
        ),
        body, reduce_scratch(tokens, dim),
        cost=60,
    )
    cross_mix, after_cross, x_ffn, hidden = third.mix, third.joined, third.held, third.hidden

    (down_core,) = weight_sums(
        "down_sums", 9, [(hidden_width, dim // 2)], [(0, hidden, g_ffn, None)], seqs, cost=14
    )
    down_part = scatter_z(down_core)
    inner_partial = turned_partial("d_hpre", "w_up")

    def ffn_partial(refs, k, store):
        w = refs.w_down
        deep = w.shape[2]
        for at, size in column_chunks(hidden_width, 640):
            columns = pl.ds(at, size)
            grad = mm_t(refs.g[k, :, pl.ds(0, deep)], w[0, columns])
            grad = grad + mm_t(refs.g[k, :, pl.ds(deep, deep)], w[1, columns])
            refs.d_hpre[k, :, columns] = (grad * refs.slope[k, :, columns]).astype(BF16)
        inner_partial(refs, k, store)

    def middle(refs, rows, step, total):
        normed, inverse = layer_norm(refs.joined[rows])
        d_cross = refs.top[rows] + norm_backward(normed, inverse, total * refs.vec[0:1])
        refs.d_cross[rows] = d_cross
        low = d_cross.astype(BF16)
        add_rows(refs.sums, 0, total, step)
        add_rows(refs.sums, 1, total * normed, step)
        add_rows(refs.sums, 2, low.astype(F32), step)
        return low

    def product(refs, k, piece):
        refs.d_mix[k] = rows_turned(piece, refs.w2).astype(BF16)

    def body(links, refs):
        reduce_slice(links, refs, ffn_partial, middle, refs.held)
        gather_slice(links, refs, refs.held, product)

    fourth = run_kernel(
        "ffn_back", 4,
        dict(
            g=after(g_ffn, down_core), w_down=full_down, slope=third.slope, w_up=full_up,
            joined=after_cross, top=out_grad_p, vec=vectors(1.0 + scale2),
            w2=full_crossout,
        ),
        dict(
            d_hpre=((4, tokens, hidden_width), BF16), d_cross=wide, held=held,
            d_mix=((4, tokens, width), BF16), sums=((3, 8, dim), F32),
        ),
        body, reduce_scratch(tokens, dim),
        cost=72,
    )
    d_hpre, d_cross, g_cross, d_cmix = fourth.d_hpre, fourth.d_cross, fourth.held, fourth.d_mix
    sums4 = jnp.sum(fourth.sums, 1)
    spread_rows = (seqs, 2, dim // (4 * seqs))
    (up_core,) = weight_sums(
        "up_sums", 10, [spread_rows + (hidden_width,)], [(0, x_ffn, d_hpre, 0)], seqs, cost=14
    )
    up_part = scatter_z(up_core.reshape(-1, hidden_width))

    def rms_back(grad, unit, inverse, mean):
        return inverse * (grad - unit * mean)

    def middle(refs, rows, step, total):
        normed, inverse = layer_norm(refs.joined[rows])
        vec = refs.vec
        d_self = refs.top[rows] + norm_backward(normed, inverse, total * vec[0:1])
        refs.d_self[rows] = d_self
        low = (d_self * vec[1:2]).astype(BF16)
        add_rows(refs.sums, 0, total * normed, step)
        add_rows(refs.sums, 1, total, step)
        add_rows(refs.sums, 2, low.astype(F32), step)
        add_rows(refs.sums, 3, d_self * refs.branch[rows], step)
        return low

    def ffn_out_partial(refs, k, store):
        half_width = refs.w_down.shape[2]
        for half in range(2):
            for at, size in column_chunks(half_width, 384):
                store(
                    pl.ds(half * half_width + at, size),
                    mm(refs.hidden[k], refs.w_down[half, :, pl.ds(at, size)]),
                )

    def ffn_out_rows(refs, rows, step, total):
        ffn_out = total + refs.vec[2:3]
        refs.block_out[rows] = refs.crossed[rows] + ffn_out * refs.vec[3:4]
        add_rows(refs.sums, 4, refs.out_grad[rows] * ffn_out, step)

    def body(links, refs):
        refs.stat[...] = jnp.zeros_like(refs.stat)
        refs.gains[...] = jnp.zeros_like(refs.gains)
        ffn_buffers = (refs.ffn_mine, refs.ffn_near, refs.ffn_far, refs.ffn_total)
        copies = reduce_begin(links, refs, ffn_buffers, ffn_out_partial)
        reduce_own(refs, ffn_buffers, ffn_out_partial)

        @pl.loop(0, 4)
        def _(k):
            square = jnp.zeros((tokens, 1), F32)
            for h in range(heads):
                q, keys, values, probs = cross_heads(refs, k, h)
                d_mix = refs.d_mix[k, :, head_at(h)]
                d_probs = mm_t(d_mix, values)
                delta = jnp.sum(probs * d_probs, -1, keepdims=True)
                d_scores = (probs * (d_probs - delta)).astype(BF16)
                d_q = mm(d_scores, keys) * SCALE
                refs.d_kv[k, :, head_at(h)] = (mm_l(d_scores, q) * SCALE).astype(BF16)
                refs.d_kv[k, :, head_at(h, width)] = mm_l(probs.astype(BF16), d_mix).astype(BF16)
                unit = refs.unit[k, :, head_at(h)]
                refs.gains[:, head_at(h)] += fold_rows(d_q * unit)
                d_q = d_q * refs.gain[2:3, head_at(h)]
                refs.d_unit[k, :, head_at(h)] = d_q
                square = square + jnp.sum(d_q * unit, -1, keepdims=True)
            refs.stat[k, pl.ds(0, 1), pl.ds(0, tokens)] = to_row(square)

        sum_stats(links, refs)
        copies = reduce_relay(links, ffn_buffers, copies)

        @pl.loop(0, 4)
        def _(k):
            inverse = to_column(refs.inv[k, pl.ds(0, 1), pl.ds(0, tokens)])
            mean = to_column(refs.stat_sum[k, pl.ds(0, 1), pl.ds(0, tokens)]) / dim
            refs.d_pre[k] = rms_back(refs.d_unit[k], refs.unit[k], inverse, mean).astype(BF16)

        def product(refs, k, piece):
            refs.outs[k] = rows_turned(piece, refs.w2).astype(BF16)
            links.send_line(
                refs.outs.at[k], refs.d_heads.at[links.z], links.clip_of(k), k
            )

        reduce_slice(links, refs, turned_partial("d_pre", "w"), middle, refs.held)
        gather_slice(links, refs, refs.held, product)
        reduce_end(refs, ffn_buffers, copies, ffn_out_rows)
        for source in range(seqs):
            links.wait_line(refs.d_heads.at[source], source)

    fifth = run_kernel(
        "cross_back", 5,
        dict(
            unit=cq_unit, inv=cq_inv, gain=gains8, kv=text_kv,
            d_mix=after(d_cmix, up_core, down_part),
            w=cross_wq, joined=after_self, top=d_cross, branch=branch,
            vec=vectors(norm_gain, gate1, down_bias, gate2), w2=full_out,
            hidden=hidden, w_down=full_down, crossed=after_cross, out_grad=out_grad_p,
        ),
        dict(
            d_pre=((4, tokens, width), BF16), d_kv=((4, texts, 2 * width), BF16),
            gains=((8, width), F32), d_self=wide, held=held,
            d_heads=((seqs, tokens, width), BF16), sums=((5, 8, dim), F32), block_out=wide,
        ),
        body,
        dict(
            d_unit=((4, tokens, width), F32), outs=((4, tokens, width), BF16),
            **reduce_scratch(tokens, dim),
            **{"ffn_" + n: v for n, v in reduce_scratch(tokens, dim).items()},
        ),
        stats=True, line=1,
        cost=80,
    )
    d_cq, d_self, g_self, d_heads = fifth.d_pre, fifth.d_self, fifth.held, fifth.d_heads
    cq_gain = jnp.sum(fifth.gains, 0)
    sums5 = jnp.sum(fifth.sums, 1)
    d_kv, mixed, cross_mix = after((fifth.d_kv, mixed, cross_mix), up_part)
    outproj_core, crossout_core = weight_sums(
        "output_sums", 11, [(width, dim // 2)] * 2,
        [(0, mixed, g_self, None), (1, cross_mix, g_cross, None)], seqs, cost=8,
    )
    d_kv = d_kv.reshape(4, seqs, -1, 2 * width).transpose(1, 0, 2, 3)
    parts = [d_kv.reshape(seqs, -1, 2 * width)]
    parts += [v.reshape(seqs, -1, 2 * width) for v in (outproj_core, crossout_core)]
    joint_core = jnp.concatenate(parts, 1)
    joint_part = lax.psum_scatter(joint_core, "z", scatter_dimension=0, tiled=True)[0]

    def middle(refs, rows, step, total):
        normed, inverse = layer_norm(refs.states[rows])
        refs.out[rows] = refs.top[rows] + norm_backward(
            normed, inverse, total * refs.vec[0:1]
        )
        add_rows(refs.sums, 0, total, step)
        add_rows(refs.sums, 1, total * normed, step)

    def body(links, refs):
        refs.stat[...] = jnp.zeros_like(refs.stat)
        refs.gains[...] = jnp.zeros_like(refs.gains)
        packed, d_heads = refs.packed, refs.d_heads
        x, y, core = links.x, links.y, lax.axis_index("core")
        refs.ups[y, x] = refs.up_part[y]
        refs.downs[x] = refs.down_part[...]
        over_y = links.send("y", refs.up_part.at[1 - y], refs.ups.at[y, x])
        over_x = [
            links.send("x", refs.up_part.at[y], refs.ups.at[y, x]),
            links.send("x", refs.down_part, refs.downs.at[x]),
        ]
        for h in range(heads):
            refs.d_keys[...] = jnp.zeros_like(refs.d_keys)
            refs.d_values[...] = jnp.zeros_like(refs.d_values)

            @pl.loop(0, seqs)
            def _(i):
                keys = packed[:, :, head_at(h, width)].reshape(clip_rows, HD)
                values = packed[:, :, head_at(h, 2 * width)].reshape(clip_rows, HD)
                q = packed[i, :, head_at(h)]
                d_mix = d_heads[i, :, head_at(h)]
                probs = softmax(masked_scores(q, keys))
                d_probs = mm_t(d_mix, values)
                delta = jnp.sum(probs * d_probs, -1, keepdims=True)
                d_scores = (probs * (d_probs - delta)).astype(BF16)
                refs.outs[h, i, :, pl.ds(0, HD)] = (mm(d_scores, keys) * SCALE).astype(BF16)
                refs.d_keys[...] += mm_l(d_scores, q)
                refs.d_values[...] += mm_l(probs.astype(BF16), d_mix)

            for i in range(seqs):
                rows = pl.ds(i * tokens, tokens)
                refs.outs[h, i, :, pl.ds(HD, HD)] = (refs.d_keys[rows] * SCALE).astype(BF16)
                refs.outs[h, i, :, pl.ds(2 * HD, HD)] = refs.d_values[rows].astype(BF16)
            for step in range(seqs):
                to = (links.z + 1 + step) % seqs
                links.send_line(
                    refs.outs.at[h, to],
                    refs.arrived.at[h, links.clip_of(links.z)],
                    to, step, h,
                )
            if h == 0:
                over_y.wait_recv()
                over_x.append(links.send("x", refs.ups.at[1 - y, x], refs.ups.at[1 - y, x]))
            if h == 1:
                over_x[1].wait_recv()
                over_core = links.send(("core",), refs.downs.at[1 - core], refs.columns)

        for copy in (over_x[0], over_x[2], over_core):
            copy.wait_recv()
        for block in range(4):
            refs.up_grad[:, pl.ds(block * hidden_width, hidden_width)] = refs.ups[
                block // 2, block % 2
            ].astype(F32)
        half = refs.columns.shape[1]
        for part, value in ((core, refs.downs.at[core]), (1 - core, refs.columns)):
            at = pl.ds(pl.multiple_of(part * half, half), half)
            refs.down_grad[:, at] = value[...].astype(F32)
        for k in range(4):
            for h in range(heads):
                links.wait_line(refs.arrived.at[h, k], links.clip_of(k), h)

        @pl.loop(0, 4)
        def _(k):
            for part in range(2):
                square = jnp.zeros((tokens, 1), F32)
                for h in range(heads):
                    at = head_at(h, part * width)
                    grad = refs.arrived[h, k, :, pl.ds(part * HD, HD)].astype(F32)
                    grad = grad * refs.tables[k, :, pl.ds(0, HD)] - swap_pairs(grad) * refs.tables[k, :, pl.ds(HD, HD)]
                    unit = refs.unit[k, :, at]
                    refs.gains[part, :, head_at(h)] += fold_rows(grad * unit)
                    grad = grad * refs.gain[pl.ds(part, 1), head_at(h)]
                    refs.d_unit[k, :, at] = grad
                    square = square + jnp.sum(grad * unit, -1, keepdims=True)
                refs.stat[k, pl.ds(part, 1), pl.ds(0, tokens)] = to_row(square)
            for h in range(heads):
                refs.d_qkv[k, :, head_at(h, 2 * width)] = refs.arrived[
                    h, k, :, pl.ds(2 * HD, HD)
                ]

        sum_stats(links, refs)

        @pl.loop(0, 4)
        def _(k):
            for part in range(2):
                row = (k, pl.ds(part, 1), pl.ds(0, tokens))
                inverse = to_column(refs.inv[row])
                mean = to_column(refs.stat_sum[row]) / dim
                at = pl.ds(part * width, width)
                refs.d_qkv[k, :, at] = rms_back(
                    refs.d_unit[k, :, at], refs.unit[k, :, at], inverse, mean
                ).astype(BF16)

        reduce_slice(links, refs, turned_partial("d_qkv", "w"), middle)

    sixth = run_kernel(
        "self_back", 6,
        dict(
            packed=packed, d_heads=d_heads, unit=self_unit, inv=self_inv,
            gain=gains8, tables=tables, w=full_qkv, states=states_p,
            top=after(d_self, joint_core), vec=vectors(1.0 + scale1),
            up_part=up_part.reshape(2, -1, hidden_width), down_part=down_part,
        ),
        dict(
            d_qkv=((4, tokens, blocks3), BF16), gains=((2, 8, width), F32),
            out=wide, sums=((2, 8, dim), F32),
            up_grad=((up_part.shape[0] // 2, 4 * hidden_width), F32),
            down_grad=((down_part.shape[0], dim), F32),
        ),
        body,
        dict(
            outs=((heads, seqs, tokens, 3 * HD), BF16),
            arrived=((heads, 4, tokens, 3 * HD), BF16),
            d_keys=((clip_rows, HD), F32), d_values=((clip_rows, HD), F32),
            d_unit=((4, tokens, 2 * width), F32),
            ups=((2, 2, up_part.shape[0] // 2, hidden_width), BF16),
            downs=((2,) + down_part.shape, BF16), columns=(down_part.shape, BF16),
            **reduce_scratch(tokens, dim),
        ),
        stats=True, line=heads, pair=True,
        cost=120,
    )
    d_qkv = tied(sixth.d_qkv, joint_part)
    d_hpre, d_cq = after((d_hpre, d_cq), d_qkv)
    text_rows, weight_rows = parts[0].shape[1], parts[1].shape[1]
    d_ckv = joint_part[:text_rows].reshape(4, -1, 2 * width)
    outproj_part = over_reps(joint_part[text_rows : text_rows + weight_rows])
    crossout_part = over_reps(joint_part[text_rows + weight_rows :])
    d_qkv_sum = jnp.sum(d_qkv.astype(F32), (0, 1))
    q_gain, k_gain = jnp.sum(sixth.gains, 1)
    states_grad = sixth.out[:own_tokens]
    sums6 = jnp.sum(sixth.sums, 1)

    d_ckn = d_ckv[..., :width].astype(F32)
    d_cv = d_ckv[..., width:]
    zpos = lax.axis_index("z")
    own = texts // seqs
    ck_unit = lax.dynamic_slice_in_dim(ck_unit, zpos * own, own, 1)
    ck_inv = lax.dynamic_slice_in_dim(ck_inv, zpos * own, own, 1)
    x_text = lax.dynamic_slice_in_dim(x_text, zpos * own, own, 1)
    d_cku = d_ckn * gain[3]
    ck_stat = sum4(jnp.sum(d_cku * ck_unit, -1)) / dim
    d_ck = rms_back(d_cku, ck_unit, ck_inv, ck_stat[..., None]).astype(BF16)
    ck_gain = jnp.sum(d_ckn * ck_unit, (0, 1))
    d_text = jnp.concatenate([d_ck, d_cv], -1)
    text_grad = reduce4(lambda k: mm_t(d_ck[k], cross_wk) + mm_t(d_cv[k], cross_wv))
    (last_core,) = weight_sums(
        "last_sums", 12, [spread_rows + (2 * blocks3,)],
        [(0, x_self, d_qkv, 0), (0, x_cross, d_cq, blocks3), (0, x_text, d_text, blocks3 + width)],
        seqs, cost=16,
    )
    last_part = scatter_z(last_core.reshape(-1, 2 * blocks3))

    block_out = fifth.block_out[:own_tokens]
    up_grad, down_grad = sixth.up_grad, sixth.down_grad
    both_grad = column_done(last_part, 6)
    qkv_grad, cross_grad = both_grad[:, :3], both_grad[:, 3:]
    outproj_grad = row_done(outproj_part)
    crossout_grad = row_done(crossout_part)

    def column_sum(v):
        return jnp.sum(v.astype(F32), tuple(range(v.ndim - 1)))

    early = jnp.stack(
        [
            sums4[0],
            sums4[1],
            sums5[4],
            spread(column_sum(d_cq)),
            spread(column_sum(d_ck)),
            spread(column_sum(d_cv)),
            sums4[2],
            spread(cq_gain),
            spread(ck_gain),
            sums5[0],
            sums5[1],
            column_sum(d_ffnout),
            sums5[2],
            sums5[3],
        ]
    )
    late = jnp.stack(
        [
            sums6[0],
            sums6[1],
            spread(d_qkv_sum[:width]),
            spread(d_qkv_sum[width : 2 * width]),
            spread(d_qkv_sum[2 * width :]),
            spread(q_gain),
            spread(k_gain),
        ]
    )
    upbias_rows = jnp.pad(spread(column_sum(d_hpre)), (0, -4 * hidden_width % dim)).reshape(-1, dim)
    counts = early.shape[0], late.shape[0], upbias_rows.shape[0]
    rows = -(-sum(counts) // 8) * 8
    small = jnp.concatenate([early, late, upbias_rows])
    small = jnp.pad(small, ((0, rows - sum(counts)), (0, 0)))

    def body(links, refs):
        refs.stages[0] = refs.small[...]
        flip = links.z + 1 - 2 * (links.z % 2)
        hops = [
            {"z": flip}, {"z": (links.z + seqs // 2) % seqs},
            {"core": 1 - lax.axis_index("core")}, {"x": 1 - links.x}, {"y": 1 - links.y},
        ]
        for step, where in enumerate(hops):
            copy = links.send_to(where, refs.stages.at[step], refs.others.at[step])
            copy.wait_recv()
            refs.stages[step + 1] = refs.stages[step] + refs.others[step]
        refs.clip[...] = refs.stages[2]
        refs.all[...] = refs.stages[5]

    shape = ((rows, dim), F32)
    summed = run_kernel(
        "small_sums", 8, dict(small=after(small, last_core)), dict(clip=shape, all=shape),
        body, dict(stages=((6, rows, dim), F32), others=((5, rows, dim), F32)),
        line=1, pair=True, cost=25,
    )
    total = over_reps(summed.all)
    early_clip, late_clip = summed.clip[: counts[0]], summed.clip[counts[0] :]
    early_all, late_all = total[: counts[0]], total[counts[0] :]
    upbias = total[counts[0] + counts[1] : sum(counts)].reshape(-1)[: 4 * hidden_width]

    def mod_rows(e, l):
        return jnp.stack([l[0], l[1], e[13], e[0], e[1], e[2]])

    time_grad = mod_rows(early_clip, late_clip)[None]
    mod_grad = mod_rows(early_all, late_all)
    bias_grad = jnp.stack(
        [late_all[2], late_all[3], late_all[4], early_all[12]] + [early_all[i] for i in (3, 4, 5, 6)]
    )
    gain_grad = jnp.stack([late_all[5], late_all[6], early_all[7], early_all[8]])
    return (
        block_out, states_grad, text_grad, time_grad, qkv_grad, outproj_grad, cross_grad,
        crossout_grad, up_grad, down_grad, bias_grad, gain_grad, early_all[9], early_all[10],
        upbias, early_all[11], mod_grad,
    )


def solution(mesh):
    reps, shards, seqs = mesh.shape["replica"], mesh.shape["shard"], mesh.shape["seq"]
    fine = Mesh(
        mesh.devices.reshape(reps // 2, 2, shards // 2, 2, seqs), ("rep", "x", "y", "core", "z")
    )
    tokens = P(("rep", "x", "y", "core", "z"), None)
    clips = P(("rep", "x", "y", "core"), None, None)
    rows2 = P(("y", "core", "z"), None)
    rows3 = P(("y", "core", "z"), None, None)
    return jax.shard_map(
        on_device,
        mesh=fine,
        in_specs=(
            tokens, tokens, P(None, ("rep", "x", "y", "core", "z")), clips,
            rows3, rows2, rows3, rows2, rows2, rows2,
            P(), P(), P(), P(), P(), P(), P(), tokens,
        ),
        out_specs=(
            tokens, tokens, tokens, clips,
            rows3, rows2, rows3, rows2, rows2, rows2,
            P(), P(), P(), P(), P(), P(), P(),
        ),
        check_vma=False,
    )
```
